128 devices in a mesh: dp: 4 (over x), seq: 32 (over y, z, core).
Axes of the slice: x: 4, y: 4, z: 4, core: 2. Of those that a mesh axis runs over, the one named last changes fastest.
Arguments:
- queries: bfloat16 [4, 8192, 2048], P('dp', 'seq'), may hold values from -6 to 6
- key_states: bfloat16 [4, 8192, 2048], P('dp', 'seq'), may hold values from -6 to 6
- value_states: bfloat16 [4, 8192, 2048], P('dp', 'seq'), may hold values from -6 to 6
- out_weight: bfloat16 [2048, 2048], replicated, may hold values from -0.125 to 0.125
- cotangent: bfloat16 [4, 8192, 2048], P('dp', 'seq'), may hold values from -6 to 6
- block_offsets: int32 [4, 64, 4], P('dp', 'seq'), may hold values from 1 to 32, as said below
Outputs:
- grad_queries: bfloat16 [4, 8192, 2048], P('dp', 'seq')
- grad_keys: bfloat16 [4, 8192, 2048], P('dp', 'seq')
- grad_values: bfloat16 [4, 8192, 2048], P('dp', 'seq')
- grad_out_weight: float32 [2048, 2048], P(('dp', 'seq'))
The draws below stay inside these ranges and needn't reach their ends.
Inputs may be any that keep to these rules, and one draw needn't show every extreme that they name: `block_offsets`: each query block lists 4 distinct offsets, each a power of two below 64; query block b always lists 2 ** (b mod log2(64)). Listed blocks before the document's start are skipped.
All inputs are finite; a program needn't handle non-finite values.
Results may differ from the reference program's by a relative error of at most 0.029.
Values may be sent and summed in bfloat16 or wider, within the bound.
No kernel may reach another device: no remote copies, remote signals or barrier semaphores. Data moves between devices by JAX's collectives and lax.ppermute only.
A program may use at most 256 MiB of HBM per device.

```python
import jax
import jax.numpy as jnp
from jax import lax

D = 2048
HEADS = 16
HEAD = 128
BLK = 128
SLOTS = 4
TOK_DEV = 256
DOCS = 4
SEQ = 8192
BLOCKS = 64
N_SEQ = 32


def attention_pair(key):
    array_shape = (DOCS, SEQ, D)
    query_base = jax.random.truncated_normal(jax.random.fold_in(key, 11), -6.0, 6.0, array_shape, jnp.float32)
    key_base = jax.random.truncated_normal(jax.random.fold_in(key, 12), -6.0, 6.0, array_shape, jnp.float32)
    query_draw = query_base
    key_draw = key_base
    return (query_draw, key_draw)


def draw_queries(key, part):
    return attention_pair(key)[0].astype(jnp.bfloat16)


def draw_key_states(key, part):
    return attention_pair(key)[1].astype(jnp.bfloat16)


def draw_block_offsets(key, part):
    levels = BLOCKS.bit_length() - 1
    row_total = DOCS * BLOCKS
    row_keys = jax.random.split(key, row_total)
    ranks = jax.vmap(lambda row_key: jax.random.permutation(row_key, levels))(row_keys).astype(jnp.int32)
    row_block = jnp.arange(row_total, dtype=jnp.int32) % BLOCKS
    forced = row_block % levels
    ranks = jnp.where(jnp.arange(levels, dtype=jnp.int32)[None, :] == forced[:, None], -1, ranks)
    order = jnp.argsort(ranks, axis=1, stable=True)[:, :SLOTS].astype(jnp.int32)
    offsets = jnp.power(jnp.int32(2), order)
    return offsets.reshape(DOCS, BLOCKS, SLOTS).astype(jnp.int32)


def block_scale(key, dims, cuts, smallest, largest):
    level, own = 1.0, jax.random.fold_in(key, 6)
    for dim, blocks in cuts:
        draws = jnp.exp(jax.random.uniform(jax.random.fold_in(own, dim), (blocks,), jnp.float32, smallest / len(cuts), largest / len(cuts)))
        level = level * jnp.repeat(draws, dims[dim] // blocks).reshape([-1 if axis == dim else 1 for axis in range(len(dims))])
    return level


def normal_values(own_key, shape, width, most, shards=(), held_as=jnp.bfloat16):
    level = block_scale(own_key, shape, shards, -0.22, 0.18) if shards else 1.0
    array = jax.random.normal(own_key, shape, jnp.float32) * width * level
    return jnp.minimum(jnp.maximum(array, -most), most).astype(held_as)


def setup_inputs(seed: int = 0) -> dict:
    splits = jax.random.split(jax.random.key(seed), 7)
    return {
        "queries": draw_queries(jax.random.fold_in(splits[6], 71), 0),
        "key_states": draw_key_states(jax.random.fold_in(splits[6], 71), 0),
        "value_states": normal_values(splits[2], (DOCS, SEQ, D), 1.0, 6.0, ((0, 4), (1, 32))),
        "out_weight": normal_values(splits[3], (D, D), D ** -0.5, 0.125),
        "cotangent": normal_values(splits[4], (DOCS, SEQ, D), 1.0, 6.0, ((0, 4), (1, 32))),
        "block_offsets": draw_block_offsets(jax.random.fold_in(splits[6], 71), 0),
    }


masked_score = -1.0e30


def level_of(ratio):
    powers = 2 ** jnp.arange(1, 24, dtype=jnp.int32)
    return jnp.sum((ratio[..., None] >= powers).astype(jnp.int32), axis=-1)


def attention_grads(query_rows, key_pool, value_pool, grad_attn, offsets, device, blocks):
    score_scale = HEAD ** -0.5
    local_block = jnp.arange(blocks, dtype=jnp.int32)
    global_block = device * blocks + local_block
    usable = (global_block[:, None] - offsets) >= 0
    nearby = offsets < blocks
    inside = local_block[:, None] >= offsets
    slot_index = jnp.where(nearby, jnp.where(inside, 0, 1), 1 + level_of(offsets // blocks))
    block_index = jnp.where(nearby, jnp.where(inside, local_block[:, None] - offsets, local_block[:, None] - offsets + blocks), local_block[:, None])
    pool_index = jnp.where(usable, slot_index * blocks + block_index, 0).astype(jnp.int32)
    all_keys = jnp.concatenate([key_pool[:blocks][:, None], jnp.take(key_pool, pool_index, axis=0)], axis=1)
    all_values = jnp.concatenate([value_pool[:blocks][:, None], jnp.take(value_pool, pool_index, axis=0)], axis=1)
    all_keys = all_keys.reshape(blocks, -1, HEADS, HEAD).astype(jnp.float32)
    all_values = all_values.reshape(blocks, -1, HEADS, HEAD).astype(jnp.float32)
    query_heads = query_rows.reshape(blocks, BLK, HEADS, HEAD).astype(jnp.float32)
    key_width = all_keys.shape[1]
    scores = jnp.einsum("pqhe,pkhe->phqk", query_heads, all_keys) * score_scale
    column = jnp.arange(key_width, dtype=jnp.int32)
    query_row = jnp.arange(BLK, dtype=jnp.int32)
    column_slot = column // BLK
    column_row = column % BLK
    slot_live = jnp.concatenate([jnp.ones((blocks, 1), dtype=bool), usable], axis=1)
    column_live = slot_live[:, column_slot]
    causal = (column_slot[None, :] > 0) | (column_row[None, :] <= query_row[:, None])
    allowed = column_live[:, None, None, :] & causal[None, None, :, :]
    scores = jnp.where(allowed, scores, masked_score)
    row_peak = jnp.max(scores, axis=-1, keepdims=True)
    weights = jnp.where(allowed, jnp.exp(scores - row_peak), 0.0)
    attn_prob = weights / jnp.sum(weights, axis=-1, keepdims=True)
    prob_low = lax.optimization_barrier(attn_prob.astype(jnp.bfloat16)).astype(jnp.float32)
    attended = jnp.einsum("phqk,pkhe->pqhe", prob_low, all_values)
    attn_out = lax.optimization_barrier(attended.astype(jnp.bfloat16))
    grad_heads = grad_attn.reshape(blocks, BLK, HEADS, HEAD).astype(jnp.float32)
    row_dot = jnp.sum(grad_heads * attn_out.astype(jnp.float32), axis=-1)
    grad_prob = jnp.einsum("pqhe,pkhe->phqk", grad_heads, all_values)
    grad_score = attn_prob * (grad_prob - jnp.transpose(row_dot, (0, 2, 1))[..., None]) * score_scale
    grad_score = lax.optimization_barrier(grad_score.astype(jnp.bfloat16)).astype(jnp.float32)
    grad_query = jnp.einsum("phqk,pkhe->pqhe", grad_score, all_keys)
    key_terms = jnp.einsum("phqk,pqhe->pkhe", grad_score, query_heads).reshape(blocks, 1 + SLOTS, BLK, D)
    value_terms = jnp.einsum("phqk,pqhe->pkhe", prob_low, grad_heads).reshape(blocks, 1 + SLOTS, BLK, D)
    pool_size = key_pool.shape[0]
    key_acc = jnp.zeros((pool_size, BLK, D), jnp.float32).at[local_block].add(key_terms[:, 0]).at[pool_index].add(key_terms[:, 1:])
    value_acc = jnp.zeros((pool_size, BLK, D), jnp.float32).at[local_block].add(value_terms[:, 0]).at[pool_index].add(value_terms[:, 1:])
    return attn_out.reshape(-1, D), grad_query.reshape(-1, D), key_acc, value_acc


def shard_at(full_array, shard_index):
    piece = lax.dynamic_index_in_dim(full_array, jnp.maximum(shard_index, 0), 0, keepdims=False)
    return jnp.where(shard_index >= 0, piece, jnp.zeros_like(piece))


def reference(queries, key_states, value_states, out_weight, cotangent, block_offsets):
    blocks = TOK_DEV // BLK
    hop_count = N_SEQ.bit_length() - 1
    grad_all = jnp.dot(cotangent.reshape(-1, D), out_weight.T, preferred_element_type=jnp.float32)
    grad_all = grad_all.astype(jnp.bfloat16).reshape(DOCS, N_SEQ, TOK_DEV, D)
    query_all = queries.reshape(DOCS, N_SEQ, TOK_DEV, D)
    key_all = key_states.reshape(DOCS, N_SEQ, TOK_DEV, D)
    value_all = value_states.reshape(DOCS, N_SEQ, TOK_DEV, D)
    offsets_all = block_offsets.reshape(DOCS, N_SEQ, blocks, SLOTS)
    hop_list = [0] + [2 ** hop_level for hop_level in range(hop_count)]
    attn_list, query_list, key_list, value_list = [], [], [], []
    for document in range(DOCS):
        query_doc = query_all[document]
        key_doc = key_all[document]
        value_doc = value_all[document]
        grad_doc = grad_all[document]
        offsets_doc = offsets_all[document]

        def device_step(state_pair, device):
            key_full, value_full = state_pair
            key_pool = jnp.stack([shard_at(key_doc, device - hop_dist) for hop_dist in hop_list], axis=0).reshape(-1, BLK, D)
            value_pool = jnp.stack([shard_at(value_doc, device - hop_dist) for hop_dist in hop_list], axis=0).reshape(-1, BLK, D)
            offsets = lax.dynamic_index_in_dim(offsets_doc, device, 0, keepdims=False)
            attn_out, grad_query, key_acc, value_acc = attention_grads(shard_at(query_doc, device), key_pool, value_pool, shard_at(grad_doc, device), offsets, device, blocks)
            key_full = key_full.at[device].add(key_acc[:blocks].reshape(TOK_DEV, D))
            value_full = value_full.at[device].add(value_acc[:blocks].reshape(TOK_DEV, D))
            for hop_level in range(hop_count):
                target = device - 2 ** hop_level
                lower = (1 + hop_level) * blocks
                key_piece = lax.optimization_barrier(key_acc[lower:lower + blocks].reshape(TOK_DEV, D).astype(jnp.bfloat16)).astype(jnp.float32)
                value_piece = lax.optimization_barrier(value_acc[lower:lower + blocks].reshape(TOK_DEV, D).astype(jnp.bfloat16)).astype(jnp.float32)
                key_full = key_full.at[jnp.maximum(target, 0)].add(jnp.where(target >= 0, key_piece, 0.0))
                value_full = value_full.at[jnp.maximum(target, 0)].add(jnp.where(target >= 0, value_piece, 0.0))
            return (key_full, value_full), (attn_out, grad_query)

        zero_state = (jnp.zeros((N_SEQ, TOK_DEV, D), jnp.float32), jnp.zeros((N_SEQ, TOK_DEV, D), jnp.float32))
        (key_full, value_full), (attn_doc, query_grad) = lax.scan(device_step, zero_state, jnp.arange(N_SEQ, dtype=jnp.int32))
        attn_list.append(attn_doc.reshape(SEQ, D))
        query_list.append(query_grad.reshape(SEQ, D).astype(jnp.bfloat16))
        key_list.append(key_full.reshape(SEQ, D).astype(jnp.bfloat16))
        value_list.append(value_full.reshape(SEQ, D).astype(jnp.bfloat16))
    attn_rows = jnp.concatenate(attn_list, axis=0)
    grad_out_weight = jnp.dot(attn_rows.T, cotangent.reshape(-1, D), preferred_element_type=jnp.float32)
    return (jnp.stack(query_list, axis=0), jnp.stack(key_list, axis=0), jnp.stack(value_list, axis=0), grad_out_weight)
```

```python
import math

import jax
import jax.numpy as jnp
from jax import lax
from jax.experimental import pallas as pl
from jax.experimental.pallas import tpu as pltpu
from jax.sharding import PartitionSpec as P

HEADS = 16
HEAD = 128
BLK = 128
SLOTS = 4
D = HEADS * HEAD
TOK = 256
CHIPS = 16
BLOCKS = 64
RIDER = 3 * TOK
ROWS = 3 * TOK + 8
SCALE = HEAD ** (-0.5)
SCALE2 = SCALE * math.log2(math.e)
NEG = -1e30
bf16 = jnp.bfloat16
f32 = jnp.float32

SAME_CORE = [[2 * c + k for c in range(CHIPS)] for k in range(2)]
CORE_SWAP = [(i, i ^ 1) for i in range(2 * CHIPS)]

VMEM_LIMIT = 56 * 1024 * 1024


def dot(a, b, ca, cb):
    return lax.dot_general(a, b, (((ca,), (cb,)), ((), ())), preferred_element_type=f32)


def exchange(x):
    return lax.all_to_all(x, "seq", 0, 0, axis_index_groups=SAME_CORE, tiled=True)


def pack_body(offs, k_ref, v_ref, q_ref, x_ref, rider, sems):
    lane = lax.broadcasted_iota(jnp.int32, (8, 128), 1)
    val = jnp.zeros((8, 128), jnp.int32)
    for j in range(2 * SLOTS):
        val = jnp.where(lane == j, offs[j // SLOTS, j % SLOTS], val)
    rider[...] = val.astype(f32).astype(bf16)
    copies = []
    for h in range(HEADS):
        for t, ref in enumerate((k_ref, v_ref, q_ref)):
            copies.append(
                pltpu.make_async_copy(
                    ref.at[:, pl.ds(h * HEAD, HEAD)],
                    x_ref.at[h, pl.ds(t * TOK, TOK), :],
                    sems.at[4 * h + t],
                )
            )
        copies.append(
            pltpu.make_async_copy(rider, x_ref.at[h, pl.ds(RIDER, 8), :], sems.at[4 * h + 3])
        )
    for copy in copies:
        copy.start()
    for copy in copies:
        copy.wait()


def pack(offs, k, v, q):
    return pl.pallas_call(
        pack_body,
        out_shape=jax.ShapeDtypeStruct((HEADS, ROWS, HEAD), bf16),
        in_specs=[pl.BlockSpec(memory_space=pltpu.SMEM)] + [pl.BlockSpec(memory_space=pl.ANY)] * 3,
        out_specs=pl.BlockSpec(memory_space=pl.ANY),
        scratch_shapes=[pltpu.VMEM((8, 128), bf16), pltpu.SemaphoreType.DMA((4 * HEADS,))],
        name="pack",
    )(offs, k, v, q)


def unpack_body(r_ref, gk_ref, gv_ref, gq_ref, sems):
    copies = []
    for h in range(HEADS):
        for t, ref in enumerate((gk_ref, gv_ref, gq_ref)):
            copies.append(
                pltpu.make_async_copy(
                    r_ref.at[h, pl.ds(t * TOK, TOK), :],
                    ref.at[:, pl.ds(h * HEAD, HEAD)],
                    sems.at[3 * h + t],
                )
            )
    for copy in copies:
        copy.start()
    for copy in copies:
        copy.wait()


def unpack(r):
    out = jax.ShapeDtypeStruct((TOK, D), bf16)
    return pl.pallas_call(
        unpack_body,
        out_shape=(out, out, out),
        in_specs=[pl.BlockSpec(memory_space=pl.ANY)],
        out_specs=[pl.BlockSpec(memory_space=pl.ANY)] * 3,
        scratch_shapes=[pltpu.SemaphoreType.DMA((3 * HEADS,))],
        name="unpack",
    )(r)


def grad_attn_body(c_ref, w_ref, o_ref):
    g = dot(c_ref[...], w_ref[...], 1, 1).astype(bf16)
    for j in range(2):
        o_ref[j] = g[:, j * HEAD : (j + 1) * HEAD]


def grad_attn_by_head(cot, weight):
    return pl.pallas_call(
        grad_attn_body,
        out_shape=jax.ShapeDtypeStruct((HEADS, TOK, HEAD), bf16),
        grid=(HEADS // 2,),
        in_specs=[
            pl.BlockSpec((TOK, D), lambda i: (0, 0)),
            pl.BlockSpec((2 * HEAD, D), lambda i: (i, 0)),
        ],
        out_specs=pl.BlockSpec((2, TOK, HEAD), lambda i: (i, 0, 0)),
        compiler_params=pltpu.CompilerParams(vmem_limit_bytes=VMEM_LIMIT),
        name="grad_attn",
    )(cot, weight)


def load_pool(x_ref, y_ref, kv, qs, sems):
    return [
        pltpu.make_async_copy(x_ref.at[:, pl.ds(0, 2 * TOK), :], kv.at[pl.ds(0, CHIPS)], sems.at[0]),
        pltpu.make_async_copy(y_ref.at[:, pl.ds(0, 2 * TOK), :], kv.at[pl.ds(CHIPS, CHIPS)], sems.at[1]),
        pltpu.make_async_copy(x_ref.at[:, pl.ds(2 * TOK, TOK), :], qs, sems.at[2]),
    ]


def listed(table, c, i):
    places = [(c, i * BLK, None)]
    for s in range(SLOTS):
        code = table[2 * c + i, s]
        f = jnp.maximum(code, 0)
        bias = jnp.where(code >= 0, 0.0, -NEG).astype(f32)
        places.append((f // 2, pl.multiple_of((f % 2) * BLK, BLK), bias))
    return places


def causal():
    u = lax.broadcasted_iota(jnp.int32, (BLK, BLK), 0)
    t = lax.broadcasted_iota(jnp.int32, (BLK, BLK), 1)
    return u <= t


def forward_body(table, x_ref, y_ref, o_ref, lse_ref, kv, qs, sems):
    copies = load_pool(x_ref, y_ref, kv, qs, sems)
    for copy in copies:
        copy.start()
    for copy in copies:
        copy.wait()

    def block(c, i):
        places = listed(table, c, i)
        q = qs[c, pl.ds(i * BLK, BLK), :]
        raw = [dot(kv[p, pl.ds(r, BLK), :], q, 1, 1) for p, r, _ in places]
        raw[0] = jnp.where(causal(), raw[0], NEG)
        peak = jnp.max(raw[0], axis=0, keepdims=True)
        for (_, _, bias), s in zip(places[1:], raw[1:]):
            peak = jnp.maximum(peak, jnp.max(s, axis=0, keepdims=True) - bias)
        peak = peak * SCALE2
        weights = []
        total = None
        for (_, _, bias), s in zip(places, raw):
            w = jnp.exp2(s * SCALE2 - (peak if bias is None else peak + bias))
            part = jnp.sum(w, axis=0, keepdims=True)
            total = part if total is None else total + part
            weights.append(w)
        inverse = 1.0 / total
        out = None
        for (p, r, _), w in zip(places, weights):
            v = kv[p, pl.ds(TOK + r, BLK), :]
            part = dot(v, (w * inverse).astype(bf16), 0, 0)
            out = part if out is None else out + part
        return out.astype(bf16), peak + jnp.log2(total)

    def step(c, carry):
        lses = []
        for i in range(2):
            out, lse = block(c, i)
            for g in range(8):
                row = (g % 2) * 64 + (g // 2) * 16
                o_ref[c, row : row + 16, i * BLK : (i + 1) * BLK] = out[g * 16 : g * 16 + 16, :]
            lses.append(lse)
        row = lax.broadcasted_iota(jnp.int32, (8, 128), 0)
        lse_ref[c] = jnp.where(row == 0, lses[0], lses[1])
        return carry

    lax.fori_loop(0, CHIPS, step, 0)


def attention_forward(table, x, y):
    return pl.pallas_call(
        forward_body,
        out_shape=(
            jax.ShapeDtypeStruct((CHIPS, HEAD, TOK), bf16),
            jax.ShapeDtypeStruct((CHIPS, 8, 128), f32),
        ),
        in_specs=[pl.BlockSpec(memory_space=pltpu.SMEM)] + [pl.BlockSpec(memory_space=pl.ANY)] * 2,
        out_specs=[pl.BlockSpec(memory_space=pltpu.VMEM)] * 2,
        scratch_shapes=[
            pltpu.VMEM((2 * CHIPS, 2 * TOK, HEAD), bf16),
            pltpu.VMEM((CHIPS, TOK, HEAD), bf16),
            pltpu.SemaphoreType.DMA((3,)),
        ],
        compiler_params=pltpu.CompilerParams(vmem_limit_bytes=VMEM_LIMIT),
        name="attn_fwd",
    )(table, x, y)


def backward_body(table, x_ref, y_ref, g_ref, lse_ref, own_ref, other_ref, gq_ref, kv, qs, acc, sems):
    copies = load_pool(x_ref, y_ref, kv, qs, sems)
    for copy in copies:
        copy.start()

    def clear(j, carry):
        acc[j] = jnp.zeros((2 * TOK, HEAD), f32)
        return carry

    lax.fori_loop(0, 2 * CHIPS, clear, 0)
    for copy in copies:
        copy.wait()

    def block(c, i):
        places = listed(table, c, i)
        q = qs[c, pl.ds(i * BLK, BLK), :]
        g = g_ref[c, pl.ds(i * BLK, BLK), :]
        lse = lse_ref[c, i : i + 1, :]
        probs, grads = [], []
        row_dot = None
        for p, r, bias in places:
            s = dot(kv[p, pl.ds(r, BLK), :], q, 1, 1)
            prob = jnp.exp2(s * SCALE2 - (lse if bias is None else lse + bias))
            if bias is None:
                prob = jnp.where(causal(), prob, 0.0)
            grad = dot(kv[p, pl.ds(TOK + r, BLK), :], g, 1, 1)
            part = jnp.sum(prob * grad, axis=0, keepdims=True)
            row_dot = part if row_dot is None else row_dot + part
            probs.append(prob)
            grads.append(grad)
        gq = None
        for (p, r, _), prob, grad in zip(places, probs, grads):
            score = (prob * (grad - row_dot) * SCALE).astype(bf16)
            acc[p, pl.ds(r, BLK), :] += dot(score, q, 1, 0)
            acc[p, pl.ds(TOK + r, BLK), :] += dot(prob.astype(bf16), g, 1, 0)
            part = dot(score, kv[p, pl.ds(r, BLK), :], 0, 0)
            gq = part if gq is None else gq + part
        gq_ref[c, pl.ds(i * BLK, BLK), :] = gq.astype(bf16)

    def step(c, carry):
        for i in range(2):
            block(c, i)
        return carry

    lax.fori_loop(0, CHIPS, step, 0)

    def flush(j, carry):
        own_ref[j] = acc[j]
        other_ref[j] = acc[CHIPS + j].astype(bf16)
        return carry

    lax.fori_loop(0, CHIPS, flush, 0)


def attention_backward(table, x, y, g, lse):
    return pl.pallas_call(
        backward_body,
        out_shape=(
            jax.ShapeDtypeStruct((CHIPS, 2 * TOK, HEAD), f32),
            jax.ShapeDtypeStruct((CHIPS, 2 * TOK, HEAD), bf16),
            jax.ShapeDtypeStruct((CHIPS, TOK, HEAD), bf16),
        ),
        in_specs=[pl.BlockSpec(memory_space=pltpu.SMEM)]
        + [pl.BlockSpec(memory_space=pl.ANY)] * 2
        + [pl.BlockSpec(memory_space=pltpu.VMEM)] * 2,
        out_specs=[pl.BlockSpec(memory_space=pltpu.VMEM)] * 3,
        scratch_shapes=[
            pltpu.VMEM((2 * CHIPS, 2 * TOK, HEAD), bf16),
            pltpu.VMEM((CHIPS, TOK, HEAD), bf16),
            pltpu.VMEM((2 * CHIPS, 2 * TOK, HEAD), f32),
            pltpu.SemaphoreType.DMA((3,)),
        ],
        compiler_params=pltpu.CompilerParams(vmem_limit_bytes=VMEM_LIMIT),
        name="attn_bwd",
    )(table, x, y, g, lse)


def combine_body(own_ref, got_ref, gq_ref, o_ref):
    o_ref[:, 0 : 2 * TOK, :] = (own_ref[...] + got_ref[...].astype(f32)).astype(bf16)
    o_ref[:, 2 * TOK : 3 * TOK, :] = gq_ref[...]


def combine(own, got, gq):
    n = 4
    return pl.pallas_call(
        combine_body,
        out_shape=jax.ShapeDtypeStruct((CHIPS, 3 * TOK, HEAD), bf16),
        grid=(CHIPS // n,),
        in_specs=[
            pl.BlockSpec((n, 2 * TOK, HEAD), lambda i: (i, 0, 0)),
            pl.BlockSpec((n, 2 * TOK, HEAD), lambda i: (i, 0, 0)),
            pl.BlockSpec((n, TOK, HEAD), lambda i: (i, 0, 0)),
        ],
        out_specs=pl.BlockSpec((n, 3 * TOK, HEAD), lambda i: (i, 0, 0)),
        compiler_params=pltpu.CompilerParams(vmem_limit_bytes=VMEM_LIMIT),
        name="combine",
    )(own, got, gq)


def weight_body(core, oa_ref, ob_ref, ca_ref, cb_ref, w_ref):
    a = oa_ref[...].reshape(4 * 64, TOK)
    b = ob_ref[...].reshape(4 * 64, TOK)
    w_ref[...] = (dot(a, ca_ref[...], 1, 0) + dot(b, cb_ref[...], 1, 0)).astype(bf16)


def weight_partial(core, oa, ob, ca, cb):
    return pl.pallas_call(
        weight_body,
        out_shape=jax.ShapeDtypeStruct((HEADS * 64, D), bf16),
        grid_spec=pltpu.PrefetchScalarGridSpec(
            num_scalar_prefetch=1,
            grid=(HEADS // 4,),
            in_specs=[
                pl.BlockSpec((4, 64, TOK), lambda i, core: (i, core[0], 0)),
                pl.BlockSpec((4, 64, TOK), lambda i, core: (i, core[0], 0)),
                pl.BlockSpec((TOK, D), lambda i, core: (0, 0)),
                pl.BlockSpec((TOK, D), lambda i, core: (0, 0)),
            ],
            out_specs=pl.BlockSpec((4 * 64, D), lambda i, core: (i, 0)),
        ),
        compiler_params=pltpu.CompilerParams(vmem_limit_bytes=VMEM_LIMIT),
        name="weight_partial",
    )(core, oa, ob, ca, cb)


def block_table(rider, core):
    offsets = rider.reshape(CHIPS, 2, SLOTS).astype(jnp.int32)
    c = jnp.arange(CHIPS, dtype=jnp.int32)[:, None, None]
    i = jnp.arange(2, dtype=jnp.int32)[None, :, None]
    target = 4 * c + 2 * core + i - offsets
    side = ((target >> 1) & 1) ^ core
    place = ((side * CHIPS + (target >> 2)) << 1) + (target & 1)
    return jnp.where(target >= 0, place, -1).reshape(2 * CHIPS, SLOTS)


def local(queries, key_states, value_states, out_weight, cotangent, block_offsets):
    core = lax.axis_index("seq") % 2
    cot = cotangent[0]
    x = exchange(pack(block_offsets[0], key_states[0], value_states[0], queries[0]))
    g = exchange(grad_attn_by_head(cot, out_weight))
    cot_other = lax.ppermute(cot, "seq", CORE_SWAP)
    y = lax.ppermute(x, "seq", CORE_SWAP)
    table = block_table(x[:, RIDER, 0 : 2 * SLOTS], core)
    out, lse = attention_forward(table, x, y)
    out_home = exchange(out)
    out_other = lax.ppermute(out_home, "seq", CORE_SWAP)
    own, other, gq = attention_backward(table, x, y, g, lse)
    got = lax.ppermute(other, "seq", CORE_SWAP)
    home = exchange(combine(own, got, gq))
    partial = weight_partial(core.reshape(1), out_home, out_other, cot, cot_other)
    by_doc = lax.psum_scatter(partial, "dp", scatter_dimension=0, tiled=True)
    pieces = exchange(by_doc.reshape(CHIPS, 16, D))
    weight_grad = jnp.sum(pieces.astype(f32), axis=0)
    gk, gv, gq = unpack(home)
    return gq[None], gk[None], gv[None], weight_grad


def solution(mesh):
    in_specs = (
        P("dp", "seq", None),
        P("dp", "seq", None),
        P("dp", "seq", None),
        P(),
        P("dp", "seq", None),
        P("dp", "seq", None),
    )
    out_specs = (
        P("dp", "seq", None),
        P("dp", "seq", None),
        P("dp", "seq", None),
        P(("dp", "seq"), None),
    )
    return jax.shard_map(local, mesh=mesh, in_specs=in_specs, out_specs=out_specs, check_vma=False)
```

```python
import math

import jax
import jax.numpy as jnp
from jax import lax
from jax.experimental import pallas as pl
from jax.experimental.pallas import tpu as pltpu
from jax.sharding import PartitionSpec as P

HEADS = 16
HEAD = 128
BLK = 128
SLOTS = 4
D = HEADS * HEAD
TOK = 256
CHIPS = 16
BLOCKS = 64
RIDER = 3 * TOK
ROWS = 3 * TOK + 8
SCALE = HEAD ** (-0.5)
SCALE2 = SCALE * math.log2(math.e)
NEG = -1e30
bf16 = jnp.bfloat16
f32 = jnp.float32

SAME_CORE = [[2 * c + k for c in range(CHIPS)] for k in range(2)]
CORE_SWAP = [(i, i ^ 1) for i in range(2 * CHIPS)]

PACK = 4
VMEM_LIMIT = 56 * 1024 * 1024


def dot(a, b, ca, cb):
    return lax.dot_general(a, b, (((ca,), (cb,)), ((), ())), preferred_element_type=f32)


def cost(flops, transcendentals=0, bytes_accessed=0):
    return pl.CostEstimate(
        flops=flops, transcendentals=transcendentals, bytes_accessed=bytes_accessed
    )


PAIRS = BLOCKS // 2 * BLK * (1 + SLOTS) * BLK
PAIR_FLOPS = 2 * HEAD * PAIRS
MIB = 1024 * 1024


def exchange(x):
    return lax.all_to_all(x, "seq", 0, 0, axis_index_groups=SAME_CORE, tiled=True)


def after(*values):
    return lax.optimization_barrier(values)


def pack_body(offs, k_ref, v_ref, q_ref, x_ref):
    lane = lax.broadcasted_iota(jnp.int32, (8, 128), 1)
    val = jnp.zeros((8, 128), jnp.int32)
    for j in range(2 * SLOTS):
        val = jnp.where(lane == j, offs[j // SLOTS, j % SLOTS], val)
    rider = val.astype(f32).astype(bf16)
    for h in range(PACK):
        for t, ref in enumerate((k_ref, v_ref, q_ref)):
            x_ref[h, t * TOK : (t + 1) * TOK, :] = ref[:, h * HEAD : (h + 1) * HEAD]
        x_ref[h, RIDER : RIDER + 8, :] = rider


def pack(offs, k, v, q):
    rows = pl.BlockSpec((TOK, PACK * HEAD), lambda i: (0, i))
    return pl.pallas_call(
        pack_body,
        out_shape=jax.ShapeDtypeStruct((HEADS, ROWS, HEAD), bf16),
        grid=(HEADS // PACK,),
        in_specs=[pl.BlockSpec(memory_space=pltpu.SMEM), rows, rows, rows],
        out_specs=pl.BlockSpec((PACK, ROWS, HEAD), lambda i: (i, 0, 0)),
        compiler_params=pltpu.CompilerParams(vmem_limit_bytes=VMEM_LIMIT),
        name="pack",
    )(offs, k, v, q)


def unpack_body(r_ref, *refs):
    for h in range(PACK):
        for t, ref in enumerate(refs):
            ref[:, h * HEAD : (h + 1) * HEAD] = r_ref[h, t * TOK : (t + 1) * TOK, :]


def unpack(r, n):
    out = jax.ShapeDtypeStruct((TOK, D), bf16)
    rows = pl.BlockSpec((TOK, PACK * HEAD), lambda i: (0, i))
    return pl.pallas_call(
        unpack_body,
        out_shape=(out,) * n,
        grid=(HEADS // PACK,),
        in_specs=[pl.BlockSpec((PACK, n * TOK, HEAD), lambda i: (i, 0, 0))],
        out_specs=[rows] * n,
        compiler_params=pltpu.CompilerParams(vmem_limit_bytes=VMEM_LIMIT),
        cost_estimate=cost(0, 0, 2 * n * MIB),
        name="unpack",
    )(r)


def grad_attn_body(c_ref, w_ref, o_ref):
    g = dot(c_ref[...], w_ref[...], 1, 1).astype(bf16)
    for j in range(2):
        o_ref[j] = g[:, j * HEAD : (j + 1) * HEAD]


def grad_attn_by_head(cot, weight):
    return pl.pallas_call(
        grad_attn_body,
        out_shape=jax.ShapeDtypeStruct((HEADS, TOK, HEAD), bf16),
        grid=(HEADS // 2,),
        in_specs=[
            pl.BlockSpec((TOK, D), lambda i: (0, 0)),
            pl.BlockSpec((2 * HEAD, D), lambda i: (i, 0)),
        ],
        out_specs=pl.BlockSpec((2, TOK, HEAD), lambda i: (i, 0, 0)),
        compiler_params=pltpu.CompilerParams(vmem_limit_bytes=VMEM_LIMIT),
        cost_estimate=cost(2 * TOK * D * D, 0, 10 * MIB),
        name="grad_attn",
    )(cot, weight)


def load_pool(x_ref, y_ref, kv, qs, sems):
    return [
        pltpu.make_async_copy(x_ref.at[:, pl.ds(0, 2 * TOK), :], kv.at[pl.ds(0, CHIPS)], sems.at[0]),
        pltpu.make_async_copy(y_ref.at[:, pl.ds(0, 2 * TOK), :], kv.at[pl.ds(CHIPS, CHIPS)], sems.at[1]),
        pltpu.make_async_copy(x_ref.at[:, pl.ds(2 * TOK, TOK), :], qs, sems.at[2]),
    ]


def listed(table, c, i):
    places = [(c, i * BLK, None)]
    for s in range(SLOTS):
        code = table[2 * c + i, s]
        f = jnp.maximum(code, 0)
        bias = jnp.where(code >= 0, 0.0, -NEG).astype(f32)
        places.append((f // 2, pl.multiple_of((f % 2) * BLK, BLK), bias))
    return places


def causal():
    u = lax.broadcasted_iota(jnp.int32, (BLK, BLK), 0)
    t = lax.broadcasted_iota(jnp.int32, (BLK, BLK), 1)
    return u <= t


def forward_body(table, x_ref, y_ref, o_ref, lse_ref, kv, qs, sems):
    copies = load_pool(x_ref, y_ref, kv, qs, sems)
    for copy in copies:
        copy.start()
    for copy in copies:
        copy.wait()

    def block(c, i):
        places = listed(table, c, i)
        q = qs[c, pl.ds(i * BLK, BLK), :]
        raw = [dot(kv[p, pl.ds(r, BLK), :], q, 1, 1) for p, r, _ in places]
        raw[0] = jnp.where(causal(), raw[0], NEG)
        peak = jnp.max(raw[0], axis=0, keepdims=True)
        for (_, _, bias), s in zip(places[1:], raw[1:]):
            peak = jnp.maximum(peak, jnp.max(s, axis=0, keepdims=True) - bias)
        peak = peak * SCALE2
        weights = []
        total = None
        for (_, _, bias), s in zip(places, raw):
            w = jnp.exp2(s * SCALE2 - (peak if bias is None else peak + bias))
            part = jnp.sum(w, axis=0, keepdims=True)
            total = part if total is None else total + part
            weights.append(w)
        inverse = 1.0 / total
        out = None
        for (p, r, _), w in zip(places, weights):
            v = kv[p, pl.ds(TOK + r, BLK), :]
            part = dot(v, (w * inverse).astype(bf16), 0, 0)
            out = part if out is None else out + part
        return out.astype(bf16), peak + jnp.log2(total)

    def step(c, carry):
        lses = []
        for i in range(2):
            out, lse = block(c, i)
            for g in range(8):
                row = (g % 2) * 64 + (g // 2) * 16
                o_ref[c, row : row + 16, i * BLK : (i + 1) * BLK] = out[g * 16 : g * 16 + 16, :]
            lses.append(lse)
        row = lax.broadcasted_iota(jnp.int32, (8, 128), 0)
        lse_ref[c] = jnp.where(row == 0, lses[0], lses[1])
        return carry

    lax.fori_loop(0, CHIPS, step, 0)


def attention_forward(table, x, y):
    return pl.pallas_call(
        forward_body,
        out_shape=(
            jax.ShapeDtypeStruct((CHIPS, HEAD, TOK), bf16),
            jax.ShapeDtypeStruct((CHIPS, 8, 128), f32),
        ),
        in_specs=[pl.BlockSpec(memory_space=pltpu.SMEM)] + [pl.BlockSpec(memory_space=pl.ANY)] * 2,
        out_specs=[pl.BlockSpec(memory_space=pltpu.VMEM)] * 2,
        scratch_shapes=[
            pltpu.VMEM((2 * CHIPS, 2 * TOK, HEAD), bf16),
            pltpu.VMEM((CHIPS, TOK, HEAD), bf16),
            pltpu.SemaphoreType.DMA((3,)),
        ],
        compiler_params=pltpu.CompilerParams(vmem_limit_bytes=VMEM_LIMIT),
        cost_estimate=cost(2 * PAIR_FLOPS, PAIRS, 7 * MIB),
        name="attn_fwd",
    )(table, x, y)


def backward_body(table, x_ref, y_ref, g_ref, lse_ref, own_ref, other_ref, gq_ref, kv, qs, acc, sems):
    copies = load_pool(x_ref, y_ref, kv, qs, sems)
    for copy in copies:
        copy.start()

    def clear(j, carry):
        acc[j] = jnp.zeros((2 * TOK, HEAD), f32)
        return carry

    lax.fori_loop(0, 2 * CHIPS, clear, 0)
    for copy in copies:
        copy.wait()

    def block(c, i):
        places = listed(table, c, i)
        q = qs[c, pl.ds(i * BLK, BLK), :]
        g = g_ref[c, pl.ds(i * BLK, BLK), :]
        lse = lse_ref[c, i : i + 1, :]
        probs, grads = [], []
        row_dot = None
        for p, r, bias in places:
            s = dot(kv[p, pl.ds(r, BLK), :], q, 1, 1)
            prob = jnp.exp2(s * SCALE2 - (lse if bias is None else lse + bias))
            if bias is None:
                prob = jnp.where(causal(), prob, 0.0)
            grad = dot(kv[p, pl.ds(TOK + r, BLK), :], g, 1, 1)
            part = jnp.sum(prob * grad, axis=0, keepdims=True)
            row_dot = part if row_dot is None else row_dot + part
            probs.append(prob)
            grads.append(grad)
        gq = None
        for (p, r, _), prob, grad in zip(places, probs, grads):
            score = (prob * (grad - row_dot) * SCALE).astype(bf16)
            acc[p, pl.ds(r, BLK), :] += dot(score, q, 1, 0)
            acc[p, pl.ds(TOK + r, BLK), :] += dot(prob.astype(bf16), g, 1, 0)
            part = dot(score, kv[p, pl.ds(r, BLK), :], 0, 0)
            gq = part if gq is None else gq + part
        gq_ref[c, pl.ds(i * BLK, BLK), :] = gq.astype(bf16)

    def step(c, carry):
        for i in range(2):
            block(c, i)
        return carry

    lax.fori_loop(0, CHIPS, step, 0)

    def flush(j, carry):
        own_ref[j] = acc[j]
        other_ref[j] = acc[CHIPS + j].astype(bf16)
        return carry

    lax.fori_loop(0, CHIPS, flush, 0)


def attention_backward(table, x, y, g, lse):
    return pl.pallas_call(
        backward_body,
        out_shape=(
            jax.ShapeDtypeStruct((CHIPS, 2 * TOK, HEAD), f32),
            jax.ShapeDtypeStruct((CHIPS, 2 * TOK, HEAD), bf16),
            jax.ShapeDtypeStruct((CHIPS, TOK, HEAD), bf16),
        ),
        in_specs=[pl.BlockSpec(memory_space=pltpu.SMEM)]
        + [pl.BlockSpec(memory_space=pl.ANY)] * 2
        + [pl.BlockSpec(memory_space=pltpu.VMEM)] * 2,
        out_specs=[pl.BlockSpec(memory_space=pltpu.VMEM)] * 3,
        scratch_shapes=[
            pltpu.VMEM((2 * CHIPS, 2 * TOK, HEAD), bf16),
            pltpu.VMEM((CHIPS, TOK, HEAD), bf16),
            pltpu.VMEM((2 * CHIPS, 2 * TOK, HEAD), f32),
            pltpu.SemaphoreType.DMA((3,)),
        ],
        compiler_params=pltpu.CompilerParams(vmem_limit_bytes=VMEM_LIMIT),
        cost_estimate=cost(5 * PAIR_FLOPS, PAIRS, 14 * MIB),
        name="attn_bwd",
    )(table, x, y, g, lse)


def combine_body(own_ref, got_ref, o_ref):
    o_ref[...] = (own_ref[...] + got_ref[...].astype(f32)).astype(bf16)


def combine(own, got):
    n = 4
    rows = pl.BlockSpec((n, 2 * TOK, HEAD), lambda i: (i, 0, 0))
    return pl.pallas_call(
        combine_body,
        out_shape=jax.ShapeDtypeStruct((CHIPS, 2 * TOK, HEAD), bf16),
        grid=(CHIPS // n,),
        in_specs=[rows, rows],
        out_specs=rows,
        compiler_params=pltpu.CompilerParams(vmem_limit_bytes=VMEM_LIMIT),
        cost_estimate=cost(CHIPS * 2 * TOK * HEAD, 0, 8 * MIB),
        name="combine",
    )(own, got)


def weight_body(core, oa_ref, ob_ref, ca_ref, cb_ref, w_ref):
    a = oa_ref[...].reshape(4 * 64, TOK)
    b = ob_ref[...].reshape(4 * 64, TOK)
    w_ref[...] = (dot(a, ca_ref[...], 1, 0) + dot(b, cb_ref[...], 1, 0)).astype(bf16)


def weight_partial(core, oa, ob, ca, cb):
    return pl.pallas_call(
        weight_body,
        out_shape=jax.ShapeDtypeStruct((HEADS * 64, D), bf16),
        grid_spec=pltpu.PrefetchScalarGridSpec(
            num_scalar_prefetch=1,
            grid=(HEADS // 4,),
            in_specs=[
                pl.BlockSpec((4, 64, TOK), lambda i, core: (i, core[0], 0)),
                pl.BlockSpec((4, 64, TOK), lambda i, core: (i, core[0], 0)),
                pl.BlockSpec((TOK, D), lambda i, core: (0, 0)),
                pl.BlockSpec((TOK, D), lambda i, core: (0, 0)),
            ],
            out_specs=pl.BlockSpec((4 * 64, D), lambda i, core: (i, 0)),
        ),
        compiler_params=pltpu.CompilerParams(vmem_limit_bytes=VMEM_LIMIT),
        cost_estimate=cost(2 * TOK * D * D, 0, 8 * MIB),
        name="weight_partial",
    )(core, oa, ob, ca, cb)


def block_table(rider, core):
    offsets = rider.reshape(CHIPS, 2, SLOTS).astype(jnp.int32)
    c = jnp.arange(CHIPS, dtype=jnp.int32)[:, None, None]
    i = jnp.arange(2, dtype=jnp.int32)[None, :, None]
    target = 4 * c + 2 * core + i - offsets
    side = ((target >> 1) & 1) ^ core
    place = ((side * CHIPS + (target >> 2)) << 1) + (target & 1)
    return jnp.where(target >= 0, place, -1).reshape(2 * CHIPS, SLOTS)


def local(queries, key_states, value_states, out_weight, cotangent, block_offsets):
    core = lax.axis_index("seq") % 2
    cot = cotangent[0]
    cot_other = lax.ppermute(cot, "seq", CORE_SWAP)
    x = exchange(pack(block_offsets[0], key_states[0], value_states[0], queries[0]))
    x, g = after(x, grad_attn_by_head(cot, out_weight))
    y = lax.ppermute(x, "seq", CORE_SWAP)
    g = exchange(g)
    table = block_table(x[:, RIDER, 0 : 2 * SLOTS], core)
    out, lse = attention_forward(table, x, y)
    g, out = after(g, out)
    out_home = exchange(out)
    own, other, gq = attention_backward(table, x, y, g, lse)
    out_home, gq, other = after(out_home, gq, other)
    gq_home = exchange(gq)
    out_other = lax.ppermute(out_home, "seq", CORE_SWAP)
    partial = weight_partial(core.reshape(1), out_home, out_other, cot, cot_other)
    by_doc = lax.psum_scatter(partial, "dp", scatter_dimension=0, tiled=True)
    got = lax.ppermute(other, "seq", CORE_SWAP)
    gq_home, gathered = after(gq_home, combine(own, got))
    kv_home = exchange(gathered)
    kv_home, by_doc = after(kv_home, by_doc)
    pieces = exchange(by_doc.reshape(CHIPS, 16, D))
    weight_grad = jnp.sum(pieces.astype(f32), axis=0)
    (gq,) = unpack(gq_home, 1)
    gk, gv = unpack(kv_home, 2)
    return gq[None], gk[None], gv[None], weight_grad


def solution(mesh):
    in_specs = (
        P("dp", "seq", None),
        P("dp", "seq", None),
        P("dp", "seq", None),
        P(),
        P("dp", "seq", None),
        P("dp", "seq", None),
    )
    out_specs = (
        P("dp", "seq", None),
        P("dp", "seq", None),
        P("dp", "seq", None),
        P(("dp", "seq"), None),
    )
    return jax.shard_map(local, mesh=mesh, in_specs=in_specs, out_specs=out_specs, check_vma=False)
```

```python
import math

import jax
import jax.numpy as jnp
from jax import lax
from jax.experimental import pallas as pl
from jax.experimental.pallas import tpu as pltpu
from jax.sharding import PartitionSpec as P

HEADS = 16
HEAD = 128
BLK = 128
SLOTS = 4
D = HEADS * HEAD
TOK = 256
CHIPS = 16
BLOCKS = 64
RIDER = 3 * TOK
ROWS = 3 * TOK + 8
SCALE = HEAD ** (-0.5)
SCALE2 = SCALE * math.log2(math.e)
NEG = -1e30
bf16 = jnp.bfloat16
f32 = jnp.float32

SAME_CORE = [[2 * c + k for c in range(CHIPS)] for k in range(2)]
CORE_SWAP = [(i, i ^ 1) for i in range(2 * CHIPS)]

UNROLL = 4
GROUP = 4
PACK = 4
VMEM_LIMIT = 56 * 1024 * 1024


def dot(a, b, ca, cb):
    return lax.dot_general(a, b, (((ca,), (cb,)), ((), ())), preferred_element_type=f32)


def cost(flops, transcendentals=0, bytes_accessed=0):
    return pl.CostEstimate(
        flops=flops, transcendentals=transcendentals, bytes_accessed=bytes_accessed
    )


PAIRS = BLOCKS // 2 * BLK * (1 + SLOTS) * BLK
PAIR_FLOPS = 2 * HEAD * PAIRS
MIB = 1024 * 1024


def exchange(x):
    return lax.all_to_all(x, "seq", 0, 0, axis_index_groups=SAME_CORE, tiled=True)


def after(*values):
    return lax.optimization_barrier(values)


def pack_body(offs, k_ref, v_ref, q_ref, x_ref):
    lane = lax.broadcasted_iota(jnp.int32, (8, 128), 1)
    val = jnp.zeros((8, 128), jnp.int32)
    for j in range(2 * SLOTS):
        val = jnp.where(lane == j, offs[j // SLOTS, j % SLOTS], val)
    rider = val.astype(f32).astype(bf16)
    for h in range(PACK):
        for t, ref in enumerate((k_ref, v_ref, q_ref)):
            x_ref[h, t * TOK : (t + 1) * TOK, :] = ref[:, h * HEAD : (h + 1) * HEAD]
        x_ref[h, RIDER : RIDER + 8, :] = rider


def pack(offs, k, v, q):
    rows = pl.BlockSpec((TOK, PACK * HEAD), lambda i: (0, i))
    return pl.pallas_call(
        pack_body,
        out_shape=jax.ShapeDtypeStruct((HEADS, ROWS, HEAD), bf16),
        grid=(HEADS // PACK,),
        in_specs=[pl.BlockSpec(memory_space=pltpu.SMEM), rows, rows, rows],
        out_specs=pl.BlockSpec((PACK, ROWS, HEAD), lambda i: (i, 0, 0)),
        compiler_params=pltpu.CompilerParams(vmem_limit_bytes=VMEM_LIMIT),
        name="pack",
    )(offs, k, v, q)


def unpack_body(r_ref, *refs):
    for h in range(PACK):
        for t, ref in enumerate(refs):
            ref[:, h * HEAD : (h + 1) * HEAD] = r_ref[h, t * TOK : (t + 1) * TOK, :]


def unpack(r, n):
    out = jax.ShapeDtypeStruct((TOK, D), bf16)
    rows = pl.BlockSpec((TOK, PACK * HEAD), lambda i: (0, i))
    return pl.pallas_call(
        unpack_body,
        out_shape=(out,) * n,
        grid=(HEADS // PACK,),
        in_specs=[pl.BlockSpec((PACK, n * TOK, HEAD), lambda i: (i, 0, 0))],
        out_specs=[rows] * n,
        compiler_params=pltpu.CompilerParams(vmem_limit_bytes=VMEM_LIMIT),
        cost_estimate=cost(0, 0, 2 * n * MIB),
        name="unpack",
    )(r)


def grad_attn_body(c_ref, w_ref, o_ref):
    g = dot(c_ref[...], w_ref[...], 1, 1).astype(bf16)
    for j in range(2):
        o_ref[j] = g[:, j * HEAD : (j + 1) * HEAD]


def grad_attn_by_head(cot, weight):
    return pl.pallas_call(
        grad_attn_body,
        out_shape=jax.ShapeDtypeStruct((HEADS, TOK, HEAD), bf16),
        grid=(HEADS // 2,),
        in_specs=[
            pl.BlockSpec((TOK, D), lambda i: (0, 0)),
            pl.BlockSpec((2 * HEAD, D), lambda i: (i, 0)),
        ],
        out_specs=pl.BlockSpec((2, TOK, HEAD), lambda i: (i, 0, 0)),
        compiler_params=pltpu.CompilerParams(vmem_limit_bytes=VMEM_LIMIT),
        cost_estimate=cost(2 * TOK * D * D, 0, 10 * MIB),
        name="grad_attn",
    )(cot, weight)


def load_pool(x_ref, y_ref, kv, qs, sems):
    groups = []
    for j in range(CHIPS // GROUP):
        at = pl.ds(j * GROUP, GROUP)
        groups.append(
            [
                pltpu.make_async_copy(
                    x_ref.at[at, pl.ds(0, 2 * TOK), :], kv.at[at], sems.at[3 * j]
                ),
                pltpu.make_async_copy(
                    y_ref.at[at, pl.ds(0, 2 * TOK), :],
                    kv.at[pl.ds(CHIPS + j * GROUP, GROUP)],
                    sems.at[3 * j + 1],
                ),
                pltpu.make_async_copy(
                    x_ref.at[at, pl.ds(2 * TOK, TOK), :], qs.at[at], sems.at[3 * j + 2]
                ),
            ]
        )
    return groups


def listed(table, c, i):
    places = [(c, i * BLK, None)]
    for s in range(SLOTS):
        code = table[2 * c + i, s]
        f = jnp.maximum(code, 0)
        bias = jnp.where(code >= 0, 0.0, -NEG).astype(f32)
        places.append((f // 2, pl.multiple_of((f % 2) * BLK, BLK), bias))
    return places


def causal():
    u = lax.broadcasted_iota(jnp.int32, (BLK, BLK), 0)
    t = lax.broadcasted_iota(jnp.int32, (BLK, BLK), 1)
    return u <= t


def forward_body(table, x_ref, y_ref, o_ref, lse_ref, kv, qs, sems):
    groups = load_pool(x_ref, y_ref, kv, qs, sems)
    for copies in groups:
        for copy in copies:
            copy.start()

    def block(c, i):
        places = listed(table, c, i)
        q = qs[c, pl.ds(i * BLK, BLK), :]
        keys = jnp.concatenate([kv[p, pl.ds(r, BLK), :] for p, r, _ in places], axis=0)
        every = dot(keys, q, 1, 1)
        raw = [every[s * BLK : (s + 1) * BLK, :] for s in range(1 + SLOTS)]
        raw[0] = jnp.where(causal(), raw[0], NEG)
        peak = jnp.max(raw[0], axis=0, keepdims=True)
        for (_, _, bias), s in zip(places[1:], raw[1:]):
            peak = jnp.maximum(peak, jnp.max(s, axis=0, keepdims=True) - bias)
        peak = peak * SCALE2
        weights = []
        total = None
        for (_, _, bias), s in zip(places, raw):
            w = jnp.exp2(s * SCALE2 - (peak if bias is None else peak + bias))
            part = jnp.sum(w, axis=0, keepdims=True)
            total = part if total is None else total + part
            weights.append(w.astype(bf16))
        values = jnp.concatenate([kv[p, pl.ds(TOK + r, BLK), :] for p, r, _ in places], axis=0)
        out = dot(values, jnp.concatenate(weights, axis=0), 0, 0) * (1.0 / total)
        return out.astype(bf16), peak + jnp.log2(total)

    def step(c, carry):
        lses = []
        for i in range(2):
            out, lse = block(c, i)
            for g in range(8):
                row = (g % 2) * 64 + (g // 2) * 16
                o_ref[c, row : row + 16, i * BLK : (i + 1) * BLK] = out[g * 16 : g * 16 + 16, :]
            lses.append(lse)
        row = lax.broadcasted_iota(jnp.int32, (8, 128), 0)
        lse_ref[c] = jnp.where(row == 0, lses[0], lses[1])
        return carry

    for j, copies in enumerate(groups):
        for copy in copies:
            copy.wait()
        lax.fori_loop(j * GROUP, (j + 1) * GROUP, step, 0, unroll=UNROLL)


def attention_forward(table, x, y):
    return pl.pallas_call(
        forward_body,
        out_shape=(
            jax.ShapeDtypeStruct((CHIPS, HEAD, TOK), bf16),
            jax.ShapeDtypeStruct((CHIPS, 8, 128), f32),
        ),
        in_specs=[pl.BlockSpec(memory_space=pltpu.SMEM)] + [pl.BlockSpec(memory_space=pl.ANY)] * 2,
        out_specs=[pl.BlockSpec(memory_space=pltpu.VMEM)] * 2,
        scratch_shapes=[
            pltpu.VMEM((2 * CHIPS, 2 * TOK, HEAD), bf16),
            pltpu.VMEM((CHIPS, TOK, HEAD), bf16),
            pltpu.SemaphoreType.DMA((3 * (CHIPS // GROUP),)),
        ],
        compiler_params=pltpu.CompilerParams(vmem_limit_bytes=VMEM_LIMIT),
        cost_estimate=cost(2 * PAIR_FLOPS, PAIRS, 7 * MIB),
        name="attn_fwd",
    )(table, x, y)


def backward_body(
    table, x_ref, y_ref, g_ref, lse_ref, home_ref, other_ref, kv, qs, gs, acck, accv, own, other, gq, sems
):
    groups = load_pool(x_ref, y_ref, kv, qs, sems)
    sends = []
    n = CHIPS // GROUP
    for j in range(n):
        at = pl.ds(j * GROUP, GROUP)
        groups[j].append(pltpu.make_async_copy(g_ref.at[at], gs.at[at], sems.at[3 * n + j]))
        sends.append(
            [
                pltpu.make_async_copy(
                    gq.at[at], home_ref.at[at, pl.ds(2 * TOK, TOK), :], sems.at[4 * n + j]
                ),
                pltpu.make_async_copy(
                    own.at[at], home_ref.at[at, pl.ds(0, 2 * TOK), :], sems.at[5 * n + j]
                ),
                pltpu.make_async_copy(other.at[at], other_ref.at[at], sems.at[6 * n + j]),
            ]
        )
    for copies in groups:
        for copy in copies:
            copy.start()

    def clear(j, carry):
        acck[CHIPS + j] = jnp.zeros((TOK, HEAD), f32)
        accv[CHIPS + j] = jnp.zeros((TOK, HEAD), f32)
        return carry

    lax.fori_loop(0, CHIPS, clear, 0)

    def block(c, i):
        places = listed(table, c, i)
        q = qs[c, pl.ds(i * BLK, BLK), :]
        g = gs[c, pl.ds(i * BLK, BLK), :]
        lse = lse_ref[c, i : i + 1, :]
        keys = jnp.concatenate([kv[p, pl.ds(r, BLK), :] for p, r, _ in places], axis=0)
        values = jnp.concatenate([kv[p, pl.ds(TOK + r, BLK), :] for p, r, _ in places], axis=0)
        every = dot(keys, q, 1, 1)
        grads = dot(values, g, 1, 1)
        probs = []
        for j, (_, _, bias) in enumerate(places):
            s = every[j * BLK : (j + 1) * BLK, :]
            prob = jnp.exp2(s * SCALE2 - (lse if bias is None else lse + bias))
            if bias is None:
                prob = jnp.where(causal(), prob, 0.0)
            probs.append(prob)
        prob = jnp.concatenate(probs, axis=0)
        row_dot = jnp.sum(prob * grads, axis=0, keepdims=True)
        score = (prob * (grads - row_dot)).astype(bf16)
        gk = dot(score, q, 1, 0)
        gv = dot(prob.astype(bf16), g, 1, 0)
        for j, (p, r, _) in enumerate(places):
            at = pl.ds(r, BLK)
            if j == 0:
                acck[p, at, :] = gk[0:BLK, :]
                accv[p, at, :] = gv[0:BLK, :]
            else:
                acck[p, at, :] += gk[j * BLK : (j + 1) * BLK, :]
                accv[p, at, :] += gv[j * BLK : (j + 1) * BLK, :]
        gq[c, pl.ds(i * BLK, BLK), :] = (dot(score, keys, 0, 0) * SCALE).astype(bf16)

    def step(c, carry):
        for i in range(2):
            block(c, i)
        return carry

    def flush(j, carry):
        own[j, 0:TOK, :] = (acck[j] * SCALE).astype(bf16)
        own[j, TOK : 2 * TOK, :] = accv[j].astype(bf16)
        other[j, 0:TOK, :] = (acck[CHIPS + j] * SCALE).astype(bf16)
        other[j, TOK : 2 * TOK, :] = accv[CHIPS + j].astype(bf16)
        return carry

    for j in range(n + 2):
        if j < n:
            for copy in groups[j]:
                copy.wait()
            lax.fori_loop(j * GROUP, (j + 1) * GROUP, step, 0, unroll=UNROLL)
            sends[j][0].start()
        if j >= 2:
            lax.fori_loop((j - 2) * GROUP, (j - 1) * GROUP, flush, 0)
            sends[j - 2][1].start()
            sends[j - 2][2].start()
    for copies in sends:
        for copy in copies:
            copy.wait()


def attention_backward(table, x, y, g, lse):
    return pl.pallas_call(
        backward_body,
        out_shape=(
            jax.ShapeDtypeStruct((CHIPS, 3 * TOK, HEAD), bf16),
            jax.ShapeDtypeStruct((CHIPS, 2 * TOK, HEAD), bf16),
        ),
        in_specs=[pl.BlockSpec(memory_space=pltpu.SMEM)]
        + [pl.BlockSpec(memory_space=pl.ANY)] * 3
        + [pl.BlockSpec(memory_space=pltpu.VMEM)],
        out_specs=[pl.BlockSpec(memory_space=pl.ANY)] * 2,
        scratch_shapes=[
            pltpu.VMEM((2 * CHIPS, 2 * TOK, HEAD), bf16),
            pltpu.VMEM((CHIPS, TOK, HEAD), bf16),
            pltpu.VMEM((CHIPS, TOK, HEAD), bf16),
            pltpu.VMEM((2 * CHIPS, TOK, HEAD), f32),
            pltpu.VMEM((2 * CHIPS, TOK, HEAD), f32),
            pltpu.VMEM((CHIPS, 2 * TOK, HEAD), bf16),
            pltpu.VMEM((CHIPS, 2 * TOK, HEAD), bf16),
            pltpu.VMEM((CHIPS, TOK, HEAD), bf16),
            pltpu.SemaphoreType.DMA((7 * (CHIPS // GROUP),)),
        ],
        compiler_params=pltpu.CompilerParams(vmem_limit_bytes=VMEM_LIMIT),
        cost_estimate=cost(5 * PAIR_FLOPS, PAIRS, 14 * MIB),
        name="attn_bwd",
    )(table, x, y, g, lse)


def combine_body(own_ref, got_ref, o_ref):
    o_ref[...] = (own_ref[...].astype(f32) + got_ref[...].astype(f32)).astype(bf16)


def combine(home, got):
    n = 4
    rows = pl.BlockSpec((n, 2 * TOK, HEAD), lambda i: (i, 0, 0))
    return pl.pallas_call(
        combine_body,
        out_shape=jax.ShapeDtypeStruct((CHIPS, 3 * TOK, HEAD), bf16),
        grid=(CHIPS // n,),
        in_specs=[rows, rows],
        out_specs=rows,
        input_output_aliases={0: 0},
        compiler_params=pltpu.CompilerParams(vmem_limit_bytes=VMEM_LIMIT),
        cost_estimate=cost(CHIPS * 2 * TOK * HEAD, 0, 6 * MIB),
        name="combine",
    )(home, got)


def weight_body(core, oa_ref, ob_ref, ca_ref, cb_ref, w_ref):
    a = oa_ref[...].reshape(HEADS * 64, TOK)
    b = ob_ref[...].reshape(HEADS * 64, TOK)
    w_ref[...] = (dot(a, ca_ref[...], 1, 0) + dot(b, cb_ref[...], 1, 0)).astype(bf16)


def weight_partial(core, oa, ob, ca, cb):
    n = 4
    rows = pl.BlockSpec((HEADS, 64, TOK), lambda i, core: (0, core[0], 0))
    columns = pl.BlockSpec((TOK, D // n), lambda i, core: (0, i))
    return pl.pallas_call(
        weight_body,
        out_shape=jax.ShapeDtypeStruct((HEADS * 64, D), bf16),
        grid_spec=pltpu.PrefetchScalarGridSpec(
            num_scalar_prefetch=1,
            grid=(n,),
            in_specs=[rows, rows, columns, columns],
            out_specs=pl.BlockSpec((HEADS * 64, D // n), lambda i, core: (0, i)),
        ),
        compiler_params=pltpu.CompilerParams(vmem_limit_bytes=VMEM_LIMIT),
        cost_estimate=cost(2 * TOK * D * D, 0, 8 * MIB),
        name="weight_partial",
    )(core, oa, ob, ca, cb)


def block_table(rider, core):
    offsets = rider.reshape(CHIPS, 2, SLOTS).astype(jnp.int32)
    c = jnp.arange(CHIPS, dtype=jnp.int32)[:, None, None]
    i = jnp.arange(2, dtype=jnp.int32)[None, :, None]
    target = 4 * c + 2 * core + i - offsets
    side = ((target >> 1) & 1) ^ core
    place = ((side * CHIPS + (target >> 2)) << 1) + (target & 1)
    return jnp.where(target >= 0, place, -1).reshape(2 * CHIPS, SLOTS)


def local(queries, key_states, value_states, out_weight, cotangent, block_offsets):
    core = lax.axis_index("seq") % 2
    cot = cotangent[0]
    cot_other = lax.ppermute(cot, "seq", CORE_SWAP)
    x = exchange(pack(block_offsets[0], key_states[0], value_states[0], queries[0]))
    x, g, cot_other = after(x, grad_attn_by_head(cot, out_weight), cot_other)
    y = lax.ppermute(x, "seq", CORE_SWAP)
    g = exchange(g)
    table = block_table(x[:, RIDER, 0 : 2 * SLOTS], core)
    out, lse = attention_forward(table, x, y)
    g, out = after(g, out)
    out_home = exchange(out)
    own, other = attention_backward(table, x, y, g, lse)
    out_home, own, other = after(out_home, own, other)
    out_other = lax.ppermute(out_home, "seq", CORE_SWAP)
    out_other, other = after(out_other, other)
    got = lax.ppermute(other, "seq", CORE_SWAP)
    partial = weight_partial(core.reshape(1), out_home, out_other, cot, cot_other)
    partial, got = after(partial, got)
    by_doc = lax.psum_scatter(partial, "dp", scatter_dimension=0, tiled=True)
    home = exchange(combine(own, got))
    home, by_doc = after(home, by_doc)
    pieces = exchange(by_doc.reshape(CHIPS, 16, D))
    weight_grad = jnp.sum(pieces.astype(f32), axis=0)
    gk, gv, gq = unpack(home, 3)
    return gq[None], gk[None], gv[None], weight_grad


def solution(mesh):
    in_specs = (
        P("dp", "seq", None),
        P("dp", "seq", None),
        P("dp", "seq", None),
        P(),
        P("dp", "seq", None),
        P("dp", "seq", None),
    )
    out_specs = (
        P("dp", "seq", None),
        P("dp", "seq", None),
        P("dp", "seq", None),
        P(("dp", "seq"), None),
    )
    return jax.shard_map(local, mesh=mesh, in_specs=in_specs, out_specs=out_specs, check_vma=False)
```

```python
import math

import jax
import jax.numpy as jnp
from jax import lax
from jax.experimental import pallas as pl
from jax.experimental.pallas import tpu as pltpu
from jax.sharding import PartitionSpec as P

HEADS = 16
HEAD = 128
BLK = 128
SLOTS = 4
D = HEADS * HEAD
TOK = 256
CHIPS = 16
BLOCKS = 64
DOCS = 4
CHUNK = D // 4 // DOCS
RIDER = 3 * TOK
ROWS = 3 * TOK + 8
SCALE = HEAD ** (-0.5)
SCALE2 = SCALE * math.log2(math.e)
NEG = -1e30
bf16 = jnp.bfloat16
f32 = jnp.float32

SAME_CORE = [[2 * c + k for c in range(CHIPS)] for k in range(2)]
CORE_SWAP = [(i, i ^ 1) for i in range(2 * CHIPS)]

UNROLL = 4
GROUP = 4
PACK = 4
VMEM_LIMIT = 56 * 1024 * 1024


def dot(a, b, ca, cb):
    return lax.dot_general(a, b, (((ca,), (cb,)), ((), ())), preferred_element_type=f32)


def cost(flops, transcendentals=0, bytes_accessed=0):
    return pl.CostEstimate(
        flops=flops, transcendentals=transcendentals, bytes_accessed=bytes_accessed
    )


PAIRS = BLOCKS // 2 * BLK * (1 + SLOTS) * BLK
PAIR_FLOPS = 2 * HEAD * PAIRS
MIB = 1024 * 1024


def exchange(x):
    return lax.all_to_all(x, "seq", 0, 0, axis_index_groups=SAME_CORE, tiled=True)


def after(*values):
    return lax.optimization_barrier(values)


def pack_body(offs, k_ref, v_ref, q_ref, x_ref):
    lane = lax.broadcasted_iota(jnp.int32, (8, 128), 1)
    val = jnp.zeros((8, 128), jnp.int32)
    for j in range(2 * SLOTS):
        val = jnp.where(lane == j, offs[j // SLOTS, j % SLOTS], val)
    rider = val.astype(f32).astype(bf16)
    for h in range(PACK):
        for t, ref in enumerate((k_ref, v_ref, q_ref)):
            x_ref[h, t * TOK : (t + 1) * TOK, :] = ref[:, h * HEAD : (h + 1) * HEAD]
        x_ref[h, RIDER : RIDER + 8, :] = rider


def pack(offs, k, v, q):
    rows = pl.BlockSpec((TOK, PACK * HEAD), lambda i: (0, i))
    return pl.pallas_call(
        pack_body,
        out_shape=jax.ShapeDtypeStruct((HEADS, ROWS, HEAD), bf16),
        grid=(HEADS // PACK,),
        in_specs=[pl.BlockSpec(memory_space=pltpu.SMEM), rows, rows, rows],
        out_specs=pl.BlockSpec((PACK, ROWS, HEAD), lambda i: (i, 0, 0)),
        compiler_params=pltpu.CompilerParams(vmem_limit_bytes=VMEM_LIMIT),
        name="pack",
    )(offs, k, v, q)


def unpack_body(r_ref, *refs):
    for h in range(PACK):
        for t, ref in enumerate(refs):
            ref[:, h * HEAD : (h + 1) * HEAD] = r_ref[h, t * TOK : (t + 1) * TOK, :]


def unpack(r, n):
    out = jax.ShapeDtypeStruct((TOK, D), bf16)
    rows = pl.BlockSpec((TOK, PACK * HEAD), lambda i: (0, i))
    return pl.pallas_call(
        unpack_body,
        out_shape=(out,) * n,
        grid=(HEADS // PACK,),
        in_specs=[pl.BlockSpec((PACK, n * TOK, HEAD), lambda i: (i, 0, 0))],
        out_specs=[rows] * n,
        compiler_params=pltpu.CompilerParams(vmem_limit_bytes=VMEM_LIMIT),
        cost_estimate=cost(0, 0, 2 * n * MIB),
        name="unpack",
    )(r)


def grad_attn_body(c_ref, w_ref, o_ref):
    g = dot(c_ref[...], w_ref[...], 1, 1).astype(bf16)
    for j in range(2):
        o_ref[j] = g[:, j * HEAD : (j + 1) * HEAD]


def grad_attn_by_head(cot, weight):
    return pl.pallas_call(
        grad_attn_body,
        out_shape=jax.ShapeDtypeStruct((HEADS, TOK, HEAD), bf16),
        grid=(HEADS // 2,),
        in_specs=[
            pl.BlockSpec((TOK, D), lambda i: (0, 0)),
            pl.BlockSpec((2 * HEAD, D), lambda i: (i, 0)),
        ],
        out_specs=pl.BlockSpec((2, TOK, HEAD), lambda i: (i, 0, 0)),
        compiler_params=pltpu.CompilerParams(vmem_limit_bytes=VMEM_LIMIT),
        cost_estimate=cost(2 * TOK * D * D, 0, 10 * MIB),
        name="grad_attn",
    )(cot, weight)


def load_pool(x_ref, y_ref, kv, qs, sems):
    groups = []
    for j in range(CHIPS // GROUP):
        at = pl.ds(j * GROUP, GROUP)
        groups.append(
            [
                pltpu.make_async_copy(
                    x_ref.at[at, pl.ds(0, 2 * TOK), :], kv.at[at], sems.at[3 * j]
                ),
                pltpu.make_async_copy(
                    y_ref.at[at, pl.ds(0, 2 * TOK), :],
                    kv.at[pl.ds(CHIPS + j * GROUP, GROUP)],
                    sems.at[3 * j + 1],
                ),
                pltpu.make_async_copy(
                    x_ref.at[at, pl.ds(2 * TOK, TOK), :], qs.at[at], sems.at[3 * j + 2]
                ),
            ]
        )
    return groups


def listed(table, c, i):
    places = [(c, i * BLK, None)]
    for s in range(SLOTS):
        code = table[2 * c + i, s]
        f = jnp.maximum(code, 0)
        bias = jnp.where(code >= 0, 0.0, -NEG).astype(f32)
        places.append((f // 2, pl.multiple_of((f % 2) * BLK, BLK), bias))
    return places


def causal():
    u = lax.broadcasted_iota(jnp.int32, (BLK, BLK), 0)
    t = lax.broadcasted_iota(jnp.int32, (BLK, BLK), 1)
    return u <= t


def forward_body(table, x_ref, y_ref, o_ref, lse_ref, kv, qs, sems):
    groups = load_pool(x_ref, y_ref, kv, qs, sems)
    for copies in groups:
        for copy in copies:
            copy.start()

    def block(c, i):
        places = listed(table, c, i)
        q = qs[c, pl.ds(i * BLK, BLK), :]
        keys = jnp.concatenate([kv[p, pl.ds(r, BLK), :] for p, r, _ in places], axis=0)
        every = dot(keys, q, 1, 1)
        raw = [every[s * BLK : (s + 1) * BLK, :] for s in range(1 + SLOTS)]
        raw[0] = jnp.where(causal(), raw[0], NEG)
        peak = jnp.max(raw[0], axis=0, keepdims=True)
        for (_, _, bias), s in zip(places[1:], raw[1:]):
            peak = jnp.maximum(peak, jnp.max(s, axis=0, keepdims=True) - bias)
        peak = peak * SCALE2
        weights = []
        total = None
        for (_, _, bias), s in zip(places, raw):
            w = jnp.exp2(s * SCALE2 - (peak if bias is None else peak + bias))
            part = jnp.sum(w, axis=0, keepdims=True)
            total = part if total is None else total + part
            weights.append(w.astype(bf16))
        values = jnp.concatenate([kv[p, pl.ds(TOK + r, BLK), :] for p, r, _ in places], axis=0)
        out = dot(values, jnp.concatenate(weights, axis=0), 0, 0) * (1.0 / total)
        return out.astype(bf16), peak + jnp.log2(total)

    def step(c, carry):
        lses = []
        for i in range(2):
            out, lse = block(c, i)
            for g in range(8):
                row = (g % 2) * 64 + (g // 2) * 16
                o_ref[c, row : row + 16, i * BLK : (i + 1) * BLK] = out[g * 16 : g * 16 + 16, :]
            lses.append(lse)
        row = lax.broadcasted_iota(jnp.int32, (8, 128), 0)
        lse_ref[c] = jnp.where(row == 0, lses[0], lses[1])
        return carry

    for j, copies in enumerate(groups):
        for copy in copies:
            copy.wait()
        lax.fori_loop(j * GROUP, (j + 1) * GROUP, step, 0, unroll=UNROLL)


def attention_forward(table, x, y):
    return pl.pallas_call(
        forward_body,
        out_shape=(
            jax.ShapeDtypeStruct((CHIPS, HEAD, TOK), bf16),
            jax.ShapeDtypeStruct((CHIPS, 8, 128), f32),
        ),
        in_specs=[pl.BlockSpec(memory_space=pltpu.SMEM)] + [pl.BlockSpec(memory_space=pl.ANY)] * 2,
        out_specs=[pl.BlockSpec(memory_space=pltpu.VMEM)] * 2,
        scratch_shapes=[
            pltpu.VMEM((2 * CHIPS, 2 * TOK, HEAD), bf16),
            pltpu.VMEM((CHIPS, TOK, HEAD), bf16),
            pltpu.SemaphoreType.DMA((3 * (CHIPS // GROUP),)),
        ],
        compiler_params=pltpu.CompilerParams(vmem_limit_bytes=VMEM_LIMIT),
        cost_estimate=cost(2 * PAIR_FLOPS, PAIRS, 7 * MIB),
        name="attn_fwd",
    )(table, x, y)


def backward_body(
    table, x_ref, y_ref, g_ref, lse_ref, home_ref, other_ref, kv, qs, gs, acck, accv, own, other, gq, sems
):
    groups = load_pool(x_ref, y_ref, kv, qs, sems)
    sends = []
    n = CHIPS // GROUP
    for j in range(n):
        at = pl.ds(j * GROUP, GROUP)
        groups[j].append(pltpu.make_async_copy(g_ref.at[at], gs.at[at], sems.at[3 * n + j]))
        sends.append(
            [
                pltpu.make_async_copy(
                    gq.at[at], home_ref.at[at, pl.ds(2 * TOK, TOK), :], sems.at[4 * n + j]
                ),
                pltpu.make_async_copy(
                    own.at[at], home_ref.at[at, pl.ds(0, 2 * TOK), :], sems.at[5 * n + j]
                ),
                pltpu.make_async_copy(other.at[at], other_ref.at[at], sems.at[6 * n + j]),
            ]
        )
    for copies in groups:
        for copy in copies:
            copy.start()

    def clear(j, carry):
        acck[CHIPS + j] = jnp.zeros((TOK, HEAD), f32)
        accv[CHIPS + j] = jnp.zeros((TOK, HEAD), f32)
        return carry

    lax.fori_loop(0, CHIPS, clear, 0)

    def block(c, i):
        places = listed(table, c, i)
        q = qs[c, pl.ds(i * BLK, BLK), :]
        g = gs[c, pl.ds(i * BLK, BLK), :]
        lse = lse_ref[c, i : i + 1, :]
        keys = jnp.concatenate([kv[p, pl.ds(r, BLK), :] for p, r, _ in places], axis=0)
        values = jnp.concatenate([kv[p, pl.ds(TOK + r, BLK), :] for p, r, _ in places], axis=0)
        every = dot(keys, q, 1, 1)
        grads = dot(values, g, 1, 1)
        probs = []
        for j, (_, _, bias) in enumerate(places):
            s = every[j * BLK : (j + 1) * BLK, :]
            prob = jnp.exp2(s * SCALE2 - (lse if bias is None else lse + bias))
            if bias is None:
                prob = jnp.where(causal(), prob, 0.0)
            probs.append(prob)
        prob = jnp.concatenate(probs, axis=0)
        row_dot = jnp.sum(prob * grads, axis=0, keepdims=True)
        score = (prob * (grads - row_dot)).astype(bf16)
        gk = dot(score, q, 1, 0)
        gv = dot(prob.astype(bf16), g, 1, 0)
        for j, (p, r, _) in enumerate(places):
            at = pl.ds(r, BLK)
            if j == 0:
                acck[p, at, :] = gk[0:BLK, :]
                accv[p, at, :] = gv[0:BLK, :]
            else:
                acck[p, at, :] += gk[j * BLK : (j + 1) * BLK, :]
                accv[p, at, :] += gv[j * BLK : (j + 1) * BLK, :]
        gq[c, pl.ds(i * BLK, BLK), :] = (dot(score, keys, 0, 0) * SCALE).astype(bf16)

    def step(c, carry):
        for i in range(2):
            block(c, i)
        return carry

    def flush(j, carry):
        own[j, 0:TOK, :] = (acck[j] * SCALE).astype(bf16)
        own[j, TOK : 2 * TOK, :] = accv[j].astype(bf16)
        other[j, 0:TOK, :] = (acck[CHIPS + j] * SCALE).astype(bf16)
        other[j, TOK : 2 * TOK, :] = accv[CHIPS + j].astype(bf16)
        return carry

    for j in range(n + 2):
        if j < n:
            for copy in groups[j]:
                copy.wait()
            lax.fori_loop(j * GROUP, (j + 1) * GROUP, step, 0, unroll=UNROLL)
            sends[j][0].start()
        if j >= 2:
            lax.fori_loop((j - 2) * GROUP, (j - 1) * GROUP, flush, 0)
            sends[j - 2][1].start()
            sends[j - 2][2].start()
    for copies in sends:
        for copy in copies:
            copy.wait()


def attention_backward(table, x, y, g, lse):
    return pl.pallas_call(
        backward_body,
        out_shape=(
            jax.ShapeDtypeStruct((CHIPS, 3 * TOK, HEAD), bf16),
            jax.ShapeDtypeStruct((CHIPS, 2 * TOK, HEAD), bf16),
        ),
        in_specs=[pl.BlockSpec(memory_space=pltpu.SMEM)]
        + [pl.BlockSpec(memory_space=pl.ANY)] * 3
        + [pl.BlockSpec(memory_space=pltpu.VMEM)],
        out_specs=[pl.BlockSpec(memory_space=pl.ANY)] * 2,
        scratch_shapes=[
            pltpu.VMEM((2 * CHIPS, 2 * TOK, HEAD), bf16),
            pltpu.VMEM((CHIPS, TOK, HEAD), bf16),
            pltpu.VMEM((CHIPS, TOK, HEAD), bf16),
            pltpu.VMEM((2 * CHIPS, TOK, HEAD), f32),
            pltpu.VMEM((2 * CHIPS, TOK, HEAD), f32),
            pltpu.VMEM((CHIPS, 2 * TOK, HEAD), bf16),
            pltpu.VMEM((CHIPS, 2 * TOK, HEAD), bf16),
            pltpu.VMEM((CHIPS, TOK, HEAD), bf16),
            pltpu.SemaphoreType.DMA((7 * (CHIPS // GROUP),)),
        ],
        compiler_params=pltpu.CompilerParams(vmem_limit_bytes=VMEM_LIMIT),
        cost_estimate=cost(5 * PAIR_FLOPS, PAIRS, 14 * MIB),
        name="attn_bwd",
    )(table, x, y, g, lse)


def combine_body(own_ref, got_ref, o_ref):
    o_ref[...] = (own_ref[...].astype(f32) + got_ref[...].astype(f32)).astype(bf16)


def combine(home, got):
    n = 4
    rows = pl.BlockSpec((n, 2 * TOK, HEAD), lambda i: (i, 0, 0))
    return pl.pallas_call(
        combine_body,
        out_shape=jax.ShapeDtypeStruct((CHIPS, 3 * TOK, HEAD), bf16),
        grid=(CHIPS // n,),
        in_specs=[rows, rows],
        out_specs=rows,
        input_output_aliases={0: 0},
        compiler_params=pltpu.CompilerParams(vmem_limit_bytes=VMEM_LIMIT),
        cost_estimate=cost(CHIPS * 2 * TOK * HEAD, 0, 6 * MIB),
        name="combine",
    )(home, got)


def weight_body(place, oa_ref, ob_ref, ca_ref, cb_ref, *rest):
    outs, buf, sems = rest[: 2 * DOCS], rest[2 * DOCS], rest[2 * DOCS + 1]
    copies = []
    for d in (3, 1, 2, 0):
        heads = pl.ds(((place[1] + d) % DOCS) * (HEADS // DOCS), HEADS // DOCS)
        a = oa_ref[heads].reshape(2 * CHUNK, TOK)
        b = ob_ref[heads].reshape(2 * CHUNK, TOK)
        buf[d] = (dot(a, ca_ref[...], 1, 0) + dot(b, cb_ref[...], 1, 0)).astype(bf16)
        for half in range(2):
            j = 2 * d + half
            copies.append(
                pltpu.make_async_copy(
                    buf.at[d, pl.ds(half * CHUNK, CHUNK), :], outs[j], sems.at[j]
                )
            )
            copies[-1].start()
    for copy in copies:
        copy.wait()


def weight_partial(place, oa, ob, ca, cb):
    rows = pl.BlockSpec((HEADS, 64, TOK), lambda i, place: (0, place[0], 0))
    whole = pl.BlockSpec((TOK, D), lambda i, place: (0, 0))
    outs = pl.pallas_call(
        weight_body,
        out_shape=(jax.ShapeDtypeStruct((CHUNK, D), bf16),) * (2 * DOCS),
        grid_spec=pltpu.PrefetchScalarGridSpec(
            num_scalar_prefetch=1,
            grid=(1,),
            in_specs=[rows, rows, whole, whole],
            out_specs=[pl.BlockSpec(memory_space=pl.ANY)] * (2 * DOCS),
            scratch_shapes=[
                pltpu.VMEM((DOCS, 2 * CHUNK, D), bf16),
                pltpu.SemaphoreType.DMA((2 * DOCS,)),
            ],
        ),
        compiler_params=pltpu.CompilerParams(vmem_limit_bytes=VMEM_LIMIT),
        cost_estimate=cost(2 * TOK * D * D, 0, 8 * MIB),
        name="weight_partial",
    )(place, oa, ob, ca, cb)
    return outs[0::2], outs[1::2]


def plus(a, b):
    return (a.astype(f32) + b.astype(f32)).astype(bf16)


def sum_over_docs(up, down):
    route_up = [(i, (i + 1) % DOCS) for i in range(DOCS)]
    route_down = [(i, (i - 1) % DOCS) for i in range(DOCS)]
    a, b = up[3], down[1]
    for step in range(1, DOCS):
        a = plus(lax.ppermute(a, "dp", route_up), up[3 - step])
        b = plus(lax.ppermute(b, "dp", route_down), down[(1 + step) % DOCS])
    return a, b


def block_table(rider, core):
    offsets = rider.reshape(CHIPS, 2, SLOTS).astype(jnp.int32)
    c = jnp.arange(CHIPS, dtype=jnp.int32)[:, None, None]
    i = jnp.arange(2, dtype=jnp.int32)[None, :, None]
    target = 4 * c + 2 * core + i - offsets
    side = ((target >> 1) & 1) ^ core
    place = ((side * CHIPS + (target >> 2)) << 1) + (target & 1)
    return jnp.where(target >= 0, place, -1).reshape(2 * CHIPS, SLOTS)


def local(queries, key_states, value_states, out_weight, cotangent, block_offsets):
    core = lax.axis_index("seq") % 2
    cot = cotangent[0]
    cot_other = lax.ppermute(cot, "seq", CORE_SWAP)
    x = exchange(pack(block_offsets[0], key_states[0], value_states[0], queries[0]))
    x, g, cot_other = after(x, grad_attn_by_head(cot, out_weight), cot_other)
    y = lax.ppermute(x, "seq", CORE_SWAP)
    g = exchange(g)
    table = block_table(x[:, RIDER, 0 : 2 * SLOTS], core)
    out, lse = attention_forward(table, x, y)
    g, out = after(g, out)
    out_home = exchange(out)
    own, other = attention_backward(table, x, y, g, lse)
    out_home, own, other = after(out_home, own, other)
    out_other = lax.ppermute(out_home, "seq", CORE_SWAP)
    out_other, other = after(out_other, other)
    got = lax.ppermute(other, "seq", CORE_SWAP)
    place = jnp.stack([core, lax.axis_index("dp")])
    partial = weight_partial(place, out_home, out_other, cot, cot_other)
    up, down = partial
    *up, got = after(*up, got)
    sums = sum_over_docs(up, down)
    home = exchange(combine(own, got))
    home, *sums = after(home, *sums)
    by_doc = jnp.concatenate([part.reshape(CHIPS // 2, 16, D) for part in sums], axis=0)
    pieces = exchange(by_doc)
    weight_grad = jnp.sum(pieces.astype(f32), axis=0)
    gk, gv, gq = unpack(home, 3)
    return gq[None], gk[None], gv[None], weight_grad


def solution(mesh):
    in_specs = (
        P("dp", "seq", None),
        P("dp", "seq", None),
        P("dp", "seq", None),
        P(),
        P("dp", "seq", None),
        P("dp", "seq", None),
    )
    out_specs = (
        P("dp", "seq", None),
        P("dp", "seq", None),
        P("dp", "seq", None),
        P(("dp", "seq"), None),
    )
    return jax.shard_map(local, mesh=mesh, in_specs=in_specs, out_specs=out_specs, check_vma=False)
```

```python
import math

import jax
import jax.numpy as jnp
from jax import lax
from jax.experimental import pallas as pl
from jax.experimental.pallas import tpu as pltpu
from jax.sharding import PartitionSpec as P

HEADS = 16
HEAD = 128
BLK = 128
SLOTS = 4
D = HEADS * HEAD
TOK = 256
CHIPS = 16
BLOCKS = 64
DOCS = 4
CHUNK = D // 4 // DOCS
RIDER = 4 * TOK
ROWS = 4 * TOK + 8
SCALE = HEAD ** (-0.5)
SCALE2 = SCALE * math.log2(math.e)
NEG = -1e30
bf16 = jnp.bfloat16
f32 = jnp.float32

SAME_CORE = [[2 * c + k for c in range(CHIPS)] for k in range(2)]
CORE_SWAP = [(i, i ^ 1) for i in range(2 * CHIPS)]

UNROLL = 4
GROUP = 4
JOIN = 2
PACK = 4
VMEM_LIMIT = 56 * 1024 * 1024


def dot(a, b, ca, cb):
    return lax.dot_general(a, b, (((ca,), (cb,)), ((), ())), preferred_element_type=f32)


def cost(flops, transcendentals=0, bytes_accessed=0):
    return pl.CostEstimate(
        flops=flops, transcendentals=transcendentals, bytes_accessed=bytes_accessed
    )


PAIRS = BLOCKS // 2 * BLK * (1 + SLOTS) * BLK
PAIR_FLOPS = 2 * HEAD * PAIRS
MIB = 1024 * 1024


def exchange(x):
    return lax.all_to_all(x, "seq", 0, 0, axis_index_groups=SAME_CORE, tiled=True)


def after(*values):
    return lax.optimization_barrier(values)


def pack_body(offs, k_ref, v_ref, q_ref, c_ref, w_ref, x_ref):
    lane = lax.broadcasted_iota(jnp.int32, (8, 128), 1)
    val = jnp.zeros((8, 128), jnp.int32)
    for j in range(2 * SLOTS):
        val = jnp.where(lane == j, offs[j // SLOTS, j % SLOTS], val)
    rider = val.astype(f32).astype(bf16)
    g = dot(c_ref[...], w_ref[...], 1, 1).astype(bf16)
    for h in range(JOIN):
        columns = slice(h * HEAD, (h + 1) * HEAD)
        for t, ref in enumerate((k_ref, v_ref, q_ref)):
            x_ref[h, t * TOK : (t + 1) * TOK, :] = ref[:, columns]
        x_ref[h, 3 * TOK : 4 * TOK, :] = g[:, columns]
        x_ref[h, RIDER : RIDER + 8, :] = rider


def pack(offs, k, v, q, cot, weight):
    rows = pl.BlockSpec((TOK, JOIN * HEAD), lambda i: (0, i))
    return pl.pallas_call(
        pack_body,
        out_shape=jax.ShapeDtypeStruct((HEADS, ROWS, HEAD), bf16),
        grid=(HEADS // JOIN,),
        in_specs=[
            pl.BlockSpec(memory_space=pltpu.SMEM),
            rows,
            rows,
            rows,
            pl.BlockSpec((TOK, D), lambda i: (0, 0)),
            pl.BlockSpec((JOIN * HEAD, D), lambda i: (i, 0)),
        ],
        out_specs=pl.BlockSpec((JOIN, ROWS, HEAD), lambda i: (i, 0, 0)),
        compiler_params=pltpu.CompilerParams(vmem_limit_bytes=VMEM_LIMIT),
        cost_estimate=cost(2 * TOK * D * D, 0, 16 * MIB),
        name="pack",
    )(offs, k, v, q, cot, weight)


def unpack_body(r_ref, *refs):
    for h in range(PACK):
        for t, ref in enumerate(refs):
            ref[:, h * HEAD : (h + 1) * HEAD] = r_ref[h, t * TOK : (t + 1) * TOK, :]


def unpack(r, n):
    out = jax.ShapeDtypeStruct((TOK, D), bf16)
    rows = pl.BlockSpec((TOK, PACK * HEAD), lambda i: (0, i))
    return pl.pallas_call(
        unpack_body,
        out_shape=(out,) * n,
        grid=(HEADS // PACK,),
        in_specs=[pl.BlockSpec((PACK, n * TOK, HEAD), lambda i: (i, 0, 0))],
        out_specs=[rows] * n,
        compiler_params=pltpu.CompilerParams(vmem_limit_bytes=VMEM_LIMIT),
        cost_estimate=cost(0, 0, 2 * n * MIB),
        name="unpack",
    )(r)


def load_pool(x_ref, y_ref, kv, qs, sems):
    groups = []
    for j in range(CHIPS // GROUP):
        at = pl.ds(j * GROUP, GROUP)
        groups.append(
            [
                pltpu.make_async_copy(
                    x_ref.at[at, pl.ds(0, 2 * TOK), :], kv.at[at], sems.at[3 * j]
                ),
                pltpu.make_async_copy(
                    y_ref.at[at],
                    kv.at[pl.ds(CHIPS + j * GROUP, GROUP)],
                    sems.at[3 * j + 1],
                ),
                pltpu.make_async_copy(
                    x_ref.at[at, pl.ds(2 * TOK, TOK), :], qs.at[at], sems.at[3 * j + 2]
                ),
            ]
        )
    return groups


def listed(table, c, i):
    places = [(c, i * BLK, None)]
    for s in range(SLOTS):
        code = table[2 * c + i, s]
        f = jnp.maximum(code, 0)
        bias = jnp.where(code >= 0, 0.0, -NEG).astype(f32)
        places.append((f // 2, pl.multiple_of((f % 2) * BLK, BLK), bias))
    return places


def causal():
    u = lax.broadcasted_iota(jnp.int32, (BLK, BLK), 0)
    t = lax.broadcasted_iota(jnp.int32, (BLK, BLK), 1)
    return u <= t


def forward_body(table, x_ref, y_ref, o_ref, lse_ref, kv, qs, sems):
    groups = load_pool(x_ref, y_ref, kv, qs, sems)
    for copies in groups:
        for copy in copies:
            copy.start()

    def block(c, i):
        places = listed(table, c, i)
        q = qs[c, pl.ds(i * BLK, BLK), :]
        keys = jnp.concatenate([kv[p, pl.ds(r, BLK), :] for p, r, _ in places], axis=0)
        every = dot(keys, q, 1, 1)
        raw = [every[s * BLK : (s + 1) * BLK, :] for s in range(1 + SLOTS)]
        raw[0] = jnp.where(causal(), raw[0], NEG)
        peak = jnp.max(raw[0], axis=0, keepdims=True)
        for (_, _, bias), s in zip(places[1:], raw[1:]):
            peak = jnp.maximum(peak, jnp.max(s, axis=0, keepdims=True) - bias)
        peak = peak * SCALE2
        weights = []
        total = None
        for (_, _, bias), s in zip(places, raw):
            w = jnp.exp2(s * SCALE2 - (peak if bias is None else peak + bias))
            part = jnp.sum(w, axis=0, keepdims=True)
            total = part if total is None else total + part
            weights.append(w.astype(bf16))
        values = jnp.concatenate([kv[p, pl.ds(TOK + r, BLK), :] for p, r, _ in places], axis=0)
        out = dot(values, jnp.concatenate(weights, axis=0), 0, 0) * (1.0 / total)
        return out.astype(bf16), peak + jnp.log2(total)

    def step(c, carry):
        lses = []
        for i in range(2):
            out, lse = block(c, i)
            for g in range(8):
                row = (g // 2) * 16
                o_ref[2 * c + g % 2, row : row + 16, i * BLK : (i + 1) * BLK] = out[
                    g * 16 : g * 16 + 16, :
                ]
            lses.append(lse)
        row = lax.broadcasted_iota(jnp.int32, (8, 128), 0)
        lse_ref[c] = jnp.where(row == 0, lses[0], lses[1])
        return carry

    for j, copies in enumerate(groups):
        for copy in copies:
            copy.wait()
        lax.fori_loop(j * GROUP, (j + 1) * GROUP, step, 0, unroll=UNROLL)


def attention_forward(table, x, y):
    return pl.pallas_call(
        forward_body,
        out_shape=(
            jax.ShapeDtypeStruct((2 * CHIPS, HEAD // 2, TOK), bf16),
            jax.ShapeDtypeStruct((CHIPS, 8, 128), f32),
        ),
        in_specs=[pl.BlockSpec(memory_space=pltpu.SMEM)] + [pl.BlockSpec(memory_space=pl.ANY)] * 2,
        out_specs=[pl.BlockSpec(memory_space=pltpu.VMEM)] * 2,
        scratch_shapes=[
            pltpu.VMEM((2 * CHIPS, 2 * TOK, HEAD), bf16),
            pltpu.VMEM((CHIPS, TOK, HEAD), bf16),
            pltpu.SemaphoreType.DMA((3 * (CHIPS // GROUP),)),
        ],
        compiler_params=pltpu.CompilerParams(vmem_limit_bytes=VMEM_LIMIT),
        cost_estimate=cost(2 * PAIR_FLOPS, PAIRS, 7 * MIB),
        name="attn_fwd",
    )(table, x, y)


def backward_body(
    table, x_ref, y_ref, lse_ref, home_ref, other_ref, kv, qs, gs, acck, accv, own, other, gq, sems
):
    groups = load_pool(x_ref, y_ref, kv, qs, sems)
    sends = []
    n = CHIPS // GROUP
    for j in range(n):
        at = pl.ds(j * GROUP, GROUP)
        groups[j].append(
            pltpu.make_async_copy(
                x_ref.at[at, pl.ds(3 * TOK, TOK), :], gs.at[at], sems.at[3 * n + j]
            )
        )
        sends.append(
            [
                pltpu.make_async_copy(
                    gq.at[at], home_ref.at[at, pl.ds(2 * TOK, TOK), :], sems.at[4 * n + j]
                ),
                pltpu.make_async_copy(
                    own.at[at], home_ref.at[at, pl.ds(0, 2 * TOK), :], sems.at[5 * n + j]
                ),
                pltpu.make_async_copy(other.at[at], other_ref.at[at], sems.at[6 * n + j]),
            ]
        )
    for copies in groups:
        for copy in copies:
            copy.start()

    def clear(j, carry):
        acck[CHIPS + j] = jnp.zeros((TOK, HEAD), f32)
        accv[CHIPS + j] = jnp.zeros((TOK, HEAD), f32)
        return carry

    lax.fori_loop(0, CHIPS, clear, 0)

    def block(c, i):
        places = listed(table, c, i)
        q = qs[c, pl.ds(i * BLK, BLK), :]
        g = gs[c, pl.ds(i * BLK, BLK), :]
        lse = lse_ref[c, i : i + 1, :]
        keys = jnp.concatenate([kv[p, pl.ds(r, BLK), :] for p, r, _ in places], axis=0)
        values = jnp.concatenate([kv[p, pl.ds(TOK + r, BLK), :] for p, r, _ in places], axis=0)
        every = dot(keys, q, 1, 1)
        grads = dot(values, g, 1, 1)
        probs = []
        for j, (_, _, bias) in enumerate(places):
            s = every[j * BLK : (j + 1) * BLK, :]
            prob = jnp.exp2(s * SCALE2 - (lse if bias is None else lse + bias))
            if bias is None:
                prob = jnp.where(causal(), prob, 0.0)
            probs.append(prob)
        prob = jnp.concatenate(probs, axis=0)
        row_dot = jnp.sum(prob * grads, axis=0, keepdims=True)
        score = (prob * (grads - row_dot)).astype(bf16)
        gk = dot(score, q, 1, 0)
        gv = dot(prob.astype(bf16), g, 1, 0)
        for j, (p, r, _) in enumerate(places):
            at = pl.ds(r, BLK)
            if j == 0:
                acck[p, at, :] = gk[0:BLK, :]
                accv[p, at, :] = gv[0:BLK, :]
            else:
                acck[p, at, :] += gk[j * BLK : (j + 1) * BLK, :]
                accv[p, at, :] += gv[j * BLK : (j + 1) * BLK, :]
        gq[c, pl.ds(i * BLK, BLK), :] = (dot(score, keys, 0, 0) * SCALE).astype(bf16)

    def step(c, carry):
        for i in range(2):
            block(c, i)
        return carry

    def flush(j, carry):
        own[j, 0:TOK, :] = (acck[j] * SCALE).astype(bf16)
        own[j, TOK : 2 * TOK, :] = accv[j].astype(bf16)
        other[j, 0:TOK, :] = (acck[CHIPS + j] * SCALE).astype(bf16)
        other[j, TOK : 2 * TOK, :] = accv[CHIPS + j].astype(bf16)
        return carry

    for j in range(n + 2):
        if j < n:
            for copy in groups[j]:
                copy.wait()
            lax.fori_loop(j * GROUP, (j + 1) * GROUP, step, 0, unroll=UNROLL)
            sends[j][0].start()
        if j >= 2:
            lax.fori_loop((j - 2) * GROUP, (j - 1) * GROUP, flush, 0)
            sends[j - 2][1].start()
            sends[j - 2][2].start()
    for copies in sends:
        for copy in copies:
            copy.wait()


def attention_backward(table, x, y, lse):
    return pl.pallas_call(
        backward_body,
        out_shape=(
            jax.ShapeDtypeStruct((CHIPS, 3 * TOK, HEAD), bf16),
            jax.ShapeDtypeStruct((CHIPS, 2 * TOK, HEAD), bf16),
        ),
        in_specs=[pl.BlockSpec(memory_space=pltpu.SMEM)]
        + [pl.BlockSpec(memory_space=pl.ANY)] * 2
        + [pl.BlockSpec(memory_space=pltpu.VMEM)],
        out_specs=[pl.BlockSpec(memory_space=pl.ANY)] * 2,
        scratch_shapes=[
            pltpu.VMEM((2 * CHIPS, 2 * TOK, HEAD), bf16),
            pltpu.VMEM((CHIPS, TOK, HEAD), bf16),
            pltpu.VMEM((CHIPS, TOK, HEAD), bf16),
            pltpu.VMEM((2 * CHIPS, TOK, HEAD), f32),
            pltpu.VMEM((2 * CHIPS, TOK, HEAD), f32),
            pltpu.VMEM((CHIPS, 2 * TOK, HEAD), bf16),
            pltpu.VMEM((CHIPS, 2 * TOK, HEAD), bf16),
            pltpu.VMEM((CHIPS, TOK, HEAD), bf16),
            pltpu.SemaphoreType.DMA((7 * (CHIPS // GROUP),)),
        ],
        compiler_params=pltpu.CompilerParams(vmem_limit_bytes=VMEM_LIMIT),
        cost_estimate=cost(5 * PAIR_FLOPS, PAIRS, 14 * MIB),
        name="attn_bwd",
    )(table, x, y, lse)


def combine_body(own_ref, got_ref, o_ref):
    o_ref[...] = (own_ref[...].astype(f32) + got_ref[...].astype(f32)).astype(bf16)


def combine(home, got):
    n = 4
    rows = pl.BlockSpec((n, 2 * TOK, HEAD), lambda i: (i, 0, 0))
    return pl.pallas_call(
        combine_body,
        out_shape=jax.ShapeDtypeStruct((CHIPS, 3 * TOK, HEAD), bf16),
        grid=(CHIPS // n,),
        in_specs=[rows, rows],
        out_specs=rows,
        input_output_aliases={0: 0},
        compiler_params=pltpu.CompilerParams(vmem_limit_bytes=VMEM_LIMIT),
        cost_estimate=cost(CHIPS * 2 * TOK * HEAD, 0, 6 * MIB),
        name="combine",
    )(home, got)


def weight_body(place, oa_ref, ob_ref, ca_ref, cb_ref, *rest):
    outs, buf, sems = rest[: 2 * DOCS], rest[2 * DOCS], rest[2 * DOCS + 1]
    copies = []
    for d in (3, 1, 2, 0):
        heads = pl.ds(((place[1] + d) % DOCS) * (HEADS // DOCS), HEADS // DOCS)
        a = oa_ref[heads].reshape(2 * CHUNK, TOK)
        b = ob_ref[heads].reshape(2 * CHUNK, TOK)
        buf[d] = (dot(a, ca_ref[...], 1, 0) + dot(b, cb_ref[...], 1, 0)).astype(bf16)
        for half in range(2):
            j = 2 * d + half
            copies.append(
                pltpu.make_async_copy(
                    buf.at[d, pl.ds(half * CHUNK, CHUNK), :], outs[j], sems.at[j]
                )
            )
            copies[-1].start()
    for copy in copies:
        copy.wait()


def weight_partial(place, out, ca, cb):
    own = pl.BlockSpec((HEADS, 1, HEAD // 2, TOK), lambda i, place: (0, place[0], 0, 0))
    other = pl.BlockSpec((HEADS, 1, HEAD // 2, TOK), lambda i, place: (0, 1 - place[0], 0, 0))
    whole = pl.BlockSpec((TOK, D), lambda i, place: (0, 0))
    outs = pl.pallas_call(
        weight_body,
        out_shape=(jax.ShapeDtypeStruct((CHUNK, D), bf16),) * (2 * DOCS),
        grid_spec=pltpu.PrefetchScalarGridSpec(
            num_scalar_prefetch=1,
            grid=(1,),
            in_specs=[own, other, whole, whole],
            out_specs=[pl.BlockSpec(memory_space=pl.ANY)] * (2 * DOCS),
            scratch_shapes=[
                pltpu.VMEM((DOCS, 2 * CHUNK, D), bf16),
                pltpu.SemaphoreType.DMA((2 * DOCS,)),
            ],
        ),
        compiler_params=pltpu.CompilerParams(vmem_limit_bytes=VMEM_LIMIT),
        cost_estimate=cost(2 * TOK * D * D, 0, 8 * MIB),
        name="weight_partial",
    )(place, out, out, ca, cb)
    return outs[0::2], outs[1::2]


def plus(a, b):
    return (a.astype(f32) + b.astype(f32)).astype(bf16)


def join_body(a_ref, b_ref, o_ref):
    n = CHIPS // 2
    o_ref[0:n] = a_ref[...].reshape(n, 16, D)
    o_ref[n : 2 * n] = b_ref[...].reshape(n, 16, D)


def join(a, b):
    return pl.pallas_call(
        join_body,
        out_shape=jax.ShapeDtypeStruct((CHIPS, 16, D), bf16),
        in_specs=[pl.BlockSpec(memory_space=pltpu.VMEM)] * 2,
        out_specs=pl.BlockSpec(memory_space=pltpu.VMEM),
        compiler_params=pltpu.CompilerParams(vmem_limit_bytes=VMEM_LIMIT),
        cost_estimate=cost(0, 0, 2 * MIB),
        name="join",
    )(a, b)


def sum_over_docs(up, down):
    route_up = [(i, (i + 1) % DOCS) for i in range(DOCS)]
    route_down = [(i, (i - 1) % DOCS) for i in range(DOCS)]
    a, b = up[3], down[1]
    for step in range(1, DOCS):
        a = plus(lax.ppermute(a, "dp", route_up), up[3 - step])
        b = plus(lax.ppermute(b, "dp", route_down), down[(1 + step) % DOCS])
    return a, b


def block_table(rider, core):
    offsets = rider.reshape(CHIPS, 2, SLOTS).astype(jnp.int32)
    c = jnp.arange(CHIPS, dtype=jnp.int32)[:, None, None]
    i = jnp.arange(2, dtype=jnp.int32)[None, :, None]
    target = 4 * c + 2 * core + i - offsets
    side = ((target >> 1) & 1) ^ core
    place = ((side * CHIPS + (target >> 2)) << 1) + (target & 1)
    return jnp.where(target >= 0, place, -1).reshape(2 * CHIPS, SLOTS)


def local(queries, key_states, value_states, out_weight, cotangent, block_offsets):
    core = lax.axis_index("seq") % 2
    cot = cotangent[0]
    packed = pack(
        block_offsets[0], key_states[0], value_states[0], queries[0], cot, out_weight
    )
    cot_other = lax.ppermute(cot, "seq", CORE_SWAP)
    packed, cot_other = after(packed, cot_other)
    x = exchange(packed)
    y = lax.ppermute(x[:, 0 : 2 * TOK], "seq", CORE_SWAP)
    table = block_table(x[:, RIDER, 0 : 2 * SLOTS], core)
    place = jnp.stack([core, lax.axis_index("dp")])
    table, place = after(table, place)
    out, lse = attention_forward(table, x, y)
    out_home = lax.all_to_all(out, "seq", 0, 0, tiled=True)
    own, other = attention_backward(table, x, y, lse)
    out_home, own, other = after(out_home, own, other)
    got = lax.ppermute(other, "seq", CORE_SWAP)
    by_core = out_home.reshape(HEADS, 2, HEAD // 2, TOK)
    up, down = weight_partial(place, by_core, cot, cot_other)
    *up, got = after(*up, got)
    sums = sum_over_docs(up, down)
    home = exchange(combine(own, got))
    home, *sums = after(home, *sums)
    pieces = exchange(join(*sums))
    weight_grad = jnp.sum(pieces.astype(f32), axis=0)
    gk, gv, gq = unpack(home, 3)
    return gq[None], gk[None], gv[None], weight_grad


def solution(mesh):
    in_specs = (
        P("dp", "seq", None),
        P("dp", "seq", None),
        P("dp", "seq", None),
        P(),
        P("dp", "seq", None),
        P("dp", "seq", None),
    )
    out_specs = (
        P("dp", "seq", None),
        P("dp", "seq", None),
        P("dp", "seq", None),
        P(("dp", "seq"), None),
    )
    return jax.shard_map(local, mesh=mesh, in_specs=in_specs, out_specs=out_specs, check_vma=False)
```

```python
import math

import jax
import jax.numpy as jnp
from jax import lax
from jax.experimental import pallas as pl
from jax.experimental.pallas import tpu as pltpu
from jax.sharding import PartitionSpec as P

HEADS = 16
HEAD = 128
BLK = 128
SLOTS = 4
D = HEADS * HEAD
TOK = 256
CHIPS = 16
BLOCKS = 64
DOCS = 4
CHUNK = D // 4 // DOCS
RIDER = 3 * TOK
ROWS = 3 * TOK + 8
SCALE = HEAD ** (-0.5)
SCALE2 = SCALE * math.log2(math.e)
NEG = -1e30
bf16 = jnp.bfloat16
f32 = jnp.float32

SAME_CORE = [[2 * c + k for c in range(CHIPS)] for k in range(2)]
CORE_SWAP = [(i, i ^ 1) for i in range(2 * CHIPS)]

UNROLL = 4
GROUP = 4
PACK = 4
VMEM_LIMIT = 56 * 1024 * 1024


def dot(a, b, ca, cb):
    return lax.dot_general(a, b, (((ca,), (cb,)), ((), ())), preferred_element_type=f32)


def cost(flops, transcendentals=0, bytes_accessed=0):
    return pl.CostEstimate(
        flops=flops, transcendentals=transcendentals, bytes_accessed=bytes_accessed
    )


PAIRS = BLOCKS // 2 * BLK * (1 + SLOTS) * BLK
PAIR_FLOPS = 2 * HEAD * PAIRS
MIB = 1024 * 1024


def exchange(x):
    return lax.all_to_all(x, "seq", 0, 0, axis_index_groups=SAME_CORE, tiled=True)


def after(*values):
    return lax.optimization_barrier(values)


def pack_body(offs, k_ref, v_ref, q_ref, x_ref):
    lane = lax.broadcasted_iota(jnp.int32, (8, 128), 1)
    val = jnp.zeros((8, 128), jnp.int32)
    for j in range(2 * SLOTS):
        val = jnp.where(lane == j, offs[j // SLOTS, j % SLOTS], val)
    rider = val.astype(f32).astype(bf16)
    for h in range(PACK):
        for t, ref in enumerate((k_ref, v_ref, q_ref)):
            x_ref[h, t * TOK : (t + 1) * TOK, :] = ref[:, h * HEAD : (h + 1) * HEAD]
        x_ref[h, RIDER : RIDER + 8, :] = rider


def pack(offs, k, v, q):
    rows = pl.BlockSpec((TOK, PACK * HEAD), lambda i: (0, i))
    return pl.pallas_call(
        pack_body,
        out_shape=jax.ShapeDtypeStruct((HEADS, ROWS, HEAD), bf16),
        grid=(HEADS // PACK,),
        in_specs=[pl.BlockSpec(memory_space=pltpu.SMEM), rows, rows, rows],
        out_specs=pl.BlockSpec((PACK, ROWS, HEAD), lambda i: (i, 0, 0)),
        compiler_params=pltpu.CompilerParams(vmem_limit_bytes=VMEM_LIMIT),
        name="pack",
    )(offs, k, v, q)


def unpack_body(r_ref, *refs):
    for h in range(PACK):
        for t, ref in enumerate(refs):
            ref[:, h * HEAD : (h + 1) * HEAD] = r_ref[h, t * TOK : (t + 1) * TOK, :]


def unpack(r, n):
    out = jax.ShapeDtypeStruct((TOK, D), bf16)
    rows = pl.BlockSpec((TOK, PACK * HEAD), lambda i: (0, i))
    return pl.pallas_call(
        unpack_body,
        out_shape=(out,) * n,
        grid=(HEADS // PACK,),
        in_specs=[pl.BlockSpec((PACK, n * TOK, HEAD), lambda i: (i, 0, 0))],
        out_specs=[rows] * n,
        compiler_params=pltpu.CompilerParams(vmem_limit_bytes=VMEM_LIMIT),
        cost_estimate=cost(0, 0, 2 * n * MIB),
        name="unpack",
    )(r)


def grad_attn_body(c_ref, w_ref, o_ref):
    g = dot(c_ref[...], w_ref[...], 1, 1).astype(bf16)
    for j in range(2):
        o_ref[j] = g[:, j * HEAD : (j + 1) * HEAD]


def grad_attn_by_head(cot, weight):
    return pl.pallas_call(
        grad_attn_body,
        out_shape=jax.ShapeDtypeStruct((HEADS, TOK, HEAD), bf16),
        grid=(HEADS // 2,),
        in_specs=[
            pl.BlockSpec((TOK, D), lambda i: (0, 0)),
            pl.BlockSpec((2 * HEAD, D), lambda i: (i, 0)),
        ],
        out_specs=pl.BlockSpec((2, TOK, HEAD), lambda i: (i, 0, 0)),
        compiler_params=pltpu.CompilerParams(vmem_limit_bytes=VMEM_LIMIT),
        cost_estimate=cost(2 * TOK * D * D, 0, 10 * MIB),
        name="grad_attn",
    )(cot, weight)


def load_pool(x_ref, y_ref, kv, qs, sems):
    groups = []
    for j in range(CHIPS // GROUP):
        at = pl.ds(j * GROUP, GROUP)
        groups.append(
            [
                pltpu.make_async_copy(
                    x_ref.at[at, pl.ds(0, 2 * TOK), :], kv.at[at], sems.at[3 * j]
                ),
                pltpu.make_async_copy(
                    y_ref.at[at, pl.ds(0, 2 * TOK), :],
                    kv.at[pl.ds(CHIPS + j * GROUP, GROUP)],
                    sems.at[3 * j + 1],
                ),
                pltpu.make_async_copy(
                    x_ref.at[at, pl.ds(2 * TOK, TOK), :], qs.at[at], sems.at[3 * j + 2]
                ),
            ]
        )
    return groups


def listed(table, c, i):
    places = [(c, i * BLK, None)]
    for s in range(SLOTS):
        code = table[2 * c + i, s]
        f = jnp.maximum(code, 0)
        bias = jnp.where(code >= 0, 0.0, -NEG).astype(f32)
        places.append((f // 2, pl.multiple_of((f % 2) * BLK, BLK), bias))
    return places


def causal():
    u = lax.broadcasted_iota(jnp.int32, (BLK, BLK), 0)
    t = lax.broadcasted_iota(jnp.int32, (BLK, BLK), 1)
    return u <= t


def forward_body(table, x_ref, y_ref, o_ref, lse_ref, kv, qs, sems):
    groups = load_pool(x_ref, y_ref, kv, qs, sems)
    for copies in groups:
        for copy in copies:
            copy.start()

    def block(c, i):
        places = listed(table, c, i)
        q = qs[c, pl.ds(i * BLK, BLK), :]
        keys = jnp.concatenate([kv[p, pl.ds(r, BLK), :] for p, r, _ in places], axis=0)
        every = dot(keys, q, 1, 1)
        raw = [every[s * BLK : (s + 1) * BLK, :] for s in range(1 + SLOTS)]
        raw[0] = jnp.where(causal(), raw[0], NEG)
        peak = jnp.max(raw[0], axis=0, keepdims=True)
        for (_, _, bias), s in zip(places[1:], raw[1:]):
            peak = jnp.maximum(peak, jnp.max(s, axis=0, keepdims=True) - bias)
        peak = peak * SCALE2
        weights = []
        total = None
        for (_, _, bias), s in zip(places, raw):
            w = jnp.exp2(s * SCALE2 - (peak if bias is None else peak + bias))
            part = jnp.sum(w, axis=0, keepdims=True)
            total = part if total is None else total + part
            weights.append(w.astype(bf16))
        values = jnp.concatenate([kv[p, pl.ds(TOK + r, BLK), :] for p, r, _ in places], axis=0)
        out = dot(values, jnp.concatenate(weights, axis=0), 0, 0) * (1.0 / total)
        return out.astype(bf16), peak + jnp.log2(total)

    def step(c, carry):
        lses = []
        for i in range(2):
            out, lse = block(c, i)
            for g in range(8):
                row = (g // 2) * 16
                o_ref[2 * c + g % 2, row : row + 16, i * BLK : (i + 1) * BLK] = out[
                    g * 16 : g * 16 + 16, :
                ]
            lses.append(lse)
        row = lax.broadcasted_iota(jnp.int32, (8, 128), 0)
        lse_ref[c] = jnp.where(row == 0, lses[0], lses[1])
        return carry

    for j, copies in enumerate(groups):
        for copy in copies:
            copy.wait()
        lax.fori_loop(j * GROUP, (j + 1) * GROUP, step, 0, unroll=UNROLL)


def attention_forward(table, x, y):
    return pl.pallas_call(
        forward_body,
        out_shape=(
            jax.ShapeDtypeStruct((2 * CHIPS, HEAD // 2, TOK), bf16),
            jax.ShapeDtypeStruct((CHIPS, 8, 128), f32),
        ),
        in_specs=[pl.BlockSpec(memory_space=pltpu.SMEM)] + [pl.BlockSpec(memory_space=pl.ANY)] * 2,
        out_specs=[pl.BlockSpec(memory_space=pltpu.VMEM)] * 2,
        scratch_shapes=[
            pltpu.VMEM((2 * CHIPS, 2 * TOK, HEAD), bf16),
            pltpu.VMEM((CHIPS, TOK, HEAD), bf16),
            pltpu.SemaphoreType.DMA((3 * (CHIPS // GROUP),)),
        ],
        compiler_params=pltpu.CompilerParams(vmem_limit_bytes=VMEM_LIMIT),
        cost_estimate=cost(2 * PAIR_FLOPS, PAIRS, 7 * MIB),
        name="attn_fwd",
    )(table, x, y)


def backward_body(
    table, x_ref, y_ref, g_ref, lse_ref, own_ref, other_ref, gq_ref, kv, qs, gs, acck, accv, own, other, gq, sems
):
    groups = load_pool(x_ref, y_ref, kv, qs, sems)
    sends = []
    n = CHIPS // GROUP
    for j in range(n):
        at = pl.ds(j * GROUP, GROUP)
        groups[j].append(pltpu.make_async_copy(g_ref.at[at], gs.at[at], sems.at[3 * n + j]))
        sends.append(
            [
                pltpu.make_async_copy(
                    gq.at[at], gq_ref.at[at], sems.at[4 * n + j]
                ),
                pltpu.make_async_copy(
                    own.at[at], own_ref.at[at], sems.at[5 * n + j]
                ),
                pltpu.make_async_copy(other.at[at], other_ref.at[at], sems.at[6 * n + j]),
            ]
        )
    for copies in groups:
        for copy in copies:
            copy.start()

    def clear(j, carry):
        acck[CHIPS + j] = jnp.zeros((TOK, HEAD), f32)
        accv[CHIPS + j] = jnp.zeros((TOK, HEAD), f32)
        return carry

    lax.fori_loop(0, CHIPS, clear, 0)

    def block(c, i):
        places = listed(table, c, i)
        q = qs[c, pl.ds(i * BLK, BLK), :]
        g = gs[c, pl.ds(i * BLK, BLK), :]
        lse = lse_ref[c, i : i + 1, :]
        keys = jnp.concatenate([kv[p, pl.ds(r, BLK), :] for p, r, _ in places], axis=0)
        values = jnp.concatenate([kv[p, pl.ds(TOK + r, BLK), :] for p, r, _ in places], axis=0)
        every = dot(keys, q, 1, 1)
        grads = dot(values, g, 1, 1)
        probs = []
        for j, (_, _, bias) in enumerate(places):
            s = every[j * BLK : (j + 1) * BLK, :]
            prob = jnp.exp2(s * SCALE2 - (lse if bias is None else lse + bias))
            if bias is None:
                prob = jnp.where(causal(), prob, 0.0)
            probs.append(prob)
        prob = jnp.concatenate(probs, axis=0)
        row_dot = jnp.sum(prob * grads, axis=0, keepdims=True)
        score = (prob * (grads - row_dot)).astype(bf16)
        gk = dot(score, q, 1, 0)
        gv = dot(prob.astype(bf16), g, 1, 0)
        for j, (p, r, _) in enumerate(places):
            at = pl.ds(r, BLK)
            if j == 0:
                acck[p, at, :] = gk[0:BLK, :]
                accv[p, at, :] = gv[0:BLK, :]
            else:
                acck[p, at, :] += gk[j * BLK : (j + 1) * BLK, :]
                accv[p, at, :] += gv[j * BLK : (j + 1) * BLK, :]
        gq[c, pl.ds(i * BLK, BLK), :] = (dot(score, keys, 0, 0) * SCALE).astype(bf16)

    def step(c, carry):
        for i in range(2):
            block(c, i)
        return carry

    def flush(j, carry):
        own[j, 0:TOK, :] = (acck[j] * SCALE).astype(bf16)
        own[j, TOK : 2 * TOK, :] = accv[j].astype(bf16)
        other[j, 0:TOK, :] = (acck[CHIPS + j] * SCALE).astype(bf16)
        other[j, TOK : 2 * TOK, :] = accv[CHIPS + j].astype(bf16)
        return carry

    for j in range(n + 2):
        if j < n:
            for copy in groups[j]:
                copy.wait()
            lax.fori_loop(j * GROUP, (j + 1) * GROUP, step, 0, unroll=UNROLL)
            sends[j][0].start()
        if j >= 2:
            lax.fori_loop((j - 2) * GROUP, (j - 1) * GROUP, flush, 0)
            sends[j - 2][1].start()
            sends[j - 2][2].start()
    for copies in sends:
        for copy in copies:
            copy.wait()


def attention_backward(table, x, y, g, lse):
    return pl.pallas_call(
        backward_body,
        out_shape=(
            jax.ShapeDtypeStruct((CHIPS, 2 * TOK, HEAD), bf16),
            jax.ShapeDtypeStruct((CHIPS, 2 * TOK, HEAD), bf16),
            jax.ShapeDtypeStruct((CHIPS, TOK, HEAD), bf16),
        ),
        in_specs=[pl.BlockSpec(memory_space=pltpu.SMEM)]
        + [pl.BlockSpec(memory_space=pl.ANY)] * 3
        + [pl.BlockSpec(memory_space=pltpu.VMEM)],
        out_specs=[pl.BlockSpec(memory_space=pl.ANY)] * 3,
        scratch_shapes=[
            pltpu.VMEM((2 * CHIPS, 2 * TOK, HEAD), bf16),
            pltpu.VMEM((CHIPS, TOK, HEAD), bf16),
            pltpu.VMEM((CHIPS, TOK, HEAD), bf16),
            pltpu.VMEM((2 * CHIPS, TOK, HEAD), f32),
            pltpu.VMEM((2 * CHIPS, TOK, HEAD), f32),
            pltpu.VMEM((CHIPS, 2 * TOK, HEAD), bf16),
            pltpu.VMEM((CHIPS, 2 * TOK, HEAD), bf16),
            pltpu.VMEM((CHIPS, TOK, HEAD), bf16),
            pltpu.SemaphoreType.DMA((7 * (CHIPS // GROUP),)),
        ],
        compiler_params=pltpu.CompilerParams(vmem_limit_bytes=VMEM_LIMIT),
        cost_estimate=cost(5 * PAIR_FLOPS, PAIRS, 14 * MIB),
        name="attn_bwd",
    )(table, x, y, g, lse)


def combine_body(own_ref, got_ref, o_ref):
    o_ref[...] = (own_ref[...].astype(f32) + got_ref[...].astype(f32)).astype(bf16)


def combine(own, got):
    n = 4
    rows = pl.BlockSpec((n, 2 * TOK, HEAD), lambda i: (i, 0, 0))
    return pl.pallas_call(
        combine_body,
        out_shape=jax.ShapeDtypeStruct((CHIPS, 2 * TOK, HEAD), bf16),
        grid=(CHIPS // n,),
        in_specs=[rows, rows],
        out_specs=rows,
        compiler_params=pltpu.CompilerParams(vmem_limit_bytes=VMEM_LIMIT),
        cost_estimate=cost(CHIPS * 2 * TOK * HEAD, 0, 6 * MIB),
        name="combine",
    )(own, got)


def weight_body(place, oa_ref, ob_ref, ca_ref, cb_ref, *rest):
    outs, buf, sems = rest[: 2 * DOCS], rest[2 * DOCS], rest[2 * DOCS + 1]
    copies = []
    for d in (3, 1, 2, 0):
        heads = pl.ds(((place[1] + d) % DOCS) * (HEADS // DOCS), HEADS // DOCS)
        a = oa_ref[heads].reshape(2 * CHUNK, TOK)
        b = ob_ref[heads].reshape(2 * CHUNK, TOK)
        buf[d] = (dot(a, ca_ref[...], 1, 0) + dot(b, cb_ref[...], 1, 0)).astype(bf16)
        for half in range(2):
            j = 2 * d + half
            copies.append(
                pltpu.make_async_copy(
                    buf.at[d, pl.ds(half * CHUNK, CHUNK), :], outs[j], sems.at[j]
                )
            )
            copies[-1].start()
    for copy in copies:
        copy.wait()


def weight_partial(place, out, ca, cb):
    own = pl.BlockSpec((HEADS, 1, HEAD // 2, TOK), lambda i, place: (0, place[0], 0, 0))
    other = pl.BlockSpec((HEADS, 1, HEAD // 2, TOK), lambda i, place: (0, 1 - place[0], 0, 0))
    whole = pl.BlockSpec((TOK, D), lambda i, place: (0, 0))
    outs = pl.pallas_call(
        weight_body,
        out_shape=(jax.ShapeDtypeStruct((CHUNK, D), bf16),) * (2 * DOCS),
        grid_spec=pltpu.PrefetchScalarGridSpec(
            num_scalar_prefetch=1,
            grid=(1,),
            in_specs=[own, other, whole, whole],
            out_specs=[pl.BlockSpec(memory_space=pl.ANY)] * (2 * DOCS),
            scratch_shapes=[
                pltpu.VMEM((DOCS, 2 * CHUNK, D), bf16),
                pltpu.SemaphoreType.DMA((2 * DOCS,)),
            ],
        ),
        compiler_params=pltpu.CompilerParams(vmem_limit_bytes=VMEM_LIMIT),
        cost_estimate=cost(2 * TOK * D * D, 0, 8 * MIB),
        name="weight_partial",
    )(place, out, out, ca, cb)
    return outs[0::2], outs[1::2]


def plus(a, b):
    return (a.astype(f32) + b.astype(f32)).astype(bf16)


def half_sum_body(a_ref, b_ref, *rest):
    o_ref = rest[-1]
    o_ref[...] = plus(a_ref[...], b_ref[...]).reshape(CHIPS // 2, 16, D)


def half_sum(a, b, half, joined=None):
    whole = pl.BlockSpec((CHUNK, D), lambda i: (0, 0))
    args = (a, b) if joined is None else (a, b, joined)
    return pl.pallas_call(
        half_sum_body,
        out_shape=jax.ShapeDtypeStruct((CHIPS, 16, D), bf16),
        grid=(1,),
        in_specs=[whole, whole] + [pl.BlockSpec(memory_space=pl.ANY)] * (len(args) - 2),
        out_specs=pl.BlockSpec((CHIPS // 2, 16, D), lambda i: (half, 0, 0)),
        input_output_aliases={} if joined is None else {2: 0},
        compiler_params=pltpu.CompilerParams(vmem_limit_bytes=VMEM_LIMIT),
        cost_estimate=cost(CHUNK * D, 0, 3 * MIB // 2),
        name="half_sum",
    )(*args)


def sum_over_docs(up, down):
    route_up = [(i, (i + 1) % DOCS) for i in range(DOCS)]
    route_down = [(i, (i - 1) % DOCS) for i in range(DOCS)]
    a, b = up[3], down[1]
    for step in range(1, DOCS):
        a = lax.ppermute(a, "dp", route_up)
        b = lax.ppermute(b, "dp", route_down)
        if step < DOCS - 1:
            a = plus(a, up[3 - step])
            b = plus(b, down[1 + step])
    return half_sum(b, down[0], 1, half_sum(a, up[0], 0))


def block_table(rider, core):
    offsets = rider.reshape(CHIPS, 2, SLOTS).astype(jnp.int32)
    c = jnp.arange(CHIPS, dtype=jnp.int32)[:, None, None]
    i = jnp.arange(2, dtype=jnp.int32)[None, :, None]
    target = 4 * c + 2 * core + i - offsets
    side = ((target >> 1) & 1) ^ core
    place = ((side * CHIPS + (target >> 2)) << 1) + (target & 1)
    return jnp.where(target >= 0, place, -1).reshape(2 * CHIPS, SLOTS)


def local(queries, key_states, value_states, out_weight, cotangent, block_offsets):
    core = lax.axis_index("seq") % 2
    cot = cotangent[0]
    cot_other = lax.ppermute(cot, "seq", CORE_SWAP)
    x = exchange(pack(block_offsets[0], key_states[0], value_states[0], queries[0]))
    x, g, cot_other = after(x, grad_attn_by_head(cot, out_weight), cot_other)
    y = lax.ppermute(x, "seq", CORE_SWAP)
    g = exchange(g)
    table = block_table(x[:, RIDER, 0 : 2 * SLOTS], core)
    table, place = after(table, jnp.stack([core, lax.axis_index("dp")]))
    out, lse = attention_forward(table, x, y)
    g, out = after(g, out)
    out_home = lax.all_to_all(out, "seq", 0, 0, tiled=True)
    own, other, gq = attention_backward(table, x, y, g, lse)
    out_home, own, other, gq = after(out_home, own, other, gq)
    gq_home = exchange(gq)
    got = lax.ppermute(other, "seq", CORE_SWAP)
    got, out_home = after(got, out_home)
    by_core = out_home.reshape(HEADS, 2, HEAD // 2, TOK)
    up, down = weight_partial(place, by_core, cot, cot_other)
    *up, got = after(*up, got)
    by_doc = sum_over_docs(up, down)
    gq_home, gathered = after(gq_home, combine(own, got))
    kv_home = exchange(gathered)
    kv_home, by_doc = after(kv_home, by_doc)
    weight_grad = jnp.sum(exchange(by_doc).astype(f32), axis=0)
    (gq,) = unpack(gq_home, 1)
    gk, gv = unpack(kv_home, 2)
    return gq[None], gk[None], gv[None], weight_grad


def solution(mesh):
    in_specs = (
        P("dp", "seq", None),
        P("dp", "seq", None),
        P("dp", "seq", None),
        P(),
        P("dp", "seq", None),
        P("dp", "seq", None),
    )
    out_specs = (
        P("dp", "seq", None),
        P("dp", "seq", None),
        P("dp", "seq", None),
        P(("dp", "seq"), None),
    )
    return jax.shard_map(local, mesh=mesh, in_specs=in_specs, out_specs=out_specs, check_vma=False)
```

```python
import math

import jax
import jax.numpy as jnp
from jax import lax
from jax.experimental import pallas as pl
from jax.experimental.pallas import tpu as pltpu
from jax.sharding import PartitionSpec as P

HEADS = 16
HEAD = 128
BLK = 128
SLOTS = 4
D = HEADS * HEAD
TOK = 256
CHIPS = 16
BLOCKS = 64
WIDTH = (1 + SLOTS) * BLK
DOCS = 4
CHUNK = D // 4 // DOCS
RIDER = 3 * TOK
ROWS = 3 * TOK + 8
SCALE = HEAD ** (-0.5)
SCALE2 = SCALE * math.log2(math.e)
NEG = -1e30
bf16 = jnp.bfloat16
f32 = jnp.float32

SAME_CORE = [[2 * c + k for c in range(CHIPS)] for k in range(2)]
CORE_SWAP = [(i, i ^ 1) for i in range(2 * CHIPS)]

UNROLL = 4
GROUP = 4
PACK = 4
VMEM_LIMIT = 56 * 1024 * 1024


def dot(a, b, ca, cb):
    return lax.dot_general(a, b, (((ca,), (cb,)), ((), ())), preferred_element_type=f32)


def cost(flops, transcendentals=0, bytes_accessed=0):
    return pl.CostEstimate(
        flops=flops, transcendentals=transcendentals, bytes_accessed=bytes_accessed
    )


PAIRS = BLOCKS // 2 * BLK * (1 + SLOTS) * BLK
PAIR_FLOPS = 2 * HEAD * PAIRS
MIB = 1024 * 1024


def exchange(x):
    return lax.all_to_all(x, "seq", 0, 0, axis_index_groups=SAME_CORE, tiled=True)


def after(*values):
    return lax.optimization_barrier(values)


def pack_body(offs, k_ref, v_ref, q_ref, x_ref):
    lane = lax.broadcasted_iota(jnp.int32, (8, 128), 1)
    val = jnp.zeros((8, 128), jnp.int32)
    for j in range(2 * SLOTS):
        val = jnp.where(lane == j, offs[j // SLOTS, j % SLOTS], val)
    rider = val.astype(f32).astype(bf16)
    for h in range(PACK):
        for t, ref in enumerate((k_ref, v_ref, q_ref)):
            x_ref[h, t * TOK : (t + 1) * TOK, :] = ref[:, h * HEAD : (h + 1) * HEAD]
        x_ref[h, RIDER : RIDER + 8, :] = rider


def pack(offs, k, v, q):
    rows = pl.BlockSpec((TOK, PACK * HEAD), lambda i: (0, i))
    return pl.pallas_call(
        pack_body,
        out_shape=jax.ShapeDtypeStruct((HEADS, ROWS, HEAD), bf16),
        grid=(HEADS // PACK,),
        in_specs=[pl.BlockSpec(memory_space=pltpu.SMEM), rows, rows, rows],
        out_specs=pl.BlockSpec((PACK, ROWS, HEAD), lambda i: (i, 0, 0)),
        compiler_params=pltpu.CompilerParams(vmem_limit_bytes=VMEM_LIMIT),
        name="pack",
    )(offs, k, v, q)


def unpack_body(r_ref, *refs):
    for h in range(PACK):
        for t, ref in enumerate(refs):
            ref[:, h * HEAD : (h + 1) * HEAD] = r_ref[h, t * TOK : (t + 1) * TOK, :]


def unpack(r, n):
    out = jax.ShapeDtypeStruct((TOK, D), bf16)
    rows = pl.BlockSpec((TOK, PACK * HEAD), lambda i: (0, i))
    return pl.pallas_call(
        unpack_body,
        out_shape=(out,) * n,
        grid=(HEADS // PACK,),
        in_specs=[pl.BlockSpec((PACK, n * TOK, HEAD), lambda i: (i, 0, 0))],
        out_specs=[rows] * n,
        compiler_params=pltpu.CompilerParams(vmem_limit_bytes=VMEM_LIMIT),
        cost_estimate=cost(0, 0, 2 * n * MIB),
        name="unpack",
    )(r)


def grad_attn_body(c_ref, w_ref, o_ref):
    g = dot(c_ref[...], w_ref[...], 1, 1).astype(bf16)
    for j in range(2):
        o_ref[j] = g[:, j * HEAD : (j + 1) * HEAD]


def grad_attn_by_head(cot, weight):
    return pl.pallas_call(
        grad_attn_body,
        out_shape=jax.ShapeDtypeStruct((HEADS, TOK, HEAD), bf16),
        grid=(HEADS // 2,),
        in_specs=[
            pl.BlockSpec((TOK, D), lambda i: (0, 0)),
            pl.BlockSpec((2 * HEAD, D), lambda i: (i, 0)),
        ],
        out_specs=pl.BlockSpec((2, TOK, HEAD), lambda i: (i, 0, 0)),
        compiler_params=pltpu.CompilerParams(vmem_limit_bytes=VMEM_LIMIT),
        cost_estimate=cost(2 * TOK * D * D, 0, 10 * MIB),
        name="grad_attn",
    )(cot, weight)


def load_pool(x_ref, y_ref, kv, qs, sems):
    groups = []
    for j in range(CHIPS // GROUP):
        at = pl.ds(j * GROUP, GROUP)
        groups.append(
            [
                pltpu.make_async_copy(
                    x_ref.at[at, pl.ds(0, 2 * TOK), :], kv.at[at], sems.at[3 * j]
                ),
                pltpu.make_async_copy(
                    y_ref.at[at, pl.ds(0, 2 * TOK), :],
                    kv.at[pl.ds(CHIPS + j * GROUP, GROUP)],
                    sems.at[3 * j + 1],
                ),
                pltpu.make_async_copy(
                    x_ref.at[at, pl.ds(2 * TOK, TOK), :], qs.at[at], sems.at[3 * j + 2]
                ),
            ]
        )
    return groups


def listed(table, c, i):
    places = [(c, i * BLK, None)]
    for s in range(SLOTS):
        code = table[2 * c + i, s]
        f = jnp.maximum(code, 0)
        bias = jnp.where(code >= 0, 0.0, -NEG).astype(f32)
        places.append((f // 2, pl.multiple_of((f % 2) * BLK, BLK), bias))
    return places


def causal():
    u = lax.broadcasted_iota(jnp.int32, (BLK, BLK), 0)
    t = lax.broadcasted_iota(jnp.int32, (BLK, BLK), 1)
    return u <= t


def forward_body(table, x_ref, y_ref, o_ref, p_ref, kv, qs, ps, sems):
    groups = load_pool(x_ref, y_ref, kv, qs, sems)
    for copies in groups:
        for copy in copies:
            copy.start()

    def block(c, i):
        places = listed(table, c, i)
        q = qs[c, pl.ds(i * BLK, BLK), :]
        keys = jnp.concatenate([kv[p, pl.ds(r, BLK), :] for p, r, _ in places], axis=0)
        every = dot(keys, q, 1, 1)
        raw = [every[s * BLK : (s + 1) * BLK, :] for s in range(1 + SLOTS)]
        raw[0] = jnp.where(causal(), raw[0], NEG)
        peak = jnp.max(raw[0], axis=0, keepdims=True)
        for (_, _, bias), s in zip(places[1:], raw[1:]):
            peak = jnp.maximum(peak, jnp.max(s, axis=0, keepdims=True) - bias)
        peak = peak * SCALE2
        weights = []
        total = None
        for (_, _, bias), s in zip(places, raw):
            w = jnp.exp2(s * SCALE2 - (peak if bias is None else peak + bias))
            part = jnp.sum(w, axis=0, keepdims=True)
            total = part if total is None else total + part
            weights.append(w)
        inverse = 1.0 / total
        prob = jnp.concatenate([(w * inverse).astype(bf16) for w in weights], axis=0)
        ps[2 * c + i] = prob
        values = jnp.concatenate([kv[p, pl.ds(TOK + r, BLK), :] for p, r, _ in places], axis=0)
        return dot(values, prob, 0, 0).astype(bf16)

    def step(c, carry):
        for i in range(2):
            out = block(c, i)
            for g in range(8):
                row = (g // 2) * 16
                o_ref[2 * c + g % 2, row : row + 16, i * BLK : (i + 1) * BLK] = out[
                    g * 16 : g * 16 + 16, :
                ]
        return carry

    sends = []
    for j, copies in enumerate(groups):
        for copy in copies:
            copy.wait()
        lax.fori_loop(j * GROUP, (j + 1) * GROUP, step, 0, unroll=UNROLL)
        at = pl.ds(2 * j * GROUP, 2 * GROUP)
        sends.append(pltpu.make_async_copy(ps.at[at], p_ref.at[at], sems.at[3 * len(groups) + j]))
        sends[j].start()
    for copy in sends:
        copy.wait()


def attention_forward(table, x, y):
    return pl.pallas_call(
        forward_body,
        out_shape=(
            jax.ShapeDtypeStruct((2 * CHIPS, HEAD // 2, TOK), bf16),
            jax.ShapeDtypeStruct((2 * CHIPS, WIDTH, BLK), bf16),
        ),
        in_specs=[pl.BlockSpec(memory_space=pltpu.SMEM)] + [pl.BlockSpec(memory_space=pl.ANY)] * 2,
        out_specs=[pl.BlockSpec(memory_space=pltpu.VMEM), pl.BlockSpec(memory_space=pl.ANY)],
        scratch_shapes=[
            pltpu.VMEM((2 * CHIPS, 2 * TOK, HEAD), bf16),
            pltpu.VMEM((CHIPS, TOK, HEAD), bf16),
            pltpu.VMEM((2 * CHIPS, WIDTH, BLK), bf16),
            pltpu.SemaphoreType.DMA((4 * (CHIPS // GROUP),)),
        ],
        compiler_params=pltpu.CompilerParams(vmem_limit_bytes=VMEM_LIMIT),
        cost_estimate=cost(2 * PAIR_FLOPS, PAIRS, 12 * MIB),
        name="attn_fwd",
    )(table, x, y)


def backward_body(
    table, x_ref, y_ref, g_ref, p_ref, own_ref, other_ref, gq_ref, kv, qs, gs, ps, acck, accv, own, other, gq, sems
):
    groups = load_pool(x_ref, y_ref, kv, qs, sems)
    sends = []
    n = CHIPS // GROUP
    for j in range(n):
        at = pl.ds(j * GROUP, GROUP)
        groups[j].append(pltpu.make_async_copy(g_ref.at[at], gs.at[at], sems.at[3 * n + j]))
        two = pl.ds(2 * j * GROUP, 2 * GROUP)
        groups[j].append(pltpu.make_async_copy(p_ref.at[two], ps.at[two], sems.at[7 * n + j]))
        sends.append(
            [
                pltpu.make_async_copy(
                    gq.at[at], gq_ref.at[at], sems.at[4 * n + j]
                ),
                pltpu.make_async_copy(
                    own.at[at], own_ref.at[at], sems.at[5 * n + j]
                ),
                pltpu.make_async_copy(other.at[at], other_ref.at[at], sems.at[6 * n + j]),
            ]
        )
    for copies in groups:
        for copy in copies:
            copy.start()

    def clear(j, carry):
        acck[CHIPS + j] = jnp.zeros((TOK, HEAD), f32)
        accv[CHIPS + j] = jnp.zeros((TOK, HEAD), f32)
        return carry

    lax.fori_loop(0, CHIPS, clear, 0)

    def block(c, i):
        places = listed(table, c, i)
        q = qs[c, pl.ds(i * BLK, BLK), :]
        g = gs[c, pl.ds(i * BLK, BLK), :]
        keys = jnp.concatenate([kv[p, pl.ds(r, BLK), :] for p, r, _ in places], axis=0)
        values = jnp.concatenate([kv[p, pl.ds(TOK + r, BLK), :] for p, r, _ in places], axis=0)
        grads = dot(values, g, 1, 1)
        low = ps[2 * c + i]
        prob = low.astype(f32)
        row_dot = jnp.sum(prob * grads, axis=0, keepdims=True)
        score = (prob * (grads - row_dot)).astype(bf16)
        gk = dot(score, q, 1, 0)
        gv = dot(low, g, 1, 0)
        for j, (p, r, _) in enumerate(places):
            at = pl.ds(r, BLK)
            if j == 0:
                acck[p, at, :] = gk[0:BLK, :]
                accv[p, at, :] = gv[0:BLK, :]
            else:
                acck[p, at, :] += gk[j * BLK : (j + 1) * BLK, :]
                accv[p, at, :] += gv[j * BLK : (j + 1) * BLK, :]
        gq[c, pl.ds(i * BLK, BLK), :] = (dot(score, keys, 0, 0) * SCALE).astype(bf16)

    def step(c, carry):
        for i in range(2):
            block(c, i)
        return carry

    def flush(j, carry):
        own[j, 0:TOK, :] = (acck[j] * SCALE).astype(bf16)
        own[j, TOK : 2 * TOK, :] = accv[j].astype(bf16)
        other[j, 0:TOK, :] = (acck[CHIPS + j] * SCALE).astype(bf16)
        other[j, TOK : 2 * TOK, :] = accv[CHIPS + j].astype(bf16)
        return carry

    for j in range(n + 2):
        if j < n:
            for copy in groups[j]:
                copy.wait()
            lax.fori_loop(j * GROUP, (j + 1) * GROUP, step, 0, unroll=UNROLL)
            sends[j][0].start()
        if j >= 2:
            lax.fori_loop((j - 2) * GROUP, (j - 1) * GROUP, flush, 0)
            sends[j - 2][1].start()
            sends[j - 2][2].start()
    for copies in sends:
        for copy in copies:
            copy.wait()


def attention_backward(table, x, y, g, prob):
    return pl.pallas_call(
        backward_body,
        out_shape=(
            jax.ShapeDtypeStruct((CHIPS, 2 * TOK, HEAD), bf16),
            jax.ShapeDtypeStruct((CHIPS, 2 * TOK, HEAD), bf16),
            jax.ShapeDtypeStruct((CHIPS, TOK, HEAD), bf16),
        ),
        in_specs=[pl.BlockSpec(memory_space=pltpu.SMEM)]
        + [pl.BlockSpec(memory_space=pl.ANY)] * 4,
        out_specs=[pl.BlockSpec(memory_space=pl.ANY)] * 3,
        scratch_shapes=[
            pltpu.VMEM((2 * CHIPS, 2 * TOK, HEAD), bf16),
            pltpu.VMEM((CHIPS, TOK, HEAD), bf16),
            pltpu.VMEM((CHIPS, TOK, HEAD), bf16),
            pltpu.VMEM((2 * CHIPS, WIDTH, BLK), bf16),
            pltpu.VMEM((2 * CHIPS, TOK, HEAD), f32),
            pltpu.VMEM((2 * CHIPS, TOK, HEAD), f32),
            pltpu.VMEM((CHIPS, 2 * TOK, HEAD), bf16),
            pltpu.VMEM((CHIPS, 2 * TOK, HEAD), bf16),
            pltpu.VMEM((CHIPS, TOK, HEAD), bf16),
            pltpu.SemaphoreType.DMA((8 * (CHIPS // GROUP),)),
        ],
        compiler_params=pltpu.CompilerParams(vmem_limit_bytes=VMEM_LIMIT),
        cost_estimate=cost(4 * PAIR_FLOPS, 0, 17 * MIB),
        name="attn_bwd",
    )(table, x, y, g, prob)


def combine_body(own_ref, got_ref, o_ref):
    o_ref[...] = (own_ref[...].astype(f32) + got_ref[...].astype(f32)).astype(bf16)


def combine(own, got):
    n = 4
    rows = pl.BlockSpec((n, 2 * TOK, HEAD), lambda i: (i, 0, 0))
    return pl.pallas_call(
        combine_body,
        out_shape=jax.ShapeDtypeStruct((CHIPS, 2 * TOK, HEAD), bf16),
        grid=(CHIPS // n,),
        in_specs=[rows, rows],
        out_specs=rows,
        compiler_params=pltpu.CompilerParams(vmem_limit_bytes=VMEM_LIMIT),
        cost_estimate=cost(CHIPS * 2 * TOK * HEAD, 0, 6 * MIB),
        name="combine",
    )(own, got)


def weight_body(place, oa_ref, ob_ref, ca_ref, cb_ref, *rest):
    outs, buf, sems = rest[: 2 * DOCS], rest[2 * DOCS], rest[2 * DOCS + 1]
    copies = []
    for d in (3, 1, 2, 0):
        heads = pl.ds(((place[1] + d) % DOCS) * (HEADS // DOCS), HEADS // DOCS)
        a = oa_ref[heads].reshape(2 * CHUNK, TOK)
        b = ob_ref[heads].reshape(2 * CHUNK, TOK)
        buf[d] = (dot(a, ca_ref[...], 1, 0) + dot(b, cb_ref[...], 1, 0)).astype(bf16)
        for half in range(2):
            j = 2 * d + half
            copies.append(
                pltpu.make_async_copy(
                    buf.at[d, pl.ds(half * CHUNK, CHUNK), :], outs[j], sems.at[j]
                )
            )
            copies[-1].start()
    for copy in copies:
        copy.wait()


def weight_partial(place, out, ca, cb):
    own = pl.BlockSpec((HEADS, 1, HEAD // 2, TOK), lambda i, place: (0, place[0], 0, 0))
    other = pl.BlockSpec((HEADS, 1, HEAD // 2, TOK), lambda i, place: (0, 1 - place[0], 0, 0))
    whole = pl.BlockSpec((TOK, D), lambda i, place: (0, 0))
    outs = pl.pallas_call(
        weight_body,
        out_shape=(jax.ShapeDtypeStruct((CHUNK, D), bf16),) * (2 * DOCS),
        grid_spec=pltpu.PrefetchScalarGridSpec(
            num_scalar_prefetch=1,
            grid=(1,),
            in_specs=[own, other, whole, whole],
            out_specs=[pl.BlockSpec(memory_space=pl.ANY)] * (2 * DOCS),
            scratch_shapes=[
                pltpu.VMEM((DOCS, 2 * CHUNK, D), bf16),
                pltpu.SemaphoreType.DMA((2 * DOCS,)),
            ],
        ),
        compiler_params=pltpu.CompilerParams(vmem_limit_bytes=VMEM_LIMIT),
        cost_estimate=cost(2 * TOK * D * D, 0, 8 * MIB),
        name="weight_partial",
    )(place, out, out, ca, cb)
    return outs[0::2], outs[1::2]


def plus(a, b):
    return (a.astype(f32) + b.astype(f32)).astype(bf16)


def sum_over_docs(up, down, room, first):
    route_up = [(i, (i + 1) % DOCS) for i in range(DOCS)]
    route_down = [(i, (i - 1) % DOCS) for i in range(DOCS)]
    a, b = up[3], down[1]
    for step in range(1, DOCS):
        a = lax.ppermute(a, "dp", route_up)
        b = lax.ppermute(b, "dp", route_down)
        if step == 1:
            a, b, first = after(a, b, first)
        a = plus(a, up[3 - step])
        b = plus(b, down[(1 + step) % DOCS])
    n = CHIPS // 2
    joined = lax.dynamic_update_slice(room, a.reshape(n, 16, D), (0, 0, 0))
    return lax.dynamic_update_slice(joined, b.reshape(n, 16, D), (n, 0, 0)), first


def block_table(rider, core):
    offsets = rider.reshape(CHIPS, 2, SLOTS).astype(jnp.int32)
    c = jnp.arange(CHIPS, dtype=jnp.int32)[:, None, None]
    i = jnp.arange(2, dtype=jnp.int32)[None, :, None]
    target = 4 * c + 2 * core + i - offsets
    side = ((target >> 1) & 1) ^ core
    place = ((side * CHIPS + (target >> 2)) << 1) + (target & 1)
    return jnp.where(target >= 0, place, -1).reshape(2 * CHIPS, SLOTS)


def local(queries, key_states, value_states, out_weight, cotangent, block_offsets):
    core = lax.axis_index("seq") % 2
    cot = cotangent[0]
    cot_other = lax.ppermute(cot, "seq", CORE_SWAP)
    x = exchange(pack(block_offsets[0], key_states[0], value_states[0], queries[0]))
    x, g, cot_other = after(x, grad_attn_by_head(cot, out_weight), cot_other)
    y = lax.ppermute(x, "seq", CORE_SWAP)
    g = exchange(g)
    table = block_table(x[:, RIDER, 0 : 2 * SLOTS], core)
    table, place = after(table, jnp.stack([core, lax.axis_index("dp")]))
    out, prob = attention_forward(table, x, y)
    g, out = after(g, out)
    out_home = lax.all_to_all(out, "seq", 0, 0, tiled=True)
    own, other, gq = attention_backward(table, x, y, g, prob)
    out_home, own, other, gq = after(out_home, own, other, gq)
    gq_home = exchange(gq)
    got = lax.ppermute(other, "seq", CORE_SWAP)
    got, out_home = after(got, out_home)
    by_core = out_home.reshape(HEADS, 2, HEAD // 2, TOK)
    up, down = weight_partial(place, by_core, cot, cot_other)
    *up, got = after(*up, got)
    room = jnp.zeros((CHIPS, 16, D), bf16)
    by_doc, (gq_home, gathered) = sum_over_docs(up, down, room, (gq_home, combine(own, got)))
    kv_home = exchange(gathered)
    kv_home, by_doc = after(kv_home, by_doc)
    weight_grad = jnp.sum(exchange(by_doc).astype(f32), axis=0)
    (gq,) = unpack(gq_home, 1)
    gk, gv = unpack(kv_home, 2)
    return gq[None], gk[None], gv[None], weight_grad


def solution(mesh):
    in_specs = (
        P("dp", "seq", None),
        P("dp", "seq", None),
        P("dp", "seq", None),
        P(),
        P("dp", "seq", None),
        P("dp", "seq", None),
    )
    out_specs = (
        P("dp", "seq", None),
        P("dp", "seq", None),
        P("dp", "seq", None),
        P(("dp", "seq"), None),
    )
    return jax.shard_map(local, mesh=mesh, in_specs=in_specs, out_specs=out_specs, check_vma=False)
```

```python
import math

import jax
import jax.numpy as jnp
from jax import lax
from jax.experimental import pallas as pl
from jax.experimental.pallas import tpu as pltpu
from jax.sharding import PartitionSpec as P

HEADS = 16
HEAD = 128
BLK = 128
SLOTS = 4
D = HEADS * HEAD
TOK = 256
CHIPS = 16
BLOCKS = 64
WIDTH = (1 + SLOTS) * BLK
DOCS = 4
CHUNK = D // 4 // DOCS
RIDER = 3 * TOK
ROWS = 3 * TOK + 8
SCALE = HEAD ** (-0.5)
SCALE2 = SCALE * math.log2(math.e)
NEG = -1e30
bf16 = jnp.bfloat16
f32 = jnp.float32

SAME_CORE = [[2 * c + k for c in range(CHIPS)] for k in range(2)]
CORE_SWAP = [(i, i ^ 1) for i in range(2 * CHIPS)]

UNROLL = 4
GROUP = 4
PACK = 8
VMEM_LIMIT = 56 * 1024 * 1024


def dot(a, b, ca, cb):
    return lax.dot_general(a, b, (((ca,), (cb,)), ((), ())), preferred_element_type=f32)


def cost(flops, transcendentals=0, bytes_accessed=0):
    return pl.CostEstimate(
        flops=flops, transcendentals=transcendentals, bytes_accessed=bytes_accessed
    )


PAIRS = BLOCKS // 2 * BLK * (1 + SLOTS) * BLK
PAIR_FLOPS = 2 * HEAD * PAIRS
MIB = 1024 * 1024


def exchange(x):
    return lax.all_to_all(x, "seq", 0, 0, axis_index_groups=SAME_CORE, tiled=True)


def after(*values):
    return lax.optimization_barrier(values)


def pack_body(offs, k_ref, v_ref, q_ref, x_ref):
    lane = lax.broadcasted_iota(jnp.int32, (8, 128), 1)
    val = jnp.zeros((8, 128), jnp.int32)
    for j in range(2 * SLOTS):
        val = jnp.where(lane == j, offs[j // SLOTS, j % SLOTS], val)
    rider = val.astype(f32).astype(bf16)
    for h in range(PACK):
        for t, ref in enumerate((k_ref, v_ref, q_ref)):
            x_ref[h, t * TOK : (t + 1) * TOK, :] = ref[:, h * HEAD : (h + 1) * HEAD]
        x_ref[h, RIDER : RIDER + 8, :] = rider


def pack(offs, k, v, q):
    rows = pl.BlockSpec((TOK, PACK * HEAD), lambda i: (0, i))
    return pl.pallas_call(
        pack_body,
        out_shape=jax.ShapeDtypeStruct((HEADS, ROWS, HEAD), bf16),
        grid=(HEADS // PACK,),
        in_specs=[pl.BlockSpec(memory_space=pltpu.SMEM), rows, rows, rows],
        out_specs=pl.BlockSpec((PACK, ROWS, HEAD), lambda i: (i, 0, 0)),
        compiler_params=pltpu.CompilerParams(vmem_limit_bytes=VMEM_LIMIT),
        name="pack",
    )(offs, k, v, q)


def unpack_body(r_ref, *refs):
    for h in range(PACK):
        for t, ref in enumerate(refs):
            ref[:, h * HEAD : (h + 1) * HEAD] = r_ref[h, t * TOK : (t + 1) * TOK, :]


def unpack(r, n):
    out = jax.ShapeDtypeStruct((TOK, D), bf16)
    rows = pl.BlockSpec((TOK, PACK * HEAD), lambda i: (0, i))
    return pl.pallas_call(
        unpack_body,
        out_shape=(out,) * n,
        grid=(HEADS // PACK,),
        in_specs=[pl.BlockSpec((PACK, n * TOK, HEAD), lambda i: (i, 0, 0))],
        out_specs=[rows] * n,
        compiler_params=pltpu.CompilerParams(vmem_limit_bytes=VMEM_LIMIT),
        cost_estimate=cost(0, 0, 2 * n * MIB),
        name="unpack",
    )(r)


def grad_attn_body(c_ref, w_ref, o_ref):
    g = dot(c_ref[...], w_ref[...], 1, 1).astype(bf16)
    for j in range(2):
        o_ref[j] = g[:, j * HEAD : (j + 1) * HEAD]


def grad_attn_by_head(cot, weight):
    return pl.pallas_call(
        grad_attn_body,
        out_shape=jax.ShapeDtypeStruct((HEADS, TOK, HEAD), bf16),
        grid=(HEADS // 2,),
        in_specs=[
            pl.BlockSpec((TOK, D), lambda i: (0, 0)),
            pl.BlockSpec((2 * HEAD, D), lambda i: (i, 0)),
        ],
        out_specs=pl.BlockSpec((2, TOK, HEAD), lambda i: (i, 0, 0)),
        compiler_params=pltpu.CompilerParams(vmem_limit_bytes=VMEM_LIMIT),
        cost_estimate=cost(2 * TOK * D * D, 0, 10 * MIB),
        name="grad_attn",
    )(cot, weight)


def load_pool(x_ref, y_ref, kv, qs, sems):
    groups = []
    for j in range(CHIPS // GROUP):
        at = pl.ds(j * GROUP, GROUP)
        groups.append(
            [
                pltpu.make_async_copy(
                    x_ref.at[at, pl.ds(0, 2 * TOK), :], kv.at[at], sems.at[3 * j]
                ),
                pltpu.make_async_copy(
                    y_ref.at[at, pl.ds(0, 2 * TOK), :],
                    kv.at[pl.ds(CHIPS + j * GROUP, GROUP)],
                    sems.at[3 * j + 1],
                ),
                pltpu.make_async_copy(
                    x_ref.at[at, pl.ds(2 * TOK, TOK), :], qs.at[at], sems.at[3 * j + 2]
                ),
            ]
        )
    return groups


def listed(table, c, i):
    places = [(c, i * BLK, None)]
    for s in range(SLOTS):
        code = table[2 * c + i, s]
        f = jnp.maximum(code, 0)
        bias = jnp.where(code >= 0, 0.0, -NEG).astype(f32)
        places.append((f // 2, pl.multiple_of((f % 2) * BLK, BLK), bias))
    return places


def causal():
    u = lax.broadcasted_iota(jnp.int32, (BLK, BLK), 0)
    t = lax.broadcasted_iota(jnp.int32, (BLK, BLK), 1)
    return u <= t


def forward_body(table, x_ref, y_ref, o_ref, p_ref, kv, qs, ps, sems):
    groups = load_pool(x_ref, y_ref, kv, qs, sems)
    for copies in groups:
        for copy in copies:
            copy.start()

    def block(c, i):
        places = listed(table, c, i)
        q = qs[c, pl.ds(i * BLK, BLK), :]
        keys = jnp.concatenate([kv[p, pl.ds(r, BLK), :] for p, r, _ in places], axis=0)
        every = dot(keys, q, 1, 1)
        raw = [every[s * BLK : (s + 1) * BLK, :] for s in range(1 + SLOTS)]
        raw[0] = jnp.where(causal(), raw[0], NEG)
        peak = jnp.max(raw[0], axis=0, keepdims=True)
        for (_, _, bias), s in zip(places[1:], raw[1:]):
            peak = jnp.maximum(peak, jnp.max(s, axis=0, keepdims=True) - bias)
        peak = peak * SCALE2
        weights = []
        total = None
        for (_, _, bias), s in zip(places, raw):
            w = jnp.exp2(s * SCALE2 - (peak if bias is None else peak + bias))
            part = jnp.sum(w, axis=0, keepdims=True)
            total = part if total is None else total + part
            weights.append(w)
        inverse = 1.0 / total
        prob = jnp.concatenate([(w * inverse).astype(bf16) for w in weights], axis=0)
        ps[2 * c + i] = prob
        values = jnp.concatenate([kv[p, pl.ds(TOK + r, BLK), :] for p, r, _ in places], axis=0)
        return dot(values, prob, 0, 0).astype(bf16)

    def step(c, carry):
        for i in range(2):
            out = block(c, i)
            for g in range(8):
                row = (g // 2) * 16
                o_ref[2 * c + g % 2, row : row + 16, i * BLK : (i + 1) * BLK] = out[
                    g * 16 : g * 16 + 16, :
                ]
        return carry

    sends = []
    for j, copies in enumerate(groups):
        for copy in copies:
            copy.wait()
        lax.fori_loop(j * GROUP, (j + 1) * GROUP, step, 0, unroll=UNROLL)
        at = pl.ds(2 * j * GROUP, 2 * GROUP)
        sends.append(pltpu.make_async_copy(ps.at[at], p_ref.at[at], sems.at[3 * len(groups) + j]))
        sends[j].start()
    for copy in sends:
        copy.wait()


def attention_forward(table, x, y):
    return pl.pallas_call(
        forward_body,
        out_shape=(
            jax.ShapeDtypeStruct((2 * CHIPS, HEAD // 2, TOK), bf16),
            jax.ShapeDtypeStruct((2 * CHIPS, WIDTH, BLK), bf16),
        ),
        in_specs=[pl.BlockSpec(memory_space=pltpu.SMEM)] + [pl.BlockSpec(memory_space=pl.ANY)] * 2,
        out_specs=[pl.BlockSpec(memory_space=pltpu.VMEM), pl.BlockSpec(memory_space=pl.ANY)],
        scratch_shapes=[
            pltpu.VMEM((2 * CHIPS, 2 * TOK, HEAD), bf16),
            pltpu.VMEM((CHIPS, TOK, HEAD), bf16),
            pltpu.VMEM((2 * CHIPS, WIDTH, BLK), bf16),
            pltpu.SemaphoreType.DMA((4 * (CHIPS // GROUP),)),
        ],
        compiler_params=pltpu.CompilerParams(vmem_limit_bytes=VMEM_LIMIT),
        cost_estimate=cost(2 * PAIR_FLOPS, PAIRS, 12 * MIB),
        name="attn_fwd",
    )(table, x, y)


def backward_body(
    table, x_ref, y_ref, g_ref, p_ref, own_ref, other_ref, gq_ref, kv, qs, gs, ps, acck, accv, own, other, gq, sems
):
    groups = load_pool(x_ref, y_ref, kv, qs, sems)
    sends = []
    n = CHIPS // GROUP
    for j in range(n):
        at = pl.ds(j * GROUP, GROUP)
        groups[j].append(pltpu.make_async_copy(g_ref.at[at], gs.at[at], sems.at[3 * n + j]))
        two = pl.ds(2 * j * GROUP, 2 * GROUP)
        groups[j].append(pltpu.make_async_copy(p_ref.at[two], ps.at[two], sems.at[7 * n + j]))
        sends.append(
            [
                pltpu.make_async_copy(
                    gq.at[at], gq_ref.at[at], sems.at[4 * n + j]
                ),
                pltpu.make_async_copy(
                    own.at[at], own_ref.at[at], sems.at[5 * n + j]
                ),
                pltpu.make_async_copy(other.at[at], other_ref.at[at], sems.at[6 * n + j]),
            ]
        )
    for copies in groups:
        for copy in copies:
            copy.start()

    def clear(j, carry):
        acck[CHIPS + j] = jnp.zeros((TOK, HEAD), f32)
        accv[CHIPS + j] = jnp.zeros((TOK, HEAD), f32)
        return carry

    lax.fori_loop(0, CHIPS, clear, 0)

    def block(c, i):
        places = listed(table, c, i)
        q = qs[c, pl.ds(i * BLK, BLK), :]
        g = gs[c, pl.ds(i * BLK, BLK), :]
        keys = jnp.concatenate([kv[p, pl.ds(r, BLK), :] for p, r, _ in places], axis=0)
        values = jnp.concatenate([kv[p, pl.ds(TOK + r, BLK), :] for p, r, _ in places], axis=0)
        grads = dot(values, g, 1, 1)
        low = ps[2 * c + i]
        prob = low.astype(f32)
        row_dot = jnp.sum(prob * grads, axis=0, keepdims=True)
        score = (prob * (grads - row_dot)).astype(bf16)
        gk = dot(score, q, 1, 0)
        gv = dot(low, g, 1, 0)
        for j, (p, r, _) in enumerate(places):
            at = pl.ds(r, BLK)
            if j == 0:
                acck[p, at, :] = gk[0:BLK, :]
                accv[p, at, :] = gv[0:BLK, :]
            else:
                acck[p, at, :] += gk[j * BLK : (j + 1) * BLK, :]
                accv[p, at, :] += gv[j * BLK : (j + 1) * BLK, :]
        gq[c, pl.ds(i * BLK, BLK), :] = (dot(score, keys, 0, 0) * SCALE).astype(bf16)

    def step(c, carry):
        for i in range(2):
            block(c, i)
        return carry

    def flush(j, carry):
        own[j, 0:TOK, :] = (acck[j] * SCALE).astype(bf16)
        own[j, TOK : 2 * TOK, :] = accv[j].astype(bf16)
        other[j, 0:TOK, :] = (acck[CHIPS + j] * SCALE).astype(bf16)
        other[j, TOK : 2 * TOK, :] = accv[CHIPS + j].astype(bf16)
        return carry

    for j in range(n + 2):
        if j < n:
            for copy in groups[j]:
                copy.wait()
            lax.fori_loop(j * GROUP, (j + 1) * GROUP, step, 0, unroll=UNROLL)
            sends[j][0].start()
        if j >= 2:
            lax.fori_loop((j - 2) * GROUP, (j - 1) * GROUP, flush, 0)
            sends[j - 2][1].start()
            sends[j - 2][2].start()
    for copies in sends:
        for copy in copies:
            copy.wait()


def attention_backward(table, x, y, g, prob):
    return pl.pallas_call(
        backward_body,
        out_shape=(
            jax.ShapeDtypeStruct((CHIPS, 2 * TOK, HEAD), bf16),
            jax.ShapeDtypeStruct((CHIPS, 2 * TOK, HEAD), bf16),
            jax.ShapeDtypeStruct((CHIPS, TOK, HEAD), bf16),
        ),
        in_specs=[pl.BlockSpec(memory_space=pltpu.SMEM)]
        + [pl.BlockSpec(memory_space=pl.ANY)] * 4,
        out_specs=[pl.BlockSpec(memory_space=pl.ANY)] * 3,
        scratch_shapes=[
            pltpu.VMEM((2 * CHIPS, 2 * TOK, HEAD), bf16),
            pltpu.VMEM((CHIPS, TOK, HEAD), bf16),
            pltpu.VMEM((CHIPS, TOK, HEAD), bf16),
            pltpu.VMEM((2 * CHIPS, WIDTH, BLK), bf16),
            pltpu.VMEM((2 * CHIPS, TOK, HEAD), f32),
            pltpu.VMEM((2 * CHIPS, TOK, HEAD), f32),
            pltpu.VMEM((CHIPS, 2 * TOK, HEAD), bf16),
            pltpu.VMEM((CHIPS, 2 * TOK, HEAD), bf16),
            pltpu.VMEM((CHIPS, TOK, HEAD), bf16),
            pltpu.SemaphoreType.DMA((8 * (CHIPS // GROUP),)),
        ],
        compiler_params=pltpu.CompilerParams(vmem_limit_bytes=VMEM_LIMIT),
        cost_estimate=cost(4 * PAIR_FLOPS, 0, 17 * MIB),
        name="attn_bwd",
    )(table, x, y, g, prob)


def combine_body(own_ref, got_ref, o_ref):
    o_ref[...] = (own_ref[...].astype(f32) + got_ref[...].astype(f32)).astype(bf16)


def combine(own, got):
    n = 8
    rows = pl.BlockSpec((n, 2 * TOK, HEAD), lambda i: (i, 0, 0))
    return pl.pallas_call(
        combine_body,
        out_shape=jax.ShapeDtypeStruct((CHIPS, 2 * TOK, HEAD), bf16),
        grid=(CHIPS // n,),
        in_specs=[rows, rows],
        out_specs=rows,
        compiler_params=pltpu.CompilerParams(vmem_limit_bytes=VMEM_LIMIT),
        cost_estimate=cost(CHIPS * 2 * TOK * HEAD, 0, 6 * MIB),
        name="combine",
    )(own, got)


def weight_body(place, oa_ref, ob_ref, ca_ref, cb_ref, *rest):
    outs, buf, sems = rest[: 2 * DOCS], rest[2 * DOCS], rest[2 * DOCS + 1]
    copies = []
    for d in (3, 1, 2, 0):
        heads = pl.ds(((place[1] + d) % DOCS) * (HEADS // DOCS), HEADS // DOCS)
        a = oa_ref[heads].reshape(2 * CHUNK, TOK)
        b = ob_ref[heads].reshape(2 * CHUNK, TOK)
        buf[d] = (dot(a, ca_ref[...], 1, 0) + dot(b, cb_ref[...], 1, 0)).astype(bf16)
        for half in range(2):
            j = 2 * d + half
            copies.append(
                pltpu.make_async_copy(
                    buf.at[d, pl.ds(half * CHUNK, CHUNK), :], outs[j], sems.at[j]
                )
            )
            copies[-1].start()
    for copy in copies:
        copy.wait()


def weight_partial(place, out, ca, cb):
    own = pl.BlockSpec((HEADS, 1, HEAD // 2, TOK), lambda i, place: (0, place[0], 0, 0))
    other = pl.BlockSpec((HEADS, 1, HEAD // 2, TOK), lambda i, place: (0, 1 - place[0], 0, 0))
    whole = pl.BlockSpec((TOK, D), lambda i, place: (0, 0))
    outs = pl.pallas_call(
        weight_body,
        out_shape=(jax.ShapeDtypeStruct((CHUNK, D), bf16),) * (2 * DOCS),
        grid_spec=pltpu.PrefetchScalarGridSpec(
            num_scalar_prefetch=1,
            grid=(1,),
            in_specs=[own, other, whole, whole],
            out_specs=[pl.BlockSpec(memory_space=pl.ANY)] * (2 * DOCS),
            scratch_shapes=[
                pltpu.VMEM((DOCS, 2 * CHUNK, D), bf16),
                pltpu.SemaphoreType.DMA((2 * DOCS,)),
            ],
        ),
        compiler_params=pltpu.CompilerParams(vmem_limit_bytes=VMEM_LIMIT),
        cost_estimate=cost(2 * TOK * D * D, 0, 8 * MIB),
        name="weight_partial",
    )(place, out, out, ca, cb)
    return outs[0::2], outs[1::2]


def plus(a, b):
    return (a.astype(f32) + b.astype(f32)).astype(bf16)


def sum_over_docs(up, down, first):
    route_up = [(i, (i + 1) % DOCS) for i in range(DOCS)]
    route_down = [(i, (i - 1) % DOCS) for i in range(DOCS)]
    a, b = up[3], down[1]
    for step in range(1, DOCS):
        a = lax.ppermute(a, "dp", route_up)
        b = lax.ppermute(b, "dp", route_down)
        if step == 1:
            a, b, first = after(a, b, first)
        if step < DOCS - 1:
            a = plus(a, up[3 - step])
            b = plus(b, down[1 + step])
    return (a, up[0], b, down[0]), first


def join(a, own_a, b, own_b):
    n = CHIPS // 2
    parts = (plus(a, own_a), plus(b, own_b))
    return jnp.concatenate([part.reshape(n, 16, D) for part in parts], axis=0)


def block_table(rider, core):
    offsets = rider.reshape(CHIPS, 2, SLOTS).astype(jnp.int32)
    c = jnp.arange(CHIPS, dtype=jnp.int32)[:, None, None]
    i = jnp.arange(2, dtype=jnp.int32)[None, :, None]
    target = 4 * c + 2 * core + i - offsets
    side = ((target >> 1) & 1) ^ core
    place = ((side * CHIPS + (target >> 2)) << 1) + (target & 1)
    return jnp.where(target >= 0, place, -1).reshape(2 * CHIPS, SLOTS)


def local(queries, key_states, value_states, out_weight, cotangent, block_offsets):
    core = lax.axis_index("seq") % 2
    cot = cotangent[0]
    cot_other = lax.ppermute(cot, "seq", CORE_SWAP)
    x = exchange(pack(block_offsets[0], key_states[0], value_states[0], queries[0]))
    x, g, cot_other = after(x, grad_attn_by_head(cot, out_weight), cot_other)
    y = lax.ppermute(x, "seq", CORE_SWAP)
    g = exchange(g)
    table = block_table(x[:, RIDER, 0 : 2 * SLOTS], core)
    table, place = after(table, jnp.stack([core, lax.axis_index("dp")]))
    out, prob = attention_forward(table, x, y)
    g, out = after(g, out)
    out_home = lax.all_to_all(out, "seq", 0, 0, tiled=True)
    own, other, gq = attention_backward(table, x, y, g, prob)
    out_home, own, other, gq = after(out_home, own, other, gq)
    gq_home = exchange(gq)
    got = lax.ppermute(other, "seq", CORE_SWAP)
    got, out_home = after(got, out_home)
    by_core = out_home.reshape(HEADS, 2, HEAD // 2, TOK)
    up, down = weight_partial(place, by_core, cot, cot_other)
    *up, got = after(*up, got)
    gq_home, gathered = after(gq_home, combine(own, got))
    sums, gq_home = sum_over_docs(up, down, gq_home)
    kv_home = exchange(gathered)
    kv_home, *sums = after(kv_home, *sums)
    weight_grad = jnp.sum(exchange(join(*sums)).astype(f32), axis=0)
    (gq,) = unpack(gq_home, 1)
    gk, gv = unpack(kv_home, 2)
    return gq[None], gk[None], gv[None], weight_grad


def solution(mesh):
    in_specs = (
        P("dp", "seq", None),
        P("dp", "seq", None),
        P("dp", "seq", None),
        P(),
        P("dp", "seq", None),
        P("dp", "seq", None),
    )
    out_specs = (
        P("dp", "seq", None),
        P("dp", "seq", None),
        P("dp", "seq", None),
        P(("dp", "seq"), None),
    )
    return jax.shard_map(local, mesh=mesh, in_specs=in_specs, out_specs=out_specs, check_vma=False)
```

```python
import math

import jax
import jax.numpy as jnp
from jax import lax
from jax.experimental import pallas as pl
from jax.experimental.pallas import tpu as pltpu
from jax.sharding import PartitionSpec as P

HEADS = 16
HEAD = 128
BLK = 128
SLOTS = 4
D = HEADS * HEAD
TOK = 256
CHIPS = 16
BLOCKS = 64
WIDTH = (1 + SLOTS) * BLK
DOCS = 4
CHUNK = D // 4 // DOCS
RIDER = 3 * TOK
ROWS = 3 * TOK + 8
SCALE = HEAD ** (-0.5)
SCALE2 = SCALE * math.log2(math.e)
NEG = -1e30
bf16 = jnp.bfloat16
f32 = jnp.float32

SAME_CORE = [[2 * c + k for c in range(CHIPS)] for k in range(2)]
CORE_SWAP = [(i, i ^ 1) for i in range(2 * CHIPS)]

UNROLL = 4
GROUP = 4
PACK = 8
VMEM_LIMIT = 56 * 1024 * 1024


def dot(a, b, ca, cb):
    return lax.dot_general(a, b, (((ca,), (cb,)), ((), ())), preferred_element_type=f32)


def cost(flops, transcendentals=0, bytes_accessed=0):
    return pl.CostEstimate(
        flops=flops, transcendentals=transcendentals, bytes_accessed=bytes_accessed
    )


PAIRS = BLOCKS // 2 * BLK * (1 + SLOTS) * BLK
PAIR_FLOPS = 2 * HEAD * PAIRS
MIB = 1024 * 1024


def exchange(x):
    return lax.all_to_all(x, "seq", 0, 0, axis_index_groups=SAME_CORE, tiled=True)


def after(*values):
    return lax.optimization_barrier(values)


def pack_body(offs, k_ref, v_ref, q_ref, x_ref):
    lane = lax.broadcasted_iota(jnp.int32, (8, 128), 1)
    val = jnp.zeros((8, 128), jnp.int32)
    for j in range(2 * SLOTS):
        val = jnp.where(lane == j, offs[j // SLOTS, j % SLOTS], val)
    rider = val.astype(f32).astype(bf16)
    for h in range(PACK):
        for t, ref in enumerate((k_ref, v_ref, q_ref)):
            x_ref[h, t * TOK : (t + 1) * TOK, :] = ref[:, h * HEAD : (h + 1) * HEAD]
        x_ref[h, RIDER : RIDER + 8, :] = rider


def pack(offs, k, v, q):
    rows = pl.BlockSpec((TOK, PACK * HEAD), lambda i: (0, i))
    return pl.pallas_call(
        pack_body,
        out_shape=jax.ShapeDtypeStruct((HEADS, ROWS, HEAD), bf16),
        grid=(HEADS // PACK,),
        in_specs=[pl.BlockSpec(memory_space=pltpu.SMEM), rows, rows, rows],
        out_specs=pl.BlockSpec((PACK, ROWS, HEAD), lambda i: (i, 0, 0)),
        compiler_params=pltpu.CompilerParams(vmem_limit_bytes=VMEM_LIMIT),
        name="pack",
    )(offs, k, v, q)


def unpack_body(r_ref, *refs):
    for h in range(PACK):
        for t, ref in enumerate(refs):
            ref[:, h * HEAD : (h + 1) * HEAD] = r_ref[h, t * TOK : (t + 1) * TOK, :]


def unpack(r, n):
    out = jax.ShapeDtypeStruct((TOK, D), bf16)
    rows = pl.BlockSpec((TOK, PACK * HEAD), lambda i: (0, i))
    return pl.pallas_call(
        unpack_body,
        out_shape=(out,) * n,
        grid=(HEADS // PACK,),
        in_specs=[pl.BlockSpec((PACK, n * TOK, HEAD), lambda i: (i, 0, 0))],
        out_specs=[rows] * n,
        compiler_params=pltpu.CompilerParams(vmem_limit_bytes=VMEM_LIMIT),
        cost_estimate=cost(0, 0, 2 * n * MIB),
        name="unpack",
    )(r)


def grad_attn_body(c_ref, w_ref, o_ref):
    g = dot(c_ref[...], w_ref[...], 1, 1).astype(bf16)
    for j in range(2):
        o_ref[j] = g[:, j * HEAD : (j + 1) * HEAD]


def grad_attn_by_head(cot, weight):
    return pl.pallas_call(
        grad_attn_body,
        out_shape=jax.ShapeDtypeStruct((HEADS, TOK, HEAD), bf16),
        grid=(HEADS // 2,),
        in_specs=[
            pl.BlockSpec((TOK, D), lambda i: (0, 0)),
            pl.BlockSpec((2 * HEAD, D), lambda i: (i, 0)),
        ],
        out_specs=pl.BlockSpec((2, TOK, HEAD), lambda i: (i, 0, 0)),
        compiler_params=pltpu.CompilerParams(vmem_limit_bytes=VMEM_LIMIT),
        cost_estimate=cost(2 * TOK * D * D, 0, 10 * MIB),
        name="grad_attn",
    )(cot, weight)


def load_pool(x_ref, y_ref, kv, qs, sems):
    groups = []
    for j in range(CHIPS // GROUP):
        at = pl.ds(j * GROUP, GROUP)
        groups.append(
            [
                pltpu.make_async_copy(
                    x_ref.at[at, pl.ds(0, 2 * TOK), :], kv.at[at], sems.at[3 * j]
                ),
                pltpu.make_async_copy(
                    y_ref.at[at],
                    kv.at[pl.ds(CHIPS + j * GROUP, GROUP)],
                    sems.at[3 * j + 1],
                ),
                pltpu.make_async_copy(
                    x_ref.at[at, pl.ds(2 * TOK, TOK), :], qs.at[at], sems.at[3 * j + 2]
                ),
            ]
        )
    return groups


def listed(table, c, i):
    places = [(c, i * BLK, None)]
    for s in range(SLOTS):
        code = table[2 * c + i, s]
        f = jnp.maximum(code, 0)
        bias = jnp.where(code >= 0, 0.0, -NEG).astype(f32)
        places.append((f // 2, pl.multiple_of((f % 2) * BLK, BLK), bias))
    return places


def causal():
    u = lax.broadcasted_iota(jnp.int32, (BLK, BLK), 0)
    t = lax.broadcasted_iota(jnp.int32, (BLK, BLK), 1)
    return u <= t


def forward_body(table, x_ref, y_ref, o_ref, p_ref, kv, qs, ps, sems):
    groups = load_pool(x_ref, y_ref, kv, qs, sems)
    for copies in groups:
        for copy in copies:
            copy.start()

    def block(c, i):
        places = listed(table, c, i)
        q = qs[c, pl.ds(i * BLK, BLK), :]
        keys = jnp.concatenate([kv[p, pl.ds(r, BLK), :] for p, r, _ in places], axis=0)
        every = dot(keys, q, 1, 1)
        raw = [every[s * BLK : (s + 1) * BLK, :] for s in range(1 + SLOTS)]
        raw[0] = jnp.where(causal(), raw[0], NEG)
        peak = jnp.max(raw[0], axis=0, keepdims=True)
        for (_, _, bias), s in zip(places[1:], raw[1:]):
            peak = jnp.maximum(peak, jnp.max(s, axis=0, keepdims=True) - bias)
        peak = peak * SCALE2
        weights = []
        total = None
        for (_, _, bias), s in zip(places, raw):
            w = jnp.exp2(s * SCALE2 - (peak if bias is None else peak + bias))
            part = jnp.sum(w, axis=0, keepdims=True)
            total = part if total is None else total + part
            weights.append(w)
        inverse = 1.0 / total
        prob = jnp.concatenate([(w * inverse).astype(bf16) for w in weights], axis=0)
        ps[2 * c + i] = prob
        values = jnp.concatenate([kv[p, pl.ds(TOK + r, BLK), :] for p, r, _ in places], axis=0)
        return dot(values, prob, 0, 0).astype(bf16)

    def step(c, carry):
        for i in range(2):
            out = block(c, i)
            for g in range(8):
                row = (g // 2) * 16
                o_ref[2 * c + g % 2, row : row + 16, i * BLK : (i + 1) * BLK] = out[
                    g * 16 : g * 16 + 16, :
                ]
        return carry

    sends = []
    for j, copies in enumerate(groups):
        for copy in copies:
            copy.wait()
        lax.fori_loop(j * GROUP, (j + 1) * GROUP, step, 0, unroll=UNROLL)
        at = pl.ds(2 * j * GROUP, 2 * GROUP)
        sends.append(pltpu.make_async_copy(ps.at[at], p_ref.at[at], sems.at[3 * len(groups) + j]))
        sends[j].start()
    for copy in sends:
        copy.wait()


def attention_forward(table, x, y):
    return pl.pallas_call(
        forward_body,
        out_shape=(
            jax.ShapeDtypeStruct((2 * CHIPS, HEAD // 2, TOK), bf16),
            jax.ShapeDtypeStruct((2 * CHIPS, WIDTH, BLK), bf16),
        ),
        in_specs=[pl.BlockSpec(memory_space=pltpu.SMEM)] + [pl.BlockSpec(memory_space=pl.ANY)] * 2,
        out_specs=[pl.BlockSpec(memory_space=pltpu.VMEM), pl.BlockSpec(memory_space=pl.ANY)],
        scratch_shapes=[
            pltpu.VMEM((2 * CHIPS, 2 * TOK, HEAD), bf16),
            pltpu.VMEM((CHIPS, TOK, HEAD), bf16),
            pltpu.VMEM((2 * CHIPS, WIDTH, BLK), bf16),
            pltpu.SemaphoreType.DMA((4 * (CHIPS // GROUP),)),
        ],
        compiler_params=pltpu.CompilerParams(vmem_limit_bytes=VMEM_LIMIT),
        cost_estimate=cost(2 * PAIR_FLOPS, PAIRS, 12 * MIB),
        name="attn_fwd",
    )(table, x, y)


def backward_body(
    table, x_ref, y_ref, g_ref, p_ref, own_ref, other_ref, gq_ref, kv, qs, gs, ps, acck, accv, own, other, gq, sems
):
    groups = load_pool(x_ref, y_ref, kv, qs, sems)
    sends = []
    n = CHIPS // GROUP
    for j in range(n):
        at = pl.ds(j * GROUP, GROUP)
        groups[j].append(pltpu.make_async_copy(g_ref.at[at], gs.at[at], sems.at[3 * n + j]))
        two = pl.ds(2 * j * GROUP, 2 * GROUP)
        groups[j].append(pltpu.make_async_copy(p_ref.at[two], ps.at[two], sems.at[7 * n + j]))
        sends.append(
            [
                pltpu.make_async_copy(
                    gq.at[at], gq_ref.at[at], sems.at[4 * n + j]
                ),
                pltpu.make_async_copy(
                    own.at[at], own_ref.at[at], sems.at[5 * n + j]
                ),
                pltpu.make_async_copy(other.at[at], other_ref.at[at], sems.at[6 * n + j]),
            ]
        )
    for copies in groups:
        for copy in copies:
            copy.start()

    def clear(j, carry):
        acck[CHIPS + j] = jnp.zeros((TOK, HEAD), f32)
        accv[CHIPS + j] = jnp.zeros((TOK, HEAD), f32)
        return carry

    lax.fori_loop(0, CHIPS, clear, 0)

    def block(c, i):
        places = listed(table, c, i)
        q = qs[c, pl.ds(i * BLK, BLK), :]
        g = gs[c, pl.ds(i * BLK, BLK), :]
        keys = jnp.concatenate([kv[p, pl.ds(r, BLK), :] for p, r, _ in places], axis=0)
        values = jnp.concatenate([kv[p, pl.ds(TOK + r, BLK), :] for p, r, _ in places], axis=0)
        grads = dot(values, g, 1, 1)
        low = ps[2 * c + i]
        prob = low.astype(f32)
        row_dot = jnp.sum(prob * grads, axis=0, keepdims=True)
        score = (prob * (grads - row_dot)).astype(bf16)
        gk = dot(score, q, 1, 0)
        gv = dot(low, g, 1, 0)
        for j, (p, r, _) in enumerate(places):
            at = pl.ds(r, BLK)
            if j == 0:
                acck[p, at, :] = gk[0:BLK, :]
                accv[p, at, :] = gv[0:BLK, :]
            else:
                acck[p, at, :] += gk[j * BLK : (j + 1) * BLK, :]
                accv[p, at, :] += gv[j * BLK : (j + 1) * BLK, :]
        gq[c, pl.ds(i * BLK, BLK), :] = (dot(score, keys, 0, 0) * SCALE).astype(bf16)

    def step(c, carry):
        for i in range(2):
            block(c, i)
        return carry

    def flush(j, carry):
        own[j, 0:TOK, :] = (acck[j] * SCALE).astype(bf16)
        own[j, TOK : 2 * TOK, :] = accv[j].astype(bf16)
        other[j, 0:TOK, :] = (acck[CHIPS + j] * SCALE).astype(bf16)
        other[j, TOK : 2 * TOK, :] = accv[CHIPS + j].astype(bf16)
        return carry

    for j in range(n + 2):
        if j < n:
            for copy in groups[j]:
                copy.wait()
            lax.fori_loop(j * GROUP, (j + 1) * GROUP, step, 0, unroll=UNROLL)
            sends[j][0].start()
        if j >= 2:
            lax.fori_loop((j - 2) * GROUP, (j - 1) * GROUP, flush, 0)
            sends[j - 2][1].start()
            sends[j - 2][2].start()
    for copies in sends:
        for copy in copies:
            copy.wait()


def attention_backward(table, x, y, g, prob):
    return pl.pallas_call(
        backward_body,
        out_shape=(
            jax.ShapeDtypeStruct((CHIPS, 2 * TOK, HEAD), bf16),
            jax.ShapeDtypeStruct((CHIPS, 2 * TOK, HEAD), bf16),
            jax.ShapeDtypeStruct((CHIPS, TOK, HEAD), bf16),
        ),
        in_specs=[pl.BlockSpec(memory_space=pltpu.SMEM)]
        + [pl.BlockSpec(memory_space=pl.ANY)] * 4,
        out_specs=[pl.BlockSpec(memory_space=pl.ANY)] * 3,
        scratch_shapes=[
            pltpu.VMEM((2 * CHIPS, 2 * TOK, HEAD), bf16),
            pltpu.VMEM((CHIPS, TOK, HEAD), bf16),
            pltpu.VMEM((CHIPS, TOK, HEAD), bf16),
            pltpu.VMEM((2 * CHIPS, WIDTH, BLK), bf16),
            pltpu.VMEM((2 * CHIPS, TOK, HEAD), f32),
            pltpu.VMEM((2 * CHIPS, TOK, HEAD), f32),
            pltpu.VMEM((CHIPS, 2 * TOK, HEAD), bf16),
            pltpu.VMEM((CHIPS, 2 * TOK, HEAD), bf16),
            pltpu.VMEM((CHIPS, TOK, HEAD), bf16),
            pltpu.SemaphoreType.DMA((8 * (CHIPS // GROUP),)),
        ],
        compiler_params=pltpu.CompilerParams(vmem_limit_bytes=VMEM_LIMIT),
        cost_estimate=cost(4 * PAIR_FLOPS, 0, 17 * MIB),
        name="attn_bwd",
    )(table, x, y, g, prob)


def combine_body(own_ref, got_ref, o_ref):
    o_ref[...] = (own_ref[...].astype(f32) + got_ref[...].astype(f32)).astype(bf16)


def combine(own, got):
    n = 8
    rows = pl.BlockSpec((n, 2 * TOK, HEAD), lambda i: (i, 0, 0))
    return pl.pallas_call(
        combine_body,
        out_shape=jax.ShapeDtypeStruct((CHIPS, 2 * TOK, HEAD), bf16),
        grid=(CHIPS // n,),
        in_specs=[rows, rows],
        out_specs=rows,
        compiler_params=pltpu.CompilerParams(vmem_limit_bytes=VMEM_LIMIT),
        cost_estimate=cost(CHIPS * 2 * TOK * HEAD, 0, 6 * MIB),
        name="combine",
    )(own, got)


def weight_body(place, oa_ref, ob_ref, ca_ref, cb_ref, *rest):
    outs, buf, sems = rest[: 2 * DOCS], rest[2 * DOCS], rest[2 * DOCS + 1]
    copies = []
    for d in (3, 1, 2, 0):
        heads = pl.ds(((place[1] + d) % DOCS) * (HEADS // DOCS), HEADS // DOCS)
        a = oa_ref[heads].reshape(2 * CHUNK, TOK)
        b = ob_ref[heads].reshape(2 * CHUNK, TOK)
        buf[d] = (dot(a, ca_ref[...], 1, 0) + dot(b, cb_ref[...], 1, 0)).astype(bf16)
        for half in range(2):
            j = 2 * d + half
            copies.append(
                pltpu.make_async_copy(
                    buf.at[d, pl.ds(half * CHUNK, CHUNK), :], outs[j], sems.at[j]
                )
            )
            copies[-1].start()
    for copy in copies:
        copy.wait()


def weight_partial(place, out, ca, cb):
    own = pl.BlockSpec((HEADS, 1, HEAD // 2, TOK), lambda i, place: (0, place[0], 0, 0))
    other = pl.BlockSpec((HEADS, 1, HEAD // 2, TOK), lambda i, place: (0, 1 - place[0], 0, 0))
    whole = pl.BlockSpec((TOK, D), lambda i, place: (0, 0))
    outs = pl.pallas_call(
        weight_body,
        out_shape=(jax.ShapeDtypeStruct((CHUNK, D), bf16),) * (2 * DOCS),
        grid_spec=pltpu.PrefetchScalarGridSpec(
            num_scalar_prefetch=1,
            grid=(1,),
            in_specs=[own, other, whole, whole],
            out_specs=[pl.BlockSpec(memory_space=pl.ANY)] * (2 * DOCS),
            scratch_shapes=[
                pltpu.VMEM((DOCS, 2 * CHUNK, D), bf16),
                pltpu.SemaphoreType.DMA((2 * DOCS,)),
            ],
        ),
        compiler_params=pltpu.CompilerParams(vmem_limit_bytes=VMEM_LIMIT),
        cost_estimate=cost(2 * TOK * D * D, 0, 8 * MIB),
        name="weight_partial",
    )(place, out, out, ca, cb)
    return outs[0::2], outs[1::2]


def plus(a, b):
    return (a.astype(f32) + b.astype(f32)).astype(bf16)


def sum_over_docs(up, down, first):
    route_up = [(i, (i + 1) % DOCS) for i in range(DOCS)]
    route_down = [(i, (i - 1) % DOCS) for i in range(DOCS)]
    a, b = up[3], down[1]
    for step in range(1, DOCS):
        a = lax.ppermute(a, "dp", route_up)
        b = lax.ppermute(b, "dp", route_down)
        if step == 1:
            a, b, first = after(a, b, first)
        if step < DOCS - 1:
            a = plus(a, up[3 - step])
            b = plus(b, down[1 + step])
    return (a, up[0], b, down[0]), first


def join_body(a_ref, own_a_ref, b_ref, own_b_ref, o_ref):
    n = CHIPS // 2
    o_ref[0:n] = plus(a_ref[...], own_a_ref[...]).reshape(n, 16, D)
    o_ref[n : 2 * n] = plus(b_ref[...], own_b_ref[...]).reshape(n, 16, D)


def join(*parts):
    return pl.pallas_call(
        join_body,
        out_shape=jax.ShapeDtypeStruct((CHIPS, 16, D), bf16),
        in_specs=[pl.BlockSpec(memory_space=pltpu.VMEM)] * 4,
        out_specs=pl.BlockSpec(memory_space=pltpu.VMEM),
        compiler_params=pltpu.CompilerParams(vmem_limit_bytes=VMEM_LIMIT),
        name="join",
    )(*parts)


def block_table(rider, core):
    offsets = rider.reshape(CHIPS, 2, SLOTS).astype(jnp.int32)
    c = jnp.arange(CHIPS, dtype=jnp.int32)[:, None, None]
    i = jnp.arange(2, dtype=jnp.int32)[None, :, None]
    target = 4 * c + 2 * core + i - offsets
    side = ((target >> 1) & 1) ^ core
    place = ((side * CHIPS + (target >> 2)) << 1) + (target & 1)
    return jnp.where(target >= 0, place, -1).reshape(2 * CHIPS, SLOTS)


def local(queries, key_states, value_states, out_weight, cotangent, block_offsets):
    core = lax.axis_index("seq") % 2
    cot = cotangent[0]
    cot_other = lax.ppermute(cot, "seq", CORE_SWAP)
    x = exchange(pack(block_offsets[0], key_states[0], value_states[0], queries[0]))
    x, g, cot_other = after(x, grad_attn_by_head(cot, out_weight), cot_other)
    y = lax.ppermute(x[:, 0 : 2 * TOK], "seq", CORE_SWAP)
    g = exchange(g)
    table = block_table(x[:, RIDER, 0 : 2 * SLOTS], core)
    table, place = after(table, jnp.stack([core, lax.axis_index("dp")]))
    out, prob = attention_forward(table, x, y)
    g, out = after(g, out)
    out_home = lax.all_to_all(out, "seq", 0, 0, tiled=True)
    own, other, gq = attention_backward(table, x, y, g, prob)
    out_home, own, other, gq = after(out_home, own, other, gq)
    gq_home = exchange(gq)
    got = lax.ppermute(other, "seq", CORE_SWAP)
    got, out_home = after(got, out_home)
    by_core = out_home.reshape(HEADS, 2, HEAD // 2, TOK)
    up, down = weight_partial(place, by_core, cot, cot_other)
    *up, got = after(*up, got)
    gq_home, gathered = after(gq_home, combine(own, got))
    sums, gq_home = sum_over_docs(up, down, gq_home)
    kv_home = exchange(gathered)
    kv_home, joined = after(kv_home, join(*sums))
    weight_grad = jnp.sum(exchange(joined).astype(f32), axis=0)
    (gq,) = unpack(gq_home, 1)
    gk, gv = unpack(kv_home, 2)
    return gq[None], gk[None], gv[None], weight_grad


def solution(mesh):
    in_specs = (
        P("dp", "seq", None),
        P("dp", "seq", None),
        P("dp", "seq", None),
        P(),
        P("dp", "seq", None),
        P("dp", "seq", None),
    )
    out_specs = (
        P("dp", "seq", None),
        P("dp", "seq", None),
        P("dp", "seq", None),
        P(("dp", "seq"), None),
    )
    return jax.shard_map(local, mesh=mesh, in_specs=in_specs, out_specs=out_specs, check_vma=False)
```

```python
import math

import jax
import jax.numpy as jnp
from jax import lax
from jax.experimental import pallas as pl
from jax.experimental.pallas import tpu as pltpu
from jax.sharding import PartitionSpec as P

HEADS = 16
HEAD = 128
BLK = 128
SLOTS = 4
D = HEADS * HEAD
TOK = 256
CHIPS = 16
BLOCKS = 64
WIDTH = (1 + SLOTS) * BLK
DOCS = 4
CHUNK = D // 4 // DOCS
RIDER = 3 * TOK
ROWS = 3 * TOK + 8
SCALE = HEAD ** (-0.5)
SCALE2 = SCALE * math.log2(math.e)
NEG = -1e30
bf16 = jnp.bfloat16
f32 = jnp.float32

SAME_CORE = [[2 * c + k for c in range(CHIPS)] for k in range(2)]
CORE_SWAP = [(i, i ^ 1) for i in range(2 * CHIPS)]

UNROLL = 4
GROUP = 4
PACK = 8
VMEM_LIMIT = 56 * 1024 * 1024


def dot(a, b, ca, cb):
    return lax.dot_general(a, b, (((ca,), (cb,)), ((), ())), preferred_element_type=f32)


def cost(flops, transcendentals=0, bytes_accessed=0):
    return pl.CostEstimate(
        flops=flops, transcendentals=transcendentals, bytes_accessed=bytes_accessed
    )


PAIRS = BLOCKS // 2 * BLK * (1 + SLOTS) * BLK
PAIR_FLOPS = 2 * HEAD * PAIRS
MIB = 1024 * 1024


def exchange(x):
    return lax.all_to_all(x, "seq", 0, 0, axis_index_groups=SAME_CORE, tiled=True)


def after(*values):
    return lax.optimization_barrier(values)


def pack_body(offs, k_ref, v_ref, q_ref, x_ref):
    lane = lax.broadcasted_iota(jnp.int32, (8, 128), 1)
    val = jnp.zeros((8, 128), jnp.int32)
    for j in range(2 * SLOTS):
        val = jnp.where(lane == j, offs[j // SLOTS, j % SLOTS], val)
    rider = val.astype(f32).astype(bf16)
    for h in range(PACK):
        for t, ref in enumerate((k_ref, v_ref, q_ref)):
            x_ref[h, t * TOK : (t + 1) * TOK, :] = ref[:, h * HEAD : (h + 1) * HEAD]
        x_ref[h, RIDER : RIDER + 8, :] = rider


def pack(offs, k, v, q):
    rows = pl.BlockSpec((TOK, PACK * HEAD), lambda i: (0, i))
    return pl.pallas_call(
        pack_body,
        out_shape=jax.ShapeDtypeStruct((HEADS, ROWS, HEAD), bf16),
        grid=(HEADS // PACK,),
        in_specs=[pl.BlockSpec(memory_space=pltpu.SMEM), rows, rows, rows],
        out_specs=pl.BlockSpec((PACK, ROWS, HEAD), lambda i: (i, 0, 0)),
        compiler_params=pltpu.CompilerParams(vmem_limit_bytes=VMEM_LIMIT),
        name="pack",
    )(offs, k, v, q)


def unpack_body(r_ref, *refs):
    for h in range(PACK):
        for t, ref in enumerate(refs):
            ref[:, h * HEAD : (h + 1) * HEAD] = r_ref[h, t * TOK : (t + 1) * TOK, :]


def unpack(r, n):
    out = jax.ShapeDtypeStruct((TOK, D), bf16)
    rows = pl.BlockSpec((TOK, PACK * HEAD), lambda i: (0, i))
    return pl.pallas_call(
        unpack_body,
        out_shape=(out,) * n,
        grid=(HEADS // PACK,),
        in_specs=[pl.BlockSpec((PACK, n * TOK, HEAD), lambda i: (i, 0, 0))],
        out_specs=[rows] * n,
        compiler_params=pltpu.CompilerParams(vmem_limit_bytes=VMEM_LIMIT),
        cost_estimate=cost(0, 0, 2 * n * MIB),
        name="unpack",
    )(r)


def grad_attn_body(c_ref, w_ref, o_ref):
    g = dot(c_ref[...], w_ref[...], 1, 1).astype(bf16)
    for j in range(2):
        o_ref[j] = g[:, j * HEAD : (j + 1) * HEAD]


def grad_attn_by_head(cot, weight):
    return pl.pallas_call(
        grad_attn_body,
        out_shape=jax.ShapeDtypeStruct((HEADS, TOK, HEAD), bf16),
        grid=(HEADS // 2,),
        in_specs=[
            pl.BlockSpec((TOK, D), lambda i: (0, 0)),
            pl.BlockSpec((2 * HEAD, D), lambda i: (i, 0)),
        ],
        out_specs=pl.BlockSpec((2, TOK, HEAD), lambda i: (i, 0, 0)),
        compiler_params=pltpu.CompilerParams(vmem_limit_bytes=VMEM_LIMIT),
        cost_estimate=cost(2 * TOK * D * D, 0, 10 * MIB),
        name="grad_attn",
    )(cot, weight)


def load_pool(x_ref, y_ref, kv, qs, sems):
    groups = []
    for j in range(CHIPS // GROUP):
        at = pl.ds(j * GROUP, GROUP)
        groups.append(
            [
                pltpu.make_async_copy(
                    x_ref.at[at, pl.ds(0, 2 * TOK), :], kv.at[at], sems.at[3 * j]
                ),
                pltpu.make_async_copy(
                    y_ref.at[at, pl.ds(0, 2 * TOK), :],
                    kv.at[pl.ds(CHIPS + j * GROUP, GROUP)],
                    sems.at[3 * j + 1],
                ),
                pltpu.make_async_copy(
                    x_ref.at[at, pl.ds(2 * TOK, TOK), :], qs.at[at], sems.at[3 * j + 2]
                ),
            ]
        )
    return groups


def listed(table, c, i):
    places = [(c, i * BLK, None)]
    for s in range(SLOTS):
        code = table[2 * c + i, s]
        f = jnp.maximum(code, 0)
        bias = jnp.where(code >= 0, 0.0, -NEG).astype(f32)
        places.append((f // 2, pl.multiple_of((f % 2) * BLK, BLK), bias))
    return places


def causal():
    u = lax.broadcasted_iota(jnp.int32, (BLK, BLK), 0)
    t = lax.broadcasted_iota(jnp.int32, (BLK, BLK), 1)
    return u <= t


def forward_body(table, x_ref, y_ref, o_ref, p_ref, kv, qs, ps, sems):
    groups = load_pool(x_ref, y_ref, kv, qs, sems)
    for copies in groups:
        for copy in copies:
            copy.start()

    def block(c, i):
        places = listed(table, c, i)
        q = qs[c, pl.ds(i * BLK, BLK), :]
        keys = jnp.concatenate([kv[p, pl.ds(r, BLK), :] for p, r, _ in places], axis=0)
        every = dot(keys, q, 1, 1)
        raw = [every[s * BLK : (s + 1) * BLK, :] for s in range(1 + SLOTS)]
        raw[0] = jnp.where(causal(), raw[0], NEG)
        peak = jnp.max(raw[0], axis=0, keepdims=True)
        for (_, _, bias), s in zip(places[1:], raw[1:]):
            peak = jnp.maximum(peak, jnp.max(s, axis=0, keepdims=True) - bias)
        peak = peak * SCALE2
        weights = []
        total = None
        for (_, _, bias), s in zip(places, raw):
            w = jnp.exp2(s * SCALE2 - (peak if bias is None else peak + bias))
            part = jnp.sum(w, axis=0, keepdims=True)
            total = part if total is None else total + part
            weights.append(w)
        inverse = 1.0 / total
        prob = jnp.concatenate([(w * inverse).astype(bf16) for w in weights], axis=0)
        ps[2 * c + i] = prob
        values = jnp.concatenate([kv[p, pl.ds(TOK + r, BLK), :] for p, r, _ in places], axis=0)
        return dot(values, prob, 0, 0).astype(bf16)

    def step(c, carry):
        for i in range(2):
            out = block(c, i)
            for g in range(8):
                row = (g // 2) * 16
                o_ref[2 * c + g % 2, row : row + 16, i * BLK : (i + 1) * BLK] = out[
                    g * 16 : g * 16 + 16, :
                ]
        return carry

    sends = []
    for j, copies in enumerate(groups):
        for copy in copies:
            copy.wait()
        lax.fori_loop(j * GROUP, (j + 1) * GROUP, step, 0, unroll=UNROLL)
        at = pl.ds(2 * j * GROUP, 2 * GROUP)
        sends.append(pltpu.make_async_copy(ps.at[at], p_ref.at[at], sems.at[3 * len(groups) + j]))
        sends[j].start()
    for copy in sends:
        copy.wait()


def attention_forward(table, x, y):
    return pl.pallas_call(
        forward_body,
        out_shape=(
            jax.ShapeDtypeStruct((2 * CHIPS, HEAD // 2, TOK), bf16),
            jax.ShapeDtypeStruct((2 * CHIPS, WIDTH, BLK), bf16),
        ),
        in_specs=[pl.BlockSpec(memory_space=pltpu.SMEM)] + [pl.BlockSpec(memory_space=pl.ANY)] * 2,
        out_specs=[pl.BlockSpec(memory_space=pltpu.VMEM), pl.BlockSpec(memory_space=pl.ANY)],
        scratch_shapes=[
            pltpu.VMEM((2 * CHIPS, 2 * TOK, HEAD), bf16),
            pltpu.VMEM((CHIPS, TOK, HEAD), bf16),
            pltpu.VMEM((2 * CHIPS, WIDTH, BLK), bf16),
            pltpu.SemaphoreType.DMA((4 * (CHIPS // GROUP),)),
        ],
        compiler_params=pltpu.CompilerParams(vmem_limit_bytes=VMEM_LIMIT),
        cost_estimate=cost(2 * PAIR_FLOPS, PAIRS, 12 * MIB),
        name="attn_fwd",
    )(table, x, y)


def backward_body(
    table, x_ref, y_ref, g_ref, p_ref, own_ref, other_ref, gq_ref, kv, qs, gs, ps, acck, accv, own, other, gq, sems
):
    groups = load_pool(x_ref, y_ref, kv, qs, sems)
    sends = []
    n = CHIPS // GROUP
    for j in range(n):
        at = pl.ds(j * GROUP, GROUP)
        groups[j].append(pltpu.make_async_copy(g_ref.at[at], gs.at[at], sems.at[3 * n + j]))
        two = pl.ds(2 * j * GROUP, 2 * GROUP)
        groups[j].append(pltpu.make_async_copy(p_ref.at[two], ps.at[two], sems.at[7 * n + j]))
        sends.append(
            [
                pltpu.make_async_copy(
                    gq.at[at], gq_ref.at[at], sems.at[4 * n + j]
                ),
                pltpu.make_async_copy(
                    own.at[at], own_ref.at[at], sems.at[5 * n + j]
                ),
                pltpu.make_async_copy(other.at[at], other_ref.at[at], sems.at[6 * n + j]),
            ]
        )
    for copies in groups:
        for copy in copies:
            copy.start()

    def clear(j, carry):
        acck[CHIPS + j] = jnp.zeros((TOK, HEAD), f32)
        accv[CHIPS + j] = jnp.zeros((TOK, HEAD), f32)
        return carry

    lax.fori_loop(0, CHIPS, clear, 0)

    def block(c, i):
        places = listed(table, c, i)
        q = qs[c, pl.ds(i * BLK, BLK), :]
        g = gs[c, pl.ds(i * BLK, BLK), :]
        keys = jnp.concatenate([kv[p, pl.ds(r, BLK), :] for p, r, _ in places], axis=0)
        values = jnp.concatenate([kv[p, pl.ds(TOK + r, BLK), :] for p, r, _ in places], axis=0)
        grads = dot(values, g, 1, 1)
        low = ps[2 * c + i]
        prob = low.astype(f32)
        row_dot = jnp.sum(prob * grads, axis=0, keepdims=True)
        score = (prob * (grads - row_dot)).astype(bf16)
        gk = dot(score, q, 1, 0)
        gv = dot(low, g, 1, 0)
        for j, (p, r, _) in enumerate(places):
            at = pl.ds(r, BLK)
            if j == 0:
                acck[p, at, :] = gk[0:BLK, :]
                accv[p, at, :] = gv[0:BLK, :]
            else:
                acck[p, at, :] += gk[j * BLK : (j + 1) * BLK, :]
                accv[p, at, :] += gv[j * BLK : (j + 1) * BLK, :]
        gq[c, pl.ds(i * BLK, BLK), :] = (dot(score, keys, 0, 0) * SCALE).astype(bf16)

    def step(c, carry):
        for i in range(2):
            block(c, i)
        return carry

    def flush(j, carry):
        own[j, 0:TOK, :] = (acck[j] * SCALE).astype(bf16)
        own[j, TOK : 2 * TOK, :] = accv[j].astype(bf16)
        other[j, 0:TOK, :] = (acck[CHIPS + j] * SCALE).astype(bf16)
        other[j, TOK : 2 * TOK, :] = accv[CHIPS + j].astype(bf16)
        return carry

    for j in range(n + 2):
        if j < n:
            for copy in groups[j]:
                copy.wait()
            lax.fori_loop(j * GROUP, (j + 1) * GROUP, step, 0, unroll=UNROLL)
            sends[j][0].start()
        if j >= 2:
            lax.fori_loop((j - 2) * GROUP, (j - 1) * GROUP, flush, 0)
            sends[j - 2][1].start()
            sends[j - 2][2].start()
    for copies in sends:
        for copy in copies:
            copy.wait()


def attention_backward(table, x, y, g, prob):
    return pl.pallas_call(
        backward_body,
        out_shape=(
            jax.ShapeDtypeStruct((CHIPS, 2 * TOK, HEAD), bf16),
            jax.ShapeDtypeStruct((CHIPS, 2 * TOK, HEAD), bf16),
            jax.ShapeDtypeStruct((CHIPS, TOK, HEAD), bf16),
        ),
        in_specs=[pl.BlockSpec(memory_space=pltpu.SMEM)]
        + [pl.BlockSpec(memory_space=pl.ANY)] * 4,
        out_specs=[pl.BlockSpec(memory_space=pl.ANY)] * 3,
        scratch_shapes=[
            pltpu.VMEM((2 * CHIPS, 2 * TOK, HEAD), bf16),
            pltpu.VMEM((CHIPS, TOK, HEAD), bf16),
            pltpu.VMEM((CHIPS, TOK, HEAD), bf16),
            pltpu.VMEM((2 * CHIPS, WIDTH, BLK), bf16),
            pltpu.VMEM((2 * CHIPS, TOK, HEAD), f32),
            pltpu.VMEM((2 * CHIPS, TOK, HEAD), f32),
            pltpu.VMEM((CHIPS, 2 * TOK, HEAD), bf16),
            pltpu.VMEM((CHIPS, 2 * TOK, HEAD), bf16),
            pltpu.VMEM((CHIPS, TOK, HEAD), bf16),
            pltpu.SemaphoreType.DMA((8 * (CHIPS // GROUP),)),
        ],
        compiler_params=pltpu.CompilerParams(vmem_limit_bytes=VMEM_LIMIT),
        cost_estimate=cost(4 * PAIR_FLOPS, 0, 17 * MIB),
        name="attn_bwd",
    )(table, x, y, g, prob)


def combine_body(own_ref, got_ref, o_ref):
    o_ref[...] = (own_ref[...].astype(f32) + got_ref[...].astype(f32)).astype(bf16)


def combine(own, got):
    n = 8
    rows = pl.BlockSpec((n, 2 * TOK, HEAD), lambda i: (i, 0, 0))
    return pl.pallas_call(
        combine_body,
        out_shape=jax.ShapeDtypeStruct((CHIPS, 2 * TOK, HEAD), bf16),
        grid=(CHIPS // n,),
        in_specs=[rows, rows],
        out_specs=rows,
        compiler_params=pltpu.CompilerParams(vmem_limit_bytes=VMEM_LIMIT),
        cost_estimate=cost(CHIPS * 2 * TOK * HEAD, 0, 6 * MIB),
        name="combine",
    )(own, got)


def weight_body(place, oa_ref, ob_ref, ca_ref, cb_ref, *rest):
    outs, buf, sems = rest[: 2 * DOCS], rest[2 * DOCS], rest[2 * DOCS + 1]
    copies = []
    for d in (3, 1, 2, 0):
        heads = pl.ds(((place[1] + d) % DOCS) * (HEADS // DOCS), HEADS // DOCS)
        a = oa_ref[heads].reshape(2 * CHUNK, TOK)
        b = ob_ref[heads].reshape(2 * CHUNK, TOK)
        buf[d] = (dot(a, ca_ref[...], 1, 0) + dot(b, cb_ref[...], 1, 0)).astype(bf16)
        for half in range(2):
            j = 2 * d + half
            copies.append(
                pltpu.make_async_copy(
                    buf.at[d, pl.ds(half * CHUNK, CHUNK), :], outs[j], sems.at[j]
                )
            )
            copies[-1].start()
    for copy in copies:
        copy.wait()


def weight_partial(place, out, ca, cb):
    own = pl.BlockSpec((HEADS, 1, HEAD // 2, TOK), lambda i, place: (0, place[0], 0, 0))
    other = pl.BlockSpec((HEADS, 1, HEAD // 2, TOK), lambda i, place: (0, 1 - place[0], 0, 0))
    whole = pl.BlockSpec((TOK, D), lambda i, place: (0, 0))
    outs = pl.pallas_call(
        weight_body,
        out_shape=(jax.ShapeDtypeStruct((CHUNK, D), bf16),) * (2 * DOCS),
        grid_spec=pltpu.PrefetchScalarGridSpec(
            num_scalar_prefetch=1,
            grid=(1,),
            in_specs=[own, other, whole, whole],
            out_specs=[pl.BlockSpec(memory_space=pl.ANY)] * (2 * DOCS),
            scratch_shapes=[
                pltpu.VMEM((DOCS, 2 * CHUNK, D), bf16),
                pltpu.SemaphoreType.DMA((2 * DOCS,)),
            ],
        ),
        compiler_params=pltpu.CompilerParams(vmem_limit_bytes=VMEM_LIMIT),
        cost_estimate=cost(2 * TOK * D * D, 0, 8 * MIB),
        name="weight_partial",
    )(place, out, out, ca, cb)
    return outs[0::2], outs[1::2]


def plus(a, b):
    return (a.astype(f32) + b.astype(f32)).astype(bf16)


def sum_over_docs(up, down, first):
    route_up = [(i, (i + 1) % DOCS) for i in range(DOCS)]
    route_down = [(i, (i - 1) % DOCS) for i in range(DOCS)]
    a, b = up[3], down[1]
    for step in range(1, DOCS):
        a = lax.ppermute(a, "dp", route_up)
        b = lax.ppermute(b, "dp", route_down)
        if step == 1:
            a, b, first = after(a, b, first)
        if step < DOCS - 1:
            a = plus(a, up[3 - step])
            b = plus(b, down[1 + step])
    return (a, up[0], b, down[0]), first


def join_body(a_ref, own_a_ref, b_ref, own_b_ref, o_ref):
    n = CHIPS // 2
    o_ref[0:n] = plus(a_ref[...], own_a_ref[...]).reshape(n, 16, D)
    o_ref[n : 2 * n] = plus(b_ref[...], own_b_ref[...]).reshape(n, 16, D)


def join(*parts):
    return pl.pallas_call(
        join_body,
        out_shape=jax.ShapeDtypeStruct((CHIPS, 16, D), bf16),
        in_specs=[pl.BlockSpec(memory_space=pltpu.VMEM)] * 4,
        out_specs=pl.BlockSpec(memory_space=pltpu.VMEM),
        compiler_params=pltpu.CompilerParams(vmem_limit_bytes=VMEM_LIMIT),
        name="join",
    )(*parts)


def block_table(rider, core):
    offsets = rider.reshape(CHIPS, 2, SLOTS).astype(jnp.int32)
    c = jnp.arange(CHIPS, dtype=jnp.int32)[:, None, None]
    i = jnp.arange(2, dtype=jnp.int32)[None, :, None]
    target = 4 * c + 2 * core + i - offsets
    side = ((target >> 1) & 1) ^ core
    place = ((side * CHIPS + (target >> 2)) << 1) + (target & 1)
    return jnp.where(target >= 0, place, -1).reshape(2 * CHIPS, SLOTS)


def local(queries, key_states, value_states, out_weight, cotangent, block_offsets):
    core = lax.axis_index("seq") % 2
    cot = cotangent[0]
    cot_other = lax.ppermute(cot, "seq", CORE_SWAP)
    x = exchange(pack(block_offsets[0], key_states[0], value_states[0], queries[0]))
    x, g, cot_other = after(x, grad_attn_by_head(cot, out_weight), cot_other)
    y = lax.ppermute(x, "seq", CORE_SWAP)
    g = exchange(g)
    table = block_table(x[:, RIDER, 0 : 2 * SLOTS], core)
    table, place = after(table, jnp.stack([core, lax.axis_index("dp")]))
    out, prob = attention_forward(table, x, y)
    g, out = after(g, out)
    out_home = lax.all_to_all(out, "seq", 0, 0, tiled=True)
    own, other, gq = attention_backward(table, x, y, g, prob)
    out_home, own, other, gq = after(out_home, own, other, gq)
    gq_home = exchange(gq)
    got = lax.ppermute(other, "seq", CORE_SWAP)
    got, out_home = after(got, out_home)
    by_core = out_home.reshape(HEADS, 2, HEAD // 2, TOK)
    up, down = weight_partial(place, by_core, cot, cot_other)
    *up, got = after(*up, got)
    gq_home, gathered = after(gq_home, combine(own, got))
    sums, gq_home = sum_over_docs(up, down, gq_home)
    kv_home = exchange(gathered)
    kv_home, joined = after(kv_home, join(*sums))
    weight_grad = jnp.sum(exchange(joined).astype(f32), axis=0)
    (gq,) = unpack(gq_home, 1)
    gk, gv = unpack(kv_home, 2)
    return gq[None], gk[None], gv[None], weight_grad


def solution(mesh):
    in_specs = (
        P("dp", "seq", None),
        P("dp", "seq", None),
        P("dp", "seq", None),
        P(),
        P("dp", "seq", None),
        P("dp", "seq", None),
    )
    out_specs = (
        P("dp", "seq", None),
        P("dp", "seq", None),
        P("dp", "seq", None),
        P(("dp", "seq"), None),
    )
    return jax.shard_map(local, mesh=mesh, in_specs=in_specs, out_specs=out_specs, check_vma=False)
```

```python
import math

import jax
import jax.numpy as jnp
from jax import lax
from jax.experimental import pallas as pl
from jax.experimental.pallas import tpu as pltpu
from jax.sharding import PartitionSpec as P

HEADS = 16
HEAD = 128
BLK = 128
SLOTS = 4
D = HEADS * HEAD
TOK = 256
CHIPS = 16
BLOCKS = 64
WIDTH = (1 + SLOTS) * BLK
DOCS = 4
CHUNK = D // 4 // DOCS
RIDER = 3 * TOK
ROWS = 3 * TOK + 8
SCALE = HEAD ** (-0.5)
SCALE2 = SCALE * math.log2(math.e)
NEG = -1e30
bf16 = jnp.bfloat16
f32 = jnp.float32

SAME_CORE = [[2 * c + k for c in range(CHIPS)] for k in range(2)]
CORE_SWAP = [(i, i ^ 1) for i in range(2 * CHIPS)]

UNROLL = 4
GROUP = 4
PACK = 16
VMEM_LIMIT = 56 * 1024 * 1024


def dot(a, b, ca, cb):
    return lax.dot_general(a, b, (((ca,), (cb,)), ((), ())), preferred_element_type=f32)


def cost(flops, transcendentals=0, bytes_accessed=0):
    return pl.CostEstimate(
        flops=flops, transcendentals=transcendentals, bytes_accessed=bytes_accessed
    )


PAIRS = BLOCKS // 2 * BLK * (1 + SLOTS) * BLK
PAIR_FLOPS = 2 * HEAD * PAIRS
MIB = 1024 * 1024


def exchange(x):
    return lax.all_to_all(x, "seq", 0, 0, axis_index_groups=SAME_CORE, tiled=True)


def after(*values):
    return lax.optimization_barrier(values)


def pack_body(offs, k_ref, v_ref, q_ref, x_ref):
    lane = lax.broadcasted_iota(jnp.int32, (8, 128), 1)
    val = jnp.zeros((8, 128), jnp.int32)
    for j in range(2 * SLOTS):
        val = jnp.where(lane == j, offs[j // SLOTS, j % SLOTS], val)
    rider = val.astype(f32).astype(bf16)
    for h in range(PACK):
        for t, ref in enumerate((k_ref, v_ref, q_ref)):
            x_ref[h, t * TOK : (t + 1) * TOK, :] = ref[:, h * HEAD : (h + 1) * HEAD]
        x_ref[h, RIDER : RIDER + 8, :] = rider


def pack(offs, k, v, q):
    rows = pl.BlockSpec((TOK, PACK * HEAD), lambda i: (0, i))
    return pl.pallas_call(
        pack_body,
        out_shape=jax.ShapeDtypeStruct((HEADS, ROWS, HEAD), bf16),
        grid=(HEADS // PACK,),
        in_specs=[pl.BlockSpec(memory_space=pltpu.SMEM), rows, rows, rows],
        out_specs=pl.BlockSpec((PACK, ROWS, HEAD), lambda i: (i, 0, 0)),
        compiler_params=pltpu.CompilerParams(vmem_limit_bytes=VMEM_LIMIT),
        name="pack",
    )(offs, k, v, q)


def unpack_body(r_ref, *refs):
    for h in range(PACK):
        for t, ref in enumerate(refs):
            ref[:, h * HEAD : (h + 1) * HEAD] = r_ref[h, t * TOK : (t + 1) * TOK, :]


def unpack(r, n):
    out = jax.ShapeDtypeStruct((TOK, D), bf16)
    rows = pl.BlockSpec((TOK, PACK * HEAD), lambda i: (0, i))
    return pl.pallas_call(
        unpack_body,
        out_shape=(out,) * n,
        grid=(HEADS // PACK,),
        in_specs=[pl.BlockSpec((PACK, n * TOK, HEAD), lambda i: (i, 0, 0))],
        out_specs=[rows] * n,
        compiler_params=pltpu.CompilerParams(vmem_limit_bytes=VMEM_LIMIT),
        cost_estimate=cost(0, 0, 2 * n * MIB),
        name="unpack",
    )(r)


def grad_attn_body(c_ref, w_ref, o_ref):
    g = dot(c_ref[...], w_ref[...], 1, 1).astype(bf16)
    for j in range(2):
        o_ref[j] = g[:, j * HEAD : (j + 1) * HEAD]


def grad_attn_by_head(cot, weight):
    return pl.pallas_call(
        grad_attn_body,
        out_shape=jax.ShapeDtypeStruct((HEADS, TOK, HEAD), bf16),
        grid=(HEADS // 2,),
        in_specs=[
            pl.BlockSpec((TOK, D), lambda i: (0, 0)),
            pl.BlockSpec((2 * HEAD, D), lambda i: (i, 0)),
        ],
        out_specs=pl.BlockSpec((2, TOK, HEAD), lambda i: (i, 0, 0)),
        compiler_params=pltpu.CompilerParams(vmem_limit_bytes=VMEM_LIMIT),
        cost_estimate=cost(2 * TOK * D * D, 0, 10 * MIB),
        name="grad_attn",
    )(cot, weight)


def load_pool(x_ref, y_ref, kv, qs, sems):
    groups = []
    for j in range(CHIPS // GROUP):
        at = pl.ds(j * GROUP, GROUP)
        groups.append(
            [
                pltpu.make_async_copy(
                    x_ref.at[at, pl.ds(0, 2 * TOK), :], kv.at[at], sems.at[3 * j]
                ),
                pltpu.make_async_copy(
                    y_ref.at[at, pl.ds(0, 2 * TOK), :],
                    kv.at[pl.ds(CHIPS + j * GROUP, GROUP)],
                    sems.at[3 * j + 1],
                ),
                pltpu.make_async_copy(
                    x_ref.at[at, pl.ds(2 * TOK, TOK), :], qs.at[at], sems.at[3 * j + 2]
                ),
            ]
        )
    return groups


def listed(table, c, i):
    places = [(c, i * BLK, None)]
    for s in range(SLOTS):
        code = table[2 * c + i, s]
        f = jnp.maximum(code, 0)
        bias = jnp.where(code >= 0, 0.0, -NEG).astype(f32)
        places.append((f // 2, pl.multiple_of((f % 2) * BLK, BLK), bias))
    return places


def causal():
    u = lax.broadcasted_iota(jnp.int32, (BLK, BLK), 0)
    t = lax.broadcasted_iota(jnp.int32, (BLK, BLK), 1)
    return u <= t


def forward_body(table, x_ref, y_ref, o_ref, p_ref, kv, qs, ps, sems):
    groups = load_pool(x_ref, y_ref, kv, qs, sems)
    for copies in groups:
        for copy in copies:
            copy.start()

    def block(c, i):
        places = listed(table, c, i)
        q = qs[c, pl.ds(i * BLK, BLK), :]
        keys = jnp.concatenate([kv[p, pl.ds(r, BLK), :] for p, r, _ in places], axis=0)
        every = dot(keys, q, 1, 1)
        raw = [every[s * BLK : (s + 1) * BLK, :] for s in range(1 + SLOTS)]
        raw[0] = jnp.where(causal(), raw[0], NEG)
        peak = jnp.max(raw[0], axis=0, keepdims=True)
        for (_, _, bias), s in zip(places[1:], raw[1:]):
            peak = jnp.maximum(peak, jnp.max(s, axis=0, keepdims=True) - bias)
        peak = peak * SCALE2
        weights = []
        total = None
        for (_, _, bias), s in zip(places, raw):
            w = jnp.exp2(s * SCALE2 - (peak if bias is None else peak + bias))
            part = jnp.sum(w, axis=0, keepdims=True)
            total = part if total is None else total + part
            weights.append(w)
        inverse = 1.0 / total
        prob = jnp.concatenate([(w * inverse).astype(bf16) for w in weights], axis=0)
        ps[2 * c + i] = prob
        values = jnp.concatenate([kv[p, pl.ds(TOK + r, BLK), :] for p, r, _ in places], axis=0)
        return dot(values, prob, 0, 0).astype(bf16)

    def step(c, carry):
        for i in range(2):
            out = block(c, i)
            for g in range(8):
                row = (g // 2) * 16
                o_ref[2 * c + g % 2, row : row + 16, i * BLK : (i + 1) * BLK] = out[
                    g * 16 : g * 16 + 16, :
                ]
        return carry

    sends = []
    for j, copies in enumerate(groups):
        for copy in copies:
            copy.wait()
        lax.fori_loop(j * GROUP, (j + 1) * GROUP, step, 0, unroll=UNROLL)
        at = pl.ds(2 * j * GROUP, 2 * GROUP)
        sends.append(pltpu.make_async_copy(ps.at[at], p_ref.at[at], sems.at[3 * len(groups) + j]))
        sends[j].start()
    for copy in sends:
        copy.wait()


def attention_forward(table, x, y):
    return pl.pallas_call(
        forward_body,
        out_shape=(
            jax.ShapeDtypeStruct((2 * CHIPS, HEAD // 2, TOK), bf16),
            jax.ShapeDtypeStruct((2 * CHIPS, WIDTH, BLK), bf16),
        ),
        in_specs=[pl.BlockSpec(memory_space=pltpu.SMEM)] + [pl.BlockSpec(memory_space=pl.ANY)] * 2,
        out_specs=[pl.BlockSpec(memory_space=pltpu.VMEM), pl.BlockSpec(memory_space=pl.ANY)],
        scratch_shapes=[
            pltpu.VMEM((2 * CHIPS, 2 * TOK, HEAD), bf16),
            pltpu.VMEM((CHIPS, TOK, HEAD), bf16),
            pltpu.VMEM((2 * CHIPS, WIDTH, BLK), bf16),
            pltpu.SemaphoreType.DMA((4 * (CHIPS // GROUP),)),
        ],
        compiler_params=pltpu.CompilerParams(vmem_limit_bytes=VMEM_LIMIT),
        cost_estimate=cost(2 * PAIR_FLOPS, PAIRS, 12 * MIB),
        name="attn_fwd",
    )(table, x, y)


def backward_body(
    table, x_ref, y_ref, g_ref, p_ref, own_ref, other_ref, gq_ref, kv, qs, gs, ps, acck, accv, own, other, gq, sems
):
    groups = load_pool(x_ref, y_ref, kv, qs, sems)
    sends = []
    n = CHIPS // GROUP
    for j in range(n):
        at = pl.ds(j * GROUP, GROUP)
        groups[j].append(pltpu.make_async_copy(g_ref.at[at], gs.at[at], sems.at[3 * n + j]))
        two = pl.ds(2 * j * GROUP, 2 * GROUP)
        groups[j].append(pltpu.make_async_copy(p_ref.at[two], ps.at[two], sems.at[7 * n + j]))
        sends.append(
            [
                pltpu.make_async_copy(
                    gq.at[at], gq_ref.at[at], sems.at[4 * n + j]
                ),
                pltpu.make_async_copy(
                    own.at[at], own_ref.at[at], sems.at[5 * n + j]
                ),
                pltpu.make_async_copy(other.at[at], other_ref.at[at], sems.at[6 * n + j]),
            ]
        )
    for copies in groups:
        for copy in copies:
            copy.start()

    def clear(j, carry):
        acck[CHIPS + j] = jnp.zeros((TOK, HEAD), f32)
        accv[CHIPS + j] = jnp.zeros((TOK, HEAD), f32)
        return carry

    lax.fori_loop(0, CHIPS, clear, 0)

    def block(c, i):
        places = listed(table, c, i)
        q = qs[c, pl.ds(i * BLK, BLK), :]
        g = gs[c, pl.ds(i * BLK, BLK), :]
        keys = jnp.concatenate([kv[p, pl.ds(r, BLK), :] for p, r, _ in places], axis=0)
        values = jnp.concatenate([kv[p, pl.ds(TOK + r, BLK), :] for p, r, _ in places], axis=0)
        grads = dot(values, g, 1, 1)
        low = ps[2 * c + i]
        prob = low.astype(f32)
        row_dot = jnp.sum(prob * grads, axis=0, keepdims=True)
        score = (prob * (grads - row_dot)).astype(bf16)
        gk = dot(score, q, 1, 0)
        gv = dot(low, g, 1, 0)
        for j, (p, r, _) in enumerate(places):
            at = pl.ds(r, BLK)
            if j == 0:
                acck[p, at, :] = gk[0:BLK, :]
                accv[p, at, :] = gv[0:BLK, :]
            else:
                acck[p, at, :] += gk[j * BLK : (j + 1) * BLK, :]
                accv[p, at, :] += gv[j * BLK : (j + 1) * BLK, :]
        gq[c, pl.ds(i * BLK, BLK), :] = (dot(score, keys, 0, 0) * SCALE).astype(bf16)

    def step(c, carry):
        for i in range(2):
            block(c, i)
        return carry

    def flush(j, carry):
        own[j, 0:TOK, :] = (acck[j] * SCALE).astype(bf16)
        own[j, TOK : 2 * TOK, :] = accv[j].astype(bf16)
        other[j, 0:TOK, :] = (acck[CHIPS + j] * SCALE).astype(bf16)
        other[j, TOK : 2 * TOK, :] = accv[CHIPS + j].astype(bf16)
        return carry

    for j in range(n + 2):
        if j < n:
            for copy in groups[j]:
                copy.wait()
            lax.fori_loop(j * GROUP, (j + 1) * GROUP, step, 0, unroll=UNROLL)
            sends[j][0].start()
        if j >= 2:
            lax.fori_loop((j - 2) * GROUP, (j - 1) * GROUP, flush, 0)
            sends[j - 2][1].start()
            sends[j - 2][2].start()
    for copies in sends:
        for copy in copies:
            copy.wait()


def attention_backward(table, x, y, g, prob):
    return pl.pallas_call(
        backward_body,
        out_shape=(
            jax.ShapeDtypeStruct((CHIPS, 2 * TOK, HEAD), bf16),
            jax.ShapeDtypeStruct((CHIPS, 2 * TOK, HEAD), bf16),
            jax.ShapeDtypeStruct((CHIPS, TOK, HEAD), bf16),
        ),
        in_specs=[pl.BlockSpec(memory_space=pltpu.SMEM)]
        + [pl.BlockSpec(memory_space=pl.ANY)] * 4,
        out_specs=[pl.BlockSpec(memory_space=pl.ANY)] * 3,
        scratch_shapes=[
            pltpu.VMEM((2 * CHIPS, 2 * TOK, HEAD), bf16),
            pltpu.VMEM((CHIPS, TOK, HEAD), bf16),
            pltpu.VMEM((CHIPS, TOK, HEAD), bf16),
            pltpu.VMEM((2 * CHIPS, WIDTH, BLK), bf16),
            pltpu.VMEM((2 * CHIPS, TOK, HEAD), f32),
            pltpu.VMEM((2 * CHIPS, TOK, HEAD), f32),
            pltpu.VMEM((CHIPS, 2 * TOK, HEAD), bf16),
            pltpu.VMEM((CHIPS, 2 * TOK, HEAD), bf16),
            pltpu.VMEM((CHIPS, TOK, HEAD), bf16),
            pltpu.SemaphoreType.DMA((8 * (CHIPS // GROUP),)),
        ],
        compiler_params=pltpu.CompilerParams(vmem_limit_bytes=VMEM_LIMIT),
        cost_estimate=cost(4 * PAIR_FLOPS, 0, 17 * MIB),
        name="attn_bwd",
    )(table, x, y, g, prob)


def combine_body(own_ref, got_ref, o_ref):
    o_ref[...] = (own_ref[...].astype(f32) + got_ref[...].astype(f32)).astype(bf16)


def combine(own, got):
    n = 8
    rows = pl.BlockSpec((n, 2 * TOK, HEAD), lambda i: (i, 0, 0))
    return pl.pallas_call(
        combine_body,
        out_shape=jax.ShapeDtypeStruct((CHIPS, 2 * TOK, HEAD), bf16),
        grid=(CHIPS // n,),
        in_specs=[rows, rows],
        out_specs=rows,
        compiler_params=pltpu.CompilerParams(vmem_limit_bytes=VMEM_LIMIT),
        cost_estimate=cost(CHIPS * 2 * TOK * HEAD, 0, 6 * MIB),
        name="combine",
    )(own, got)


def weight_body(place, oa_ref, ob_ref, ca_ref, cb_ref, *rest):
    outs, buf, sems = rest[: 2 * DOCS], rest[2 * DOCS], rest[2 * DOCS + 1]
    copies = []
    for d in (3, 1, 2, 0):
        heads = pl.ds(((place[1] + d) % DOCS) * (HEADS // DOCS), HEADS // DOCS)
        a = oa_ref[heads].reshape(2 * CHUNK, TOK)
        b = ob_ref[heads].reshape(2 * CHUNK, TOK)
        buf[d] = (dot(a, ca_ref[...], 1, 0) + dot(b, cb_ref[...], 1, 0)).astype(bf16)
        for half in range(2):
            j = 2 * d + half
            copies.append(
                pltpu.make_async_copy(
                    buf.at[d, pl.ds(half * CHUNK, CHUNK), :], outs[j], sems.at[j]
                )
            )
            copies[-1].start()
    for copy in copies:
        copy.wait()


def weight_partial(place, out, ca, cb):
    own = pl.BlockSpec((HEADS, 1, HEAD // 2, TOK), lambda i, place: (0, place[0], 0, 0))
    other = pl.BlockSpec((HEADS, 1, HEAD // 2, TOK), lambda i, place: (0, 1 - place[0], 0, 0))
    whole = pl.BlockSpec((TOK, D), lambda i, place: (0, 0))
    outs = pl.pallas_call(
        weight_body,
        out_shape=(jax.ShapeDtypeStruct((CHUNK, D), bf16),) * (2 * DOCS),
        grid_spec=pltpu.PrefetchScalarGridSpec(
            num_scalar_prefetch=1,
            grid=(1,),
            in_specs=[own, other, whole, whole],
            out_specs=[pl.BlockSpec(memory_space=pl.ANY)] * (2 * DOCS),
            scratch_shapes=[
                pltpu.VMEM((DOCS, 2 * CHUNK, D), bf16),
                pltpu.SemaphoreType.DMA((2 * DOCS,)),
            ],
        ),
        compiler_params=pltpu.CompilerParams(vmem_limit_bytes=VMEM_LIMIT),
        cost_estimate=cost(2 * TOK * D * D, 0, 8 * MIB),
        name="weight_partial",
    )(place, out, out, ca, cb)
    return outs[0::2], outs[1::2]


def plus(a, b):
    return (a.astype(f32) + b.astype(f32)).astype(bf16)


def sum_over_docs(up, down, first):
    route_up = [(i, (i + 1) % DOCS) for i in range(DOCS)]
    route_down = [(i, (i - 1) % DOCS) for i in range(DOCS)]
    a, b = up[3], down[1]
    for step in range(1, DOCS):
        a = lax.ppermute(a, "dp", route_up)
        b = lax.ppermute(b, "dp", route_down)
        if step == 1:
            a, b, first = after(a, b, first)
        if step < DOCS - 1:
            a = plus(a, up[3 - step])
            b = plus(b, down[1 + step])
    return (a, up[0], b, down[0]), first


def join_body(a_ref, own_a_ref, b_ref, own_b_ref, o_ref):
    n = CHIPS // 2
    o_ref[0:n] = plus(a_ref[...], own_a_ref[...]).reshape(n, 16, D)
    o_ref[n : 2 * n] = plus(b_ref[...], own_b_ref[...]).reshape(n, 16, D)


def join(*parts):
    return pl.pallas_call(
        join_body,
        out_shape=jax.ShapeDtypeStruct((CHIPS, 16, D), bf16),
        in_specs=[pl.BlockSpec(memory_space=pltpu.VMEM)] * 4,
        out_specs=pl.BlockSpec(memory_space=pltpu.VMEM),
        compiler_params=pltpu.CompilerParams(vmem_limit_bytes=VMEM_LIMIT),
        name="join",
    )(*parts)


def block_table(rider, core):
    offsets = rider.reshape(CHIPS, 2, SLOTS).astype(jnp.int32)
    c = jnp.arange(CHIPS, dtype=jnp.int32)[:, None, None]
    i = jnp.arange(2, dtype=jnp.int32)[None, :, None]
    target = 4 * c + 2 * core + i - offsets
    side = ((target >> 1) & 1) ^ core
    place = ((side * CHIPS + (target >> 2)) << 1) + (target & 1)
    return jnp.where(target >= 0, place, -1).reshape(2 * CHIPS, SLOTS)


def local(queries, key_states, value_states, out_weight, cotangent, block_offsets):
    core = lax.axis_index("seq") % 2
    cot = cotangent[0]
    cot_other = lax.ppermute(cot, "seq", CORE_SWAP)
    x = exchange(pack(block_offsets[0], key_states[0], value_states[0], queries[0]))
    x, g, cot_other = after(x, grad_attn_by_head(cot, out_weight), cot_other)
    y = lax.ppermute(x, "seq", CORE_SWAP)
    g = exchange(g)
    table = block_table(x[:, RIDER, 0 : 2 * SLOTS], core)
    table, place = after(table, jnp.stack([core, lax.axis_index("dp")]))
    out, prob = attention_forward(table, x, y)
    g, out = after(g, out)
    out_home = lax.all_to_all(out, "seq", 0, 0, tiled=True)
    own, other, gq = attention_backward(table, x, y, g, prob)
    out_home, own, other, gq = after(out_home, own, other, gq)
    gq_home = exchange(gq)
    got = lax.ppermute(other, "seq", CORE_SWAP)
    got, out_home = after(got, out_home)
    by_core = out_home.reshape(HEADS, 2, HEAD // 2, TOK)
    up, down = weight_partial(place, by_core, cot, cot_other)
    *up, got = after(*up, got)
    gq_home, gathered = after(gq_home, combine(own, got))
    sums, gq_home = sum_over_docs(up, down, gq_home)
    kv_home = exchange(gathered)
    kv_home, joined = after(kv_home, join(*sums))
    weight_grad = jnp.sum(exchange(joined).astype(f32), axis=0)
    (gq,) = unpack(gq_home, 1)
    gk, gv = unpack(kv_home, 2)
    return gq[None], gk[None], gv[None], weight_grad


def solution(mesh):
    in_specs = (
        P("dp", "seq", None),
        P("dp", "seq", None),
        P("dp", "seq", None),
        P(),
        P("dp", "seq", None),
        P("dp", "seq", None),
    )
    out_specs = (
        P("dp", "seq", None),
        P("dp", "seq", None),
        P("dp", "seq", None),
        P(("dp", "seq"), None),
    )
    return jax.shard_map(local, mesh=mesh, in_specs=in_specs, out_specs=out_specs, check_vma=False)
```
